32 devices in a mesh: gx: 8 (over y, x, core), gz: 4 (over z).
Axes of the slice: x: 2, y: 2, z: 4, core: 2. Of those that a mesh axis runs over, the one named last changes fastest.
Arguments:
- velocity_old: float32 [3, 64, 64, 128], P(None, 'gx', 'gz'), may hold values from -6 to 6
- source: float32 [3, 64, 64, 128], P(None, 'gx', 'gz'), may hold values from -6 to 6
- diag_coef: float32 [64, 64, 128], P('gx', 'gz'), may hold values from 0.5 to 2
- face_coef: float32 [3, 64, 64, 128], P(None, 'gx', 'gz'), may hold values from 0.2 to 2
- bc_flags: int32 [2, 64, 64], P(None, 'gx', 'gz'), may hold values from 0 to 1
- coarse_map: int32 [64, 64, 128], P('gx', 'gz'), may hold values from 0 to 15
- coarse_inverse: float32 [512, 64], P('gx'), may hold values from -0.1 to 0.3
Outputs:
- velocity: float32 [3, 64, 64, 128], P(None, 'gx', 'gz')
- pressure: float32 [64, 64, 128], P('gx', 'gz')
The draws below stay inside these ranges and needn't reach their ends.
All inputs are finite; a program needn't handle non-finite values.
Results may differ from the reference program's by a relative error of at most 0.0003.
Values sent between devices are 32-bit elements; how exact they have to be, the bound alone decides.
A program may use at most 64 MiB of HBM per device.

```python
import math
import jax
import jax.numpy as jnp
from jax import lax

CX = 8
CZ = 16
NY = 128
COARSE = 16
NX = 64
NZ = 64
GROUP = 64
N_GX = 8
N_GZ = 4


def draw_coarse_inverse(key, part):
    first, second = jax.random.split(jax.random.fold_in(key, 7))
    spread = jnp.clip(jax.random.normal(first, (N_GX * GROUP, GROUP), jnp.float32), -4.0, 4.0) / jnp.sqrt(jnp.float32(GROUP))
    scales = jax.random.uniform(second, (N_GX * GROUP, 1), jnp.float32, 0.05, 0.2)
    identity = jnp.tile(jnp.eye(GROUP, dtype=jnp.float32), (N_GX, 1))
    return ((identity + 0.5 * spread) * scales).astype(jnp.float32)


def plant(array, rng, least, high):
    dims = array.shape
    index_at = [jax.random.randint(jax.random.fold_in(rng, axis), (), 0, dims[axis]) for axis in range(len(dims))]
    array = array.at[tuple(index_at)].set(least)
    longest = dims.index(max(dims))
    index_at[longest] = (index_at[longest] + 1) % dims[longest]
    return array.at[tuple(index_at)].set(high)


def level_of(key, extent, cuts, smallest, largest):
    def one(dim, parts):
        draws = jax.random.uniform(jax.random.fold_in(jax.random.fold_in(key, 6), dim), (parts,), jnp.float32, smallest / len(cuts), largest / len(cuts))
        return jnp.repeat(jnp.exp(draws), extent[dim] // parts).reshape((-1,) + (1,) * (len(extent) - dim - 1))

    level = one(*cuts[0])
    for cut in cuts[1:]:
        level = level * one(*cut)
    return level


def centred(rng, shape, width, limit, shards=(), kind=jnp.bfloat16):
    result = width * jax.random.normal(rng, shape, jnp.float32)
    if shards:
        result = result * level_of(rng, shape, shards, -0.22, 0.18)
    return jnp.clip(result, -limit, limit).astype(kind)


def setup_inputs(seed: int = 0) -> dict:
    splits = jax.random.split(jax.random.key(seed), 8)
    return {
        "velocity_old": centred(splits[0], (3, NX, NZ, NY), 1.0, 6.0, ((1, 8), (2, 4)), jnp.float32),
        "source": centred(splits[1], (3, NX, NZ, NY), 1.0, 6.0, ((1, 8), (2, 4)), jnp.float32),
        "diag_coef": jnp.clip(jnp.exp(math.log(2.0) - 1.3862944 * jax.random.uniform(splits[2], (NX, NZ, NY), jnp.float32) ** level_of(splits[2], (NX, NZ, NY), ((0, 8), (1, 4)), -0.2, 0.2)), 0.5, 2.0),
        "face_coef": jnp.clip(jnp.exp(math.log(2.0) - 2.3025851 * jax.random.uniform(splits[3], (3, NX, NZ, NY), jnp.float32) ** level_of(splits[3], (3, NX, NZ, NY), ((1, 8), (2, 4)), -0.2, 0.2)), 0.2, 2.0),
        "bc_flags": plant(jax.random.randint(splits[4], (2, NX, NZ), 0, 2), jax.random.fold_in(splits[4], 1), 0, 1).astype(jnp.int32),
        "coarse_map": plant(jax.random.randint(splits[5], (NX, NZ, NY), 0, COARSE), jax.random.fold_in(splits[5], 1), 0, COARSE - 1).astype(jnp.int32),
        "coarse_inverse": draw_coarse_inverse(jax.random.fold_in(splits[7], 71), 0),
    }


jacobi_weight = 2.0 / 3.0


def momentum_apply(field, diag_coef, face_coef):
    coef_x, coef_z, coef_y = face_coef[0], face_coef[1], face_coef[2]
    count_y = coef_y.shape[-1]
    level = lax.broadcasted_iota(jnp.int32, coef_y.shape, 2)
    wall = jnp.where((level == 0) | (level == count_y - 1), coef_y[..., -1:], 0.0)
    flux_x = coef_x * (field - jnp.roll(field, -1, axis=1))
    flux_z = coef_z * (field - jnp.roll(field, -1, axis=2))
    planar = (flux_x - jnp.roll(flux_x, 1, axis=1)) + (flux_z - jnp.roll(flux_z, 1, axis=2))
    grad_y = coef_y[..., :-1] * (field[..., :-1] - field[..., 1:])
    zero = jnp.zeros_like(field[..., :1])
    vertical = jnp.concatenate([grad_y, zero], -1) - jnp.concatenate([zero, grad_y], -1) + wall * field
    return diag_coef * field + planar + vertical


def pressure_apply(field, pdiag):
    zero = jnp.zeros_like(field[..., :1])
    beside = (jnp.roll(field, -1, 0) + jnp.roll(field, 1, 0)) + (jnp.roll(field, -1, 1) + jnp.roll(field, 1, 1))
    beside = beside + (jnp.concatenate([field[..., 1:], zero], -1) + jnp.concatenate([zero, field[..., :-1]], -1))
    return pdiag * field - beside


def inner(left, right):
    return jnp.sum(left * right, axis=(1, 2, 3))


def widen(value):
    return value[:, None, None, None]


def reference(velocity_old, source, diag_coef, face_coef, bc_flags, coarse_map, coarse_inverse):
    def apply(field):
        return momentum_apply(field, diag_coef, face_coef)

    x = velocity_old
    r = source - apply(x)
    r0 = r
    p = r
    v = apply(p)
    rho = inner(r0, r0)
    alpha = rho / inner(r0, v)
    s = r - widen(alpha) * v
    t = apply(s)
    omega = inner(t, s) / inner(t, t)
    x = x + widen(alpha) * p + widen(omega) * s
    r = s - widen(omega) * t
    rho_new = inner(r0, s) - omega * inner(r0, t)
    beta = (rho_new / rho) * (alpha / omega)
    p = r + widen(beta) * (p - widen(omega) * v)
    v = apply(p)
    alpha = rho_new / inner(r0, v)
    s = r - widen(alpha) * v
    t = apply(s)
    omega = inner(t, s) / inner(t, t)
    velocity = x + widen(alpha) * p + widen(omega) * s

    along_x, along_z, along_y = velocity[0], velocity[1], velocity[2]
    zero = jnp.zeros_like(along_y[..., :1])
    div = (along_x - jnp.roll(along_x, 1, 0)) + (along_z - jnp.roll(along_z, 1, 1))
    div = div + (along_y - jnp.concatenate([zero, along_y[..., :-1]], -1))
    level = lax.broadcasted_iota(jnp.int32, div.shape, 2)
    flags = bc_flags.astype(jnp.float32)
    bottom = level == 0
    top = level == NY - 1
    pdiag = 6.0 - bottom.astype(jnp.float32) - top.astype(jnp.float32)
    pdiag = pdiag + jnp.where(bottom, flags[0][..., None], 0.0) + jnp.where(top, flags[1][..., None], 0.0)

    q = jacobi_weight * div / pdiag
    q = q + jacobi_weight * (div - pressure_apply(q, pdiag)) / pdiag
    res = div - pressure_apply(q, pdiag)
    block_x = lax.broadcasted_iota(jnp.int32, div.shape, 0) // CX
    block_z = lax.broadcasted_iota(jnp.int32, div.shape, 1) // CZ
    ids = ((block_x * N_GZ + block_z) * COARSE + coarse_map).astype(jnp.int32)
    coarse = jax.ops.segment_sum(res.reshape(-1), ids.reshape(-1), num_segments=N_GX * N_GZ * COARSE)
    coarse = coarse.reshape(N_GX, GROUP)
    blocks = coarse_inverse.reshape(N_GX, GROUP, GROUP)
    corr = jnp.einsum("gab,gb->ga", blocks, coarse, precision=lax.Precision.HIGHEST).reshape(-1)
    q = q + corr[ids]
    for sweep in range(2):
        q = q + jacobi_weight * (div - pressure_apply(q, pdiag)) / pdiag
    return velocity, q
```

```python
import functools

import jax
import jax.numpy as jnp
from jax import lax
from jax.experimental import pallas as pl
from jax.experimental.pallas import tpu as pltpu
from jax.sharding import PartitionSpec as P

COARSE = 16
PAD = 8
DIRECT = 64

jacobi_weight = 2.0 / 3.0
MESH = pl.DeviceIdType.MESH


def kernel(
    dims,
    x0_in, src_in, diag_in, face_in, bc_in, map_in, inv_in,
    vel_ref, out_ref,
    x0_ref, src_ref, face_ref, bc_ref, map_ref, inv_ref,
    coef, res_ref, r_far, vk_ref, a1_ref, a2_ref, a3_ref,
    prs, pxlo, pxhi, pzlo, pzhi, pzsend,
    qxlo, qxhi, qzlo, qzhi, qzsend, qc_send, qc,
    mxlo, mxhi, mzlo, mzhi, mzsend, mc_send, mc,
    dxlo, dxhi, dzlo, dzhi, dzsend, inv_w, inv_e,
    msg, got, msg_z, got_z, msg_c, got_c, got_w, got_e,
    send_sem, recv_sem, near_s, near_r,
    sum_s, sum_r, sum_sz, sum_rz, coarse_s, coarse_r,
    load_sem, side_s, side_r,
):
    n_gx, n_gz, cx_n, cz_n, ny, lanes = dims
    rows = cx_n * cz_n
    deep = x0_ref.shape[2]
    gx = lax.axis_index("gx")
    gz = lax.axis_index("gz")
    east = (lax.rem(gx + 1, n_gx), gz)
    west = (lax.rem(gx + n_gx - 1, n_gx), gz)
    north = (gx, lax.rem(gz + 1, n_gz))
    south = (gx, lax.rem(gz + n_gz - 1, n_gz))
    row_x = [(lax.rem(gx + d, n_gx), gz) for d in range(1, n_gx)]
    row_z = [(gx, lax.rem(gz + d, n_gz)) for d in range(1, n_gz)]
    direct = n_gx * n_gz <= DIRECT
    pending = []

    def send(src, dst, ssem, rsem, to):
        copy = pltpu.make_async_remote_copy(
            src_ref=src, dst_ref=dst, send_sem=ssem, recv_sem=rsem,
            device_id=to, device_id_type=MESH,
        )
        copy.start()
        pending.append(copy)
        return copy

    aside_w = [(west[0], to[1]) for to in row_z]
    aside_e = [(east[0], to[1]) for to in row_z]
    corners = [
        (east[0], north[1]), (east[0], south[1]), (west[0], north[1]), (west[0], south[1])
    ]
    if direct:
        sum_to = [
            (lax.rem(gx + d, n_gx), lax.rem(gz + k, n_gz))
            for k in sorted(range(n_gz), key=lambda k: -min(k, n_gz - k))
            for d in sorted(range(n_gx), key=lambda d: -min(d, n_gx - d))
            if d or k
        ]
        partners = sum_to
    else:
        sum_to = row_x
        partners = row_x + row_z + aside_w + aside_e

    def inner(ref, halo):
        return ref.at[..., pl.ds(halo, cx_n), pl.ds(0, cz_n), :]

    loads = [
        pltpu.make_async_copy(a, b, load_sem.at[i])
        for i, (a, b) in enumerate(
            [
                (x0_in, inner(x0_ref, 2)), (face_in, inner(face_ref.at[pl.ds(0, 3)], 3)),
                (diag_in, inner(face_ref.at[3], 3)), (src_in, inner(src_ref, 1)),
                (bc_in, bc_ref), (map_in, map_ref), (inv_in, inv_ref),
            ]
        )
    ]
    for load in loads:
        load.start()
    barrier = pltpu.get_barrier_semaphore()
    for other in partners:
        pl.semaphore_signal(barrier, inc=1, device_id=other, device_id_type=MESH)
    for load in loads[:4]:
        load.wait()
    pl.semaphore_wait(barrier, len(partners))

    last = rows - cz_n

    def side_x(sign, halo, a, b):
        if sign > 0:
            return pl.ds(halo + cx_n - b, b - a + 1), pl.ds(halo - b, b - a + 1)
        return pl.ds(halo + a - 1, b - a + 1), pl.ds(halo + cx_n + a - 1, b - a + 1)

    def side_z(sign, a, b):
        if sign > 0:
            return pl.ds(cz_n - b, b - a + 1), pl.ds(deep - b, b - a + 1)
        return pl.ds(a - 1, b - a + 1), pl.ds(cz_n + a - 1, b - a + 1)

    used = []

    def ship(src, dst, to, where_from, where_to):
        i = len(used)
        used.append(i)
        return send(
            src.at[(..., *where_from, slice(None))], dst.at[(..., *where_to, slice(None))],
            near_s.at[i], near_r.at[i], to,
        )

    def to_corners(src, dst, halo, n):
        out = []
        for to, sx, sz in zip(corners, (1, 1, -1, -1), (1, -1, 1, -1)):
            (fx, tx), (fz, tz) = side_x(sx, halo, 1, n), side_z(sz, 1, n)
            out.append(ship(src, dst, to, (fx, fz), (tx, tz)))
        return out

    def to_z(src, dst, halo, a, b, ways=(1, -1)):
        out = []
        for sz in ways:
            fz, tz = side_z(sz, a, b)
            x = pl.ds(halo, cx_n)
            out.append(ship(src, dst, north if sz > 0 else south, (x, fz), (x, tz)))
        return out

    def to_x(src, dst, halo, a, b, ways=(1, -1)):
        out = []
        for sx in ways:
            fx, tx = side_x(sx, halo, a, b)
            z = pl.ds(0, cz_n)
            out.append(ship(src, dst, east if sx > 0 else west, (fx, z), (tx, z)))
        return out

    first = to_corners(x0_ref, x0_ref, 2, 1)
    first += to_corners(face_ref, face_ref, 3, 2)
    first += to_z(x0_ref, x0_ref, 2, 1, 2)
    first += to_z(face_ref, face_ref, 3, 1, 2)
    first += to_z(face_ref.at[1], face_ref.at[1], 3, 3, 3, (1,))
    first += to_z(src_ref, src_ref, 1, 1, 1)
    first += to_x(x0_ref, x0_ref, 2, 1, 2)
    first += to_x(face_ref, face_ref, 3, 1, 2)
    first += to_x(face_ref.at[0], face_ref.at[0], 3, 3, 3, (1,))
    first += to_x(src_ref, src_ref, 1, 1, 1)

    def exchange(phase, src, zs, lo_x, hi_x, lo_z, hi_z):
        zs[0] = src[:, pl.ds(cz_n - 1, cx_n, stride=cz_n), :]
        zs[1] = src[:, pl.ds(0, cx_n, stride=cz_n), :]
        sems = [(send_sem.at[phase, i], recv_sem.at[phase, i]) for i in range(4)]
        return [
            send(zs.at[0], lo_z, *sems[2], north),
            send(zs.at[1], hi_z, *sems[3], south),
            send(src.at[:, pl.ds(last, cz_n), :], lo_x, *sems[0], east),
            send(src.at[:, pl.ds(0, cz_n), :], hi_x, *sems[1], west),
        ]

    def exchange_pressure(i):
        return exchange(
            i, prs.at[i], pzsend.at[i], pxlo.at[i], pxhi.at[i], pzlo.at[i], pzhi.at[i]
        )

    def part(ref, which):
        return (slice(None),) * (len(ref.shape) - 2) + (which, slice(None))

    def exchange_wide(base, f, zs, cs, lo_x, hi_x, lo_z, hi_z, hold):
        sem = [(side_s.at[base + i], side_r.at[base + i]) for i in range(8)]
        for k, r in enumerate((rows - 1, last, cz_n - 1, 0)):
            cs[k] = f[part(f, pl.ds(r, 1))]
        for k in range(2):
            zs[0, k] = f[part(f, pl.ds(cz_n - 2 + k, cx_n, stride=cz_n))]
            zs[1, k] = f[part(f, pl.ds(k, cx_n, stride=cz_n))]
        copies = [
            send(cs.at[k], hold.at[k], *sem[k], to) for k, to in enumerate(corners)
        ]
        copies.append(send(zs.at[0], lo_z, *sem[4], north))
        copies.append(send(zs.at[1], hi_z, *sem[5], south))
        copies.append(send(f.at[part(f, pl.ds(last - cz_n, 2 * cz_n))], lo_x, *sem[6], east))
        copies.append(send(f.at[part(f, pl.ds(0, 2 * cz_n))], hi_x, *sem[7], west))
        return copies

    def arrive(copies):
        for copy in copies:
            copy.wait_recv()

    level = lax.broadcasted_iota(jnp.int32, (rows, ny), 1)
    depth = lax.rem(lax.broadcasted_iota(jnp.int32, (rows, ny), 0), cz_n)
    bottom = level == 0
    top = level == ny - 1
    front = depth == 0
    back = depth == cz_n - 1

    def spread(edge):
        wide = jnp.broadcast_to(edge[..., None, :], edge.shape[:-1] + (cz_n, ny))
        return wide.reshape(edge.shape[:-2] + (rows, ny))

    def x_prev(f, edge):
        return jnp.concatenate([edge, f[..., : rows - cz_n, :]], -2)

    def x_next(f, edge):
        return jnp.concatenate([f[..., cz_n:, :], edge], -2)

    def z_prev(f, edge):
        return jnp.where(front, spread(edge), pltpu.roll(f, 1, f.ndim - 2))

    def z_next(f, edge):
        return jnp.where(back, spread(edge), pltpu.roll(f, rows - 1, f.ndim - 2))

    def y_prev(f):
        return pltpu.roll(f, 1, f.ndim - 1)

    def y_next(f):
        return pltpu.roll(f, ny - 1, f.ndim - 1)

    eye = lax.broadcasted_iota(jnp.int32, (cz_n, cz_n), 0) == lax.broadcasted_iota(
        jnp.int32, (cz_n, cz_n), 1
    )

    def column(side):
        flags = bc_ref[side].astype(jnp.float32)
        parts = [
            jnp.sum(
                jnp.where(eye, jnp.broadcast_to(flags[i : i + 1], (cz_n, cz_n)), 0.0),
                axis=1, keepdims=True,
            )
            for i in range(cx_n)
        ]
        return jnp.broadcast_to(jnp.concatenate(parts, 0), (rows, ny))

    edge_rows = (cz_n, cz_n, cx_n, cx_n)
    around = ((0, 1), (2, 3), (0, 2), (1, 3))

    def insides(ref):
        return (
            ref[part(ref, pl.ds(0, cz_n))],
            ref[part(ref, pl.ds(last, cz_n))],
            ref[part(ref, pl.ds(0, cx_n, stride=cz_n))],
            ref[part(ref, pl.ds(cz_n - 1, cx_n, stride=cz_n))],
        )

    def split(lo_x, hi_x, lo_z, hi_z):
        near = (lo_x[..., cz_n:, :], hi_x[..., :cz_n, :], lo_z[1], hi_z[0])
        far = (lo_x[..., :cz_n, :], hi_x[..., cz_n:, :], lo_z[0], hi_z[1])
        return near, far

    def along_face(k, f, before, after):
        n = edge_rows[k]
        pos = lax.broadcasted_iota(jnp.int32, (n, ny), 0)
        return (
            jnp.where(pos == 0, before, pltpu.roll(f, 1, f.ndim - 2)),
            jnp.where(pos == n - 1, after, pltpu.roll(f, n - 1, f.ndim - 2)),
        )

    def scatter(msg, got, ssem, rsem, others):
        return [
            send(msg, got.at[d], ssem.at[d], rsem, to) for d, to in enumerate(others)
        ]

    def gathered(msg, got, rsem):
        pltpu.make_async_copy(got, got, rsem).wait()
        return msg[...] + jnp.sum(got[...], axis=0)


    def z_roll(f, shift):
        flat = f.reshape((-1,) + f.shape[-2:])
        return pltpu.roll(flat, shift % deep, 1).reshape(f.shape)

    def apply(f, c):
        h = (f.shape[0] - cx_n) // 2 - 1
        n = cx_n + 2 * h
        g = f[1:-1]
        total = coef[0, pl.ds(2 - h, n)] * g
        total -= face_ref[0, pl.ds(3 - h, n)] * f[2:] + face_ref[0, pl.ds(2 - h, n)] * f[:-2]
        total -= face_ref[1, pl.ds(3 - h, n)] * z_roll(g, -1) + coef[1, pl.ds(2 - h, n)] * z_roll(g, 1)
        total -= coef[2, pl.ds(2 - h, n)] * y_next(g) + coef[3, pl.ds(2 - h, n)] * y_prev(g)
        return total

    def own(f):
        h = (f.shape[0] - cx_n) // 2
        return f[h : h + cx_n, :cz_n].reshape(rows, ny)

    def pack(pairs):
        sums = [jnp.sum(a * b, axis=0, keepdims=True) for a, b in pairs]
        while len(sums) < 3 * PAD:
            sums.append(jnp.zeros_like(sums[0]))
        total = jnp.sum(jnp.concatenate(sums, 0), axis=1, keepdims=True)
        shape = (3 * PAD, 128)
        pick = lax.broadcasted_iota(jnp.int32, shape, 0) == lax.broadcasted_iota(
            jnp.int32, shape, 1
        )
        return jnp.sum(
            jnp.where(pick, jnp.broadcast_to(total, shape), 0.0), axis=0, keepdims=True
        )

    def sums_start(i, pairs):
        msg[i] = pack(pairs)
        scatter(msg.at[i], got.at[i], sum_s.at[i], sum_r.at[i], sum_to)

    def sums_end(i, count):
        total = gathered(msg.at[i], got.at[i], sum_r.at[i])
        if not direct:
            msg_z[i] = total
            scatter(msg_z.at[i], got_z.at[i], sum_sz.at[i], sum_rz.at[i], row_z)
            total = gathered(msg_z.at[i], got_z.at[i], sum_rz.at[i])
        shape = (8, 128)
        place = lax.broadcasted_iota(jnp.int32, shape, 0) * PAD
        lane = lax.broadcasted_iota(jnp.int32, shape, 1)
        wide = jnp.broadcast_to(total, shape)
        return [
            jnp.broadcast_to(
                jnp.sum(jnp.where(lane == place + k, wide, 0.0), axis=1, keepdims=True), shape
            )
            for k in range(count)
        ]

    slot = lax.broadcasted_iota(jnp.int32, (deep, ny), 0)
    floor = lax.broadcasted_iota(jnp.int32, (deep, ny), 1) == 0
    lid = lax.broadcasted_iota(jnp.int32, (deep, ny), 1) == ny - 1
    pdiag = 6.0 - jnp.where(bottom | top, 1.0, 0.0)
    loads[4].wait()
    pdiag = pdiag + jnp.where(bottom, column(0), 0.0) + jnp.where(top, column(1), 0.0)
    share = jacobi_weight / pdiag
    prs[4, 0] = pdiag
    loads[5].wait()
    loads[6].wait()

    arrive(first)
    for x in range(cx_n + 4):
        cx, cx_low = face_ref[0, x + 1], face_ref[0, x]
        cz, cy = face_ref[1, x + 1], face_ref[2, x + 1]
        cz_low = pltpu.roll(cz, 1, 0)
        upper = jnp.where(lid, 0.0, cy)
        lower = jnp.where(floor, 0.0, y_prev(cy))
        wall = jnp.where(floor | lid, jnp.broadcast_to(cy[:, ny - 1 :], (deep, ny)), 0.0)
        coef[0, x] = (face_ref[3, x + 1] + (cx + cz)) + ((upper + lower) + wall) + (cx_low + cz_low)
        coef[1, x] = cz_low
        coef[2, x] = upper
        coef[3, x] = lower

    dots = []
    for c in range(3):
        r = src_ref[c] - apply(x0_ref[c], c)
        res_ref[c] = r
        r_own = own(r)
        v = apply(r, c)
        v_own = own(v)
        vk_ref[c, pl.ds(3, cx_n), pl.ds(0, cz_n)] = v[:, :cz_n]
        dots.append([(r_own, r_own), (r_own, v_own)])
    second = to_corners(vk_ref, vk_ref, 3, 2)
    for to, sx, sz in zip(corners, (1, 1, -1, -1), (1, -1, 1, -1)):
        (fx, _), (fz, tz) = side_x(sx, 1, 1, 1), side_z(sz, 1, 1)
        second.append(ship(res_ref, r_far, to, (fx, fz), (side_x(sx, 2, 1, 1)[1], tz)))
    second += to_z(vk_ref, vk_ref, 3, 1, 3)
    for sz in (1, -1):
        fz, tz = side_z(sz, 2, 2)
        second.append(
            ship(res_ref, r_far, north if sz > 0 else south,
                 (pl.ds(1, cx_n), fz), (pl.ds(2, cx_n), tz))
        )
    second += to_x(vk_ref, vk_ref, 3, 1, 3)
    for sx in (1, -1):
        fx, tx = side_x(sx, 1, 2, 2)[0], side_x(sx, 2, 2, 2)[1]
        z = pl.ds(0, cz_n)
        second.append(ship(res_ref, r_far, east if sx > 0 else west, (fx, z), (tx, z)))
    zero = jnp.zeros((8, ny), jnp.float32)
    sums_start(0, [p for d in dots for p in d + [(zero, zero)] * (PAD - 2)])

    aside = exchange_wide(0, map_ref, mzsend, mc_send, mxlo, mxhi, mzlo, mzhi, mc)
    aside.append(send(inv_ref, inv_w, side_s.at[16], side_r.at[16], east))
    aside.append(send(inv_ref, inv_e, side_s.at[17], side_r.at[17], west))
    aside += exchange(3, prs.at[4], dzsend, dxlo, dxhi, dzlo, dzhi)

    arrive(second)
    m0, m1 = sums_end(0, 2)
    sigma = m1 / m0
    mine = (slot <= cz_n) | (slot == deep - 1)
    body_rows = slot < cz_n
    dots = []
    for c in range(3):
        s = sigma[c : c + 1]
        v = vk_ref[c]
        mid_r = jnp.where(mine, res_ref[c, pl.ds(1, cx_n)], r_far[c, pl.ds(2, cx_n)])
        lo_r = jnp.where(body_rows, res_ref[c, 0], r_far[c, 1])
        hi_r = jnp.where(body_rows, res_ref[c, cx_n + 1], r_far[c, cx_n + 2])
        r = jnp.concatenate(
            [r_far[c, pl.ds(0, 1)], lo_r[None], mid_r, hi_r[None], r_far[c, pl.ds(cx_n + 3, 1)]], 0
        )
        u = apply(v, c)
        v = v[1:-1]
        a1 = v - s * r
        a2 = (u - s * v) - s * a1
        a3 = apply(a2, c) - s * a2[1:-1]
        a4 = apply(a3, c) - s * a3[1:-1]
        r0, b1, b2, b3, b4 = own(r), own(a1), own(a2), own(a3), own(a4)
        dots += [
            (r0, b1), (b1, b1), (b1, b2), (b2, b2), (b2, b3), (b3, b3), (b3, b4), (b4, b4)
        ]
        a1_ref[c] = a1[1:-1]
        a2_ref[c] = a2[1:-1]
        a3_ref[c] = a3
    sums_start(1, dots)
    mu = [m0] + sums_end(1, PAD)

    def times(p):
        out = [sigma * p[0]]
        for i in range(1, len(p)):
            out.append(p[i - 1] + sigma * p[i])
        return out + [p[-1]]

    def dot(p, q):
        total = 0.0
        for n in range(len(p) + len(q) - 1):
            terms = [p[i] * q[n - i] for i in range(len(p)) if 0 <= n - i < len(q)]
            total = total + sum(terms[1:], terms[0]) * mu[n]
        return total

    def against(p):
        return sum((p[i] * mu[i] for i in range(1, len(p))), p[0] * mu[0])

    alpha = m0 / (sigma * m0 + mu[1])
    s1 = [1.0 - alpha * sigma, -alpha]
    t1 = times(s1)
    omega = dot(s1, t1) / dot(t1, t1)
    rho_new = against(s1) - omega * against(t1)
    beta = (rho_new / m0) * (alpha / omega)
    r1 = [s1[0] - omega * t1[0], s1[1] - omega * t1[1], -omega * t1[2]]
    p2 = [r1[0] + beta * (1.0 - omega * sigma), r1[1] - beta * omega, r1[2]]
    v2 = times(p2)
    alpha2 = rho_new / against(v2)
    s2 = [r1[i] - alpha2 * v2[i] for i in range(3)] + [-alpha2 * v2[3]]
    t2 = times(s2)
    omega2 = dot(s2, t2) / dot(t2, t2)
    weight = [
        alpha + omega * s1[0] + alpha2 * p2[0] + omega2 * s2[0],
        omega * s1[1] + alpha2 * p2[1] + omega2 * s2[1],
        alpha2 * p2[2] + omega2 * s2[2],
        omega2 * s2[3],
    ]
    speed = []
    for c in range(3):
        w = [k[c : c + 1] for k in weight]
        field = x0_ref[c, pl.ds(1, cx_n + 2)] + w[0] * res_ref[c]
        field += w[1] * a1_ref[c] + w[2] * a2_ref[c] + w[3] * a3_ref[c]
        vel_ref[c] = field[1:-1, :cz_n]
        speed.append(field)
    ux, uz, uy = speed
    div = (ux[1:-1] - ux[:-2]) + (uz[1:-1] - z_roll(uz[1:-1], 1))
    uy = uy[1:-1]
    div = div + (uy - jnp.where(floor, 0.0, y_prev(uy)))
    div = div[:, :cz_n].reshape(rows, ny)

    def operate(f, edges):
        near = x_next(f, edges[1]) + x_prev(f, edges[0])
        near += z_next(f, edges[3]) + z_prev(f, edges[2])
        near += jnp.where(top, 0.0, y_next(f)) + jnp.where(bottom, 0.0, y_prev(f))
        return pdiag * f - near

    def at_face(k, f, beyond, inside, before, after):
        lane = lax.broadcasted_iota(jnp.int32, f.shape, 1)
        before, after = along_face(k, f, before, after)
        near = (beyond + inside) + (before + after)
        near += jnp.where(lane == ny - 1, 0.0, y_next(f)) + jnp.where(lane == 0, 0.0, y_prev(f))
        return face_d[k] * f - near

    def operate_faces(ref, near, far, corner):
        return [
            at_face(k, near[k], far[k], inside, corner[around[k][0]], corner[around[k][1]])
            for k, inside in enumerate(insides(ref))
        ]

    q = share * div
    qref = prs.at[0, 0]
    qref[...] = q
    wide = exchange_wide(8, qref, qzsend, qc_send, qxlo, qxhi, qzlo, qzhi, qc)
    arrive(aside)
    face_d = (dxlo[0], dxhi[0], dzlo[0], dzhi[0])
    face_share = [jacobi_weight / d for d in face_d]
    arrive(wide)
    near, far = split(qxlo[...], qxhi[...], qzlo[...], qzhi[...])
    edges = [
        2.0 * near[k] - face_share[k] * out
        for k, out in enumerate(operate_faces(qref, near, far, [qc[k] for k in range(4)]))
    ]
    q = 2.0 * q - share * operate(q, near)
    res = div - operate(q, edges)
    cells = map_ref[...]
    parts = [
        jnp.sum(jnp.where(cells == m, res, 0.0), axis=0, keepdims=True) for m in range(COARSE)
    ]
    total = jnp.sum(jnp.concatenate(parts, 0), axis=1, keepdims=True)
    shape = (COARSE, lanes)
    place = lax.broadcasted_iota(jnp.int32, shape, 1) == (
        lax.broadcasted_iota(jnp.int32, shape, 0) + gz * COARSE
    )
    msg_c[...] = jnp.sum(
        jnp.where(place, jnp.broadcast_to(total, shape), 0.0), axis=0, keepdims=True
    )
    side = n_gz - 1
    scatter(msg_c, got_w, coarse_s.at[pl.ds(0, n_gz)], coarse_r.at[0], [east] + aside_e)
    scatter(msg_c, got_e, coarse_s.at[pl.ds(n_gz, n_gz)], coarse_r.at[1], [west] + aside_w)
    scatter(msg_c, got_c, coarse_s.at[pl.ds(2 * n_gz, side)], coarse_r.at[2], row_z)
    q = q + share * res
    prs[1, 0] = q
    halo = exchange_pressure(1)
    arrive(halo)
    q = q + share * (div - operate(q, (pxlo[1, 0], pxhi[1, 0], pzlo[1, 0], pzhi[1, 0])))

    spots = (south[1], gz, north[1])

    def corrections(inv, coarse):
        out = []
        for spot in spots:
            block = inv[pl.ds(pl.multiple_of(spot * COARSE, COARSE), COARSE), :]
            col = jnp.sum(block * coarse[:, : block.shape[1]], axis=1, keepdims=True)
            out.append(jnp.broadcast_to(col, (COARSE, ny)))
        return out

    def lift(cell, corr):
        add = jnp.broadcast_to(corr[0:1], cell.shape)
        for m in range(1, COARSE):
            add = jnp.where(cell == m, corr[m : m + 1], add)
        return add

    def whole(got, rsem):
        pltpu.make_async_copy(got, got, rsem).wait()
        return jnp.sum(got[...], axis=0)

    south_k, own_k, north_k = corrections(inv_ref, gathered(msg_c, got_c, coarse_r.at[2]))
    west_k = corrections(inv_w, whole(got_w, coarse_r.at[0]))
    east_k = corrections(inv_e, whole(got_e, coarse_r.at[1]))
    e = lift(cells, own_k)
    eref = prs.at[2, 0]
    eref[...] = e
    near, far = split(
        lift(mxlo[...], west_k[1]),
        lift(mxhi[...], east_k[1]),
        lift(mzlo[...], south_k),
        lift(mzhi[...], north_k),
    )
    points = [
        lift(mc[k], c) for k, c in enumerate((west_k[0], west_k[2], east_k[0], east_k[2]))
    ]
    edges = [
        near[k] - face_share[k] * out
        for k, out in enumerate(operate_faces(eref, near, far, points))
    ]
    e = e - share * operate(e, near)
    e = e - share * operate(e, edges)
    out_ref[...] = q + e
    for copy in pending:
        copy.wait_send()


def body(n_gx, n_gz, velocity_old, source, diag_coef, face_coef, bc_flags, coarse_map, coarse_inverse):
    cx_n, cz_n, ny = diag_coef.shape
    rows = cx_n * cz_n
    deep = cz_n + 8
    group = coarse_inverse.shape[1]
    lanes = -(-group // 128) * 128
    f32 = jnp.float32
    vmem = pltpu.VMEM
    dma = pltpu.SemaphoreType.DMA
    n_sum = n_gx * n_gz - 1 if n_gx * n_gz <= DIRECT else n_gx - 1

    def block(fields, halo):
        return vmem((fields, cx_n + 2 * halo, deep, ny), f32)

    def wide_set(kind):
        return [
            vmem((2 * cz_n, ny), kind),
            vmem((2 * cz_n, ny), kind),
            vmem((2, cx_n, ny), kind),
            vmem((2, cx_n, ny), kind),
            vmem((2, 2, cx_n, ny), kind),
            vmem((4, 1, ny), kind),
            vmem((4, 1, ny), kind),
        ]

    scratch = [
        block(3, 2),
        block(3, 1),
        block(4, 3),
        vmem(bc_flags.shape, jnp.int32),
        vmem((rows, ny), jnp.int32),
        vmem(coarse_inverse.shape, f32),
        block(4, 2),
        block(3, 1),
        block(3, 2),
        block(3, 3),
        block(3, 1),
        block(3, 1),
        block(3, 1),
        vmem((5, 1, rows, ny), f32),
        vmem((2, 1, cz_n, ny), f32),
        vmem((2, 1, cz_n, ny), f32),
        vmem((2, 1, cx_n, ny), f32),
        vmem((2, 1, cx_n, ny), f32),
        vmem((2, 2, 1, cx_n, ny), f32),
        *wide_set(f32),
        *wide_set(jnp.int32),
        vmem((1, cz_n, ny), f32),
        vmem((1, cz_n, ny), f32),
        vmem((1, cx_n, ny), f32),
        vmem((1, cx_n, ny), f32),
        vmem((2, 1, cx_n, ny), f32),
        vmem(coarse_inverse.shape, f32),
        vmem(coarse_inverse.shape, f32),
        vmem((2, 1, 128), f32),
        vmem((2, n_sum, 1, 128), f32),
        vmem((2, 1, 128), f32),
        vmem((2, n_gz - 1, 1, 128), f32),
        vmem((1, lanes), f32),
        vmem((n_gz - 1, 1, lanes), f32),
        vmem((n_gz, 1, lanes), f32),
        vmem((n_gz, 1, lanes), f32),
        dma((4, 4)),
        dma((4, 4)),
        dma((48,)),
        dma((48,)),
        dma((2, n_sum)),
        dma((2,)),
        dma((2, n_gz - 1)),
        dma((2,)),
        dma((3 * n_gz - 1,)),
        dma((3,)),
        dma((7,)),
        dma((18,)),
        dma((18,)),
    ]
    spec = pl.BlockSpec(memory_space=pltpu.VMEM)
    velocity, pressure = pl.pallas_call(
        functools.partial(kernel, (n_gx, n_gz, cx_n, cz_n, ny, lanes)),
        out_shape=(
            jax.ShapeDtypeStruct((3, cx_n, cz_n, ny), f32),
            jax.ShapeDtypeStruct((rows, ny), f32),
        ),
        in_specs=[pl.BlockSpec(memory_space=pltpu.HBM)] * 7,
        out_specs=(spec, spec),
        scratch_shapes=scratch,
        compiler_params=pltpu.CompilerParams(
            collective_id=0, has_side_effects=True, vmem_limit_bytes=48 * 1024 * 1024
        ),
        name="corrector",
    )(
        *[
            pltpu.with_memory_space_constraint(a, pltpu.HBM)
            for a in (
                velocity_old,
                source,
                diag_coef,
                face_coef,
                bc_flags,
                coarse_map.reshape(rows, ny),
                coarse_inverse,
            )
        ]
    )
    return velocity, pressure.reshape(cx_n, cz_n, ny)


def solution(mesh):
    placed = (
        P(None, "gx", "gz", None),
        P(None, "gx", "gz", None),
        P("gx", "gz", None),
        P(None, "gx", "gz", None),
        P(None, "gx", "gz"),
        P("gx", "gz", None),
        P("gx", None),
    )
    return jax.shard_map(
        functools.partial(body, mesh.shape["gx"], mesh.shape["gz"]),
        mesh=mesh,
        in_specs=placed,
        out_specs=(P(None, "gx", "gz", None), P("gx", "gz", None)),
        check_vma=False,
    )
```

```python
import functools

import jax
import jax.numpy as jnp
from jax import lax
from jax.experimental import pallas as pl
from jax.experimental.pallas import tpu as pltpu
from jax.sharding import PartitionSpec as P

COARSE = 16
PAD = 8
DIRECT = 64

jacobi_weight = 2.0 / 3.0
MESH = pl.DeviceIdType.MESH


def kernel(
    dims,
    x0_in, src_in, diag_in, face_in, bc_in, map_in, inv_in,
    vel_ref, out_ref,
    x0_ref, src_ref, face_ref, bc_ref, map_ref, inv_ref,
    coef, res_ref, r_far, vk_ref, a1_ref, a2_ref, a3_ref,
    code_ref, cell_ref, pd_ref, share_ref, q_ref, inv_w, inv_e,
    msg, got, msg_z, got_z, msg_c, got_c,
    near_s, near_r, sum_s, sum_r, sum_sz, sum_rz, coarse_s, coarse_r,
    load_sem, side_s, side_r,
):
    n_gx, n_gz, cx_n, cz_n, ny, lanes = dims
    rows = cx_n * cz_n
    deep = x0_ref.shape[2]
    gx = lax.axis_index("gx")
    gz = lax.axis_index("gz")
    east = (lax.rem(gx + 1, n_gx), gz)
    west = (lax.rem(gx + n_gx - 1, n_gx), gz)
    north = (gx, lax.rem(gz + 1, n_gz))
    south = (gx, lax.rem(gz + n_gz - 1, n_gz))
    row_x = [(lax.rem(gx + d, n_gx), gz) for d in range(1, n_gx)]
    row_z = [(gx, lax.rem(gz + d, n_gz)) for d in range(1, n_gz)]
    direct = n_gx * n_gz <= DIRECT
    pending = []

    def send(src, dst, ssem, rsem, to):
        copy = pltpu.make_async_remote_copy(
            src_ref=src, dst_ref=dst, send_sem=ssem, recv_sem=rsem,
            device_id=to, device_id_type=MESH,
        )
        copy.start()
        pending.append(copy)
        return copy

    corners = [
        (east[0], north[1]), (east[0], south[1]), (west[0], north[1]), (west[0], south[1])
    ]

    def at(offset):
        return (lax.rem(gx + offset[0], n_gx), lax.rem(gz + offset[1], n_gz))

    def fold(d, k):
        return (d % n_gx, k % n_gz)

    around = {fold(d, k) for d in (-1, 0, 1) for k in (-1, 0, 1)} - {(0, 0)}
    spread_to = sorted({fold(d, k) for d in range(-2, 3) for k in range(n_gz)} - {(0, 0)})
    every = {(d, k) for d in range(n_gx) for k in range(n_gz)}
    if direct:
        sum_to = [
            (d, k)
            for k in sorted(range(n_gz), key=lambda k: -min(k, n_gz - k))
            for d in sorted(range(n_gx), key=lambda d: -min(d, n_gx - d))
            if d or k
        ]
        met = set(around)
        while True:
            seen = met | {fold(a + d, b + k) for a, b in around for d, k in met} | {(0, 0)}
            left = sorted(every - seen, key=lambda o: (min(o[1], n_gz - o[1]), o))
            if not left:
                break
            met |= {left[0], fold(-left[0][0], -left[0][1])}
        sum_to = [at(o) for o in sum_to]
    else:
        sum_to = row_x
        met = around | set(spread_to)
        met |= {(d, 0) for d in range(1, n_gx)} | {(0, k) for k in range(1, n_gz)}
    partners = [at(o) for o in sorted(around)] + [at(o) for o in sorted(met - around)]

    def inner(ref, halo):
        return ref.at[..., pl.ds(halo, cx_n), pl.ds(0, cz_n), :]

    loads = [
        pltpu.make_async_copy(a, b, load_sem.at[i])
        for i, (a, b) in enumerate(
            [
                (x0_in, inner(x0_ref, 2)), (face_in, inner(face_ref.at[pl.ds(0, 3)], 3)),
                (diag_in, inner(face_ref.at[3], 3)), (src_in, inner(src_ref, 1)),
                (bc_in, bc_ref), (map_in, map_ref), (inv_in, inv_ref),
            ]
        )
    ]
    for load in loads:
        load.start()
    barrier = pltpu.get_barrier_semaphore()
    for other in partners:
        pl.semaphore_signal(barrier, inc=1, device_id=other, device_id_type=MESH)
    for load in loads[:4]:
        load.wait()
    pl.semaphore_wait(barrier, len(partners))


    def side_x(sign, halo, a, b):
        if sign > 0:
            return pl.ds(halo + cx_n - b, b - a + 1), pl.ds(halo - b, b - a + 1)
        return pl.ds(halo + a - 1, b - a + 1), pl.ds(halo + cx_n + a - 1, b - a + 1)

    def side_z(sign, a, b):
        if sign > 0:
            return pl.ds(cz_n - b, b - a + 1), pl.ds(deep - b, b - a + 1)
        return pl.ds(a - 1, b - a + 1), pl.ds(cz_n + a - 1, b - a + 1)

    used = []

    def ship(src, dst, to, where_from, where_to):
        i = len(used)
        used.append(i)
        return send(
            src.at[(..., *where_from, slice(None))], dst.at[(..., *where_to, slice(None))],
            near_s.at[i], near_r.at[i], to,
        )

    def to_corners(src, dst, halo, n):
        out = []
        for to, sx, sz in zip(corners, (1, 1, -1, -1), (1, -1, 1, -1)):
            (fx, tx), (fz, tz) = side_x(sx, halo, 1, n), side_z(sz, 1, n)
            out.append(ship(src, dst, to, (fx, fz), (tx, tz)))
        return out

    def to_z(src, dst, halo, a, b, ways=(1, -1)):
        out = []
        for sz in ways:
            fz, tz = side_z(sz, a, b)
            x = pl.ds(halo, cx_n)
            out.append(ship(src, dst, north if sz > 0 else south, (x, fz), (x, tz)))
        return out

    def to_x(src, dst, halo, a, b, ways=(1, -1)):
        out = []
        for sx in ways:
            fx, tx = side_x(sx, halo, a, b)
            z = pl.ds(0, cz_n)
            out.append(ship(src, dst, east if sx > 0 else west, (fx, z), (tx, z)))
        return out

    first = to_corners(x0_ref, x0_ref, 2, 1)
    first += to_corners(face_ref, face_ref, 3, 2)
    first += to_z(x0_ref, x0_ref, 2, 1, 2)
    first += to_z(face_ref, face_ref, 3, 1, 2)
    first += to_z(face_ref.at[1], face_ref.at[1], 3, 3, 3, (1,))
    first += to_z(src_ref, src_ref, 1, 1, 1)
    first += to_x(x0_ref, x0_ref, 2, 1, 2)
    first += to_x(face_ref, face_ref, 3, 1, 2)
    first += to_x(face_ref.at[0], face_ref.at[0], 3, 3, 3, (1,))
    first += to_x(src_ref, src_ref, 1, 1, 1)

    def arrive(copies):
        for copy in copies:
            copy.wait_recv()

    level = lax.broadcasted_iota(jnp.int32, (rows, ny), 1)
    bottom = level == 0
    top = level == ny - 1
    def y_prev(f):
        return pltpu.roll(f, 1, f.ndim - 1)

    def y_next(f):
        return pltpu.roll(f, ny - 1, f.ndim - 1)

    eye = lax.broadcasted_iota(jnp.int32, (cz_n, cz_n), 0) == lax.broadcasted_iota(
        jnp.int32, (cz_n, cz_n), 1
    )

    def column(side):
        flags = bc_ref[side]
        parts = [
            jnp.sum(
                jnp.where(eye, jnp.broadcast_to(flags[i : i + 1], (cz_n, cz_n)), 0),
                axis=1, keepdims=True,
            )
            for i in range(cx_n)
        ]
        return jnp.broadcast_to(jnp.concatenate(parts, 0), (rows, ny))

    def scatter(msg, got, ssem, rsem, others):
        return [
            send(msg, got.at[d], ssem.at[d], rsem, to) for d, to in enumerate(others)
        ]

    def gathered(msg, got, rsem):
        pltpu.make_async_copy(got, got, rsem).wait()
        return msg[...] + jnp.sum(got[...], axis=0)


    def z_roll(f, shift):
        flat = f.reshape((-1,) + f.shape[-2:])
        return pltpu.roll(flat, shift % deep, 1).reshape(f.shape)

    def apply(f, c):
        h = (f.shape[0] - cx_n) // 2 - 1
        n = cx_n + 2 * h
        g = f[1:-1]
        total = coef[0, pl.ds(2 - h, n)] * g
        total -= face_ref[0, pl.ds(3 - h, n)] * f[2:] + face_ref[0, pl.ds(2 - h, n)] * f[:-2]
        total -= face_ref[1, pl.ds(3 - h, n)] * z_roll(g, -1) + coef[1, pl.ds(2 - h, n)] * z_roll(g, 1)
        total -= coef[2, pl.ds(2 - h, n)] * y_next(g) + coef[3, pl.ds(2 - h, n)] * y_prev(g)
        return total

    def own(f):
        h = (f.shape[0] - cx_n) // 2
        return f[h : h + cx_n, :cz_n].reshape(rows, ny)

    def pack(pairs):
        sums = [jnp.sum(a * b, axis=0, keepdims=True) for a, b in pairs]
        while len(sums) < 3 * PAD:
            sums.append(jnp.zeros_like(sums[0]))
        total = jnp.sum(jnp.concatenate(sums, 0), axis=1, keepdims=True)
        shape = (3 * PAD, 128)
        pick = lax.broadcasted_iota(jnp.int32, shape, 0) == lax.broadcasted_iota(
            jnp.int32, shape, 1
        )
        return jnp.sum(
            jnp.where(pick, jnp.broadcast_to(total, shape), 0.0), axis=0, keepdims=True
        )

    def sums_start(i, pairs):
        msg[i] = pack(pairs)
        scatter(msg.at[i], got.at[i], sum_s.at[i], sum_r.at[i], sum_to)

    def sums_end(i, count):
        total = gathered(msg.at[i], got.at[i], sum_r.at[i])
        if not direct:
            msg_z[i] = total
            scatter(msg_z.at[i], got_z.at[i], sum_sz.at[i], sum_rz.at[i], row_z)
            total = gathered(msg_z.at[i], got_z.at[i], sum_rz.at[i])
        shape = (8, 128)
        place = lax.broadcasted_iota(jnp.int32, shape, 0) * PAD
        lane = lax.broadcasted_iota(jnp.int32, shape, 1)
        wide = jnp.broadcast_to(total, shape)
        return [
            jnp.broadcast_to(
                jnp.sum(jnp.where(lane == place + k, wide, 0.0), axis=1, keepdims=True), shape
            )
            for k in range(count)
        ]

    slot = lax.broadcasted_iota(jnp.int32, (deep, ny), 0)
    floor = lax.broadcasted_iota(jnp.int32, (deep, ny), 1) == 0
    lid = lax.broadcasted_iota(jnp.int32, (deep, ny), 1) == ny - 1
    for load in loads[4:]:
        load.wait()
    flag = jnp.where(bottom, column(0), 0) + jnp.where(top, column(1), 0)
    code = map_ref[...] + COARSE * flag
    code_ref[pl.ds(2, cx_n), pl.ds(0, cz_n)] = code.reshape(cx_n, cz_n, ny)

    arrive(first)
    for x in range(cx_n + 4):
        cx, cx_low = face_ref[0, x + 1], face_ref[0, x]
        cz, cy = face_ref[1, x + 1], face_ref[2, x + 1]
        cz_low = pltpu.roll(cz, 1, 0)
        upper = jnp.where(lid, 0.0, cy)
        lower = jnp.where(floor, 0.0, y_prev(cy))
        wall = jnp.where(floor | lid, jnp.broadcast_to(cy[:, ny - 1 :], (deep, ny)), 0.0)
        coef[0, x] = (face_ref[3, x + 1] + (cx + cz)) + ((upper + lower) + wall) + (cx_low + cz_low)
        coef[1, x] = cz_low
        coef[2, x] = upper
        coef[3, x] = lower

    dots = []
    for c in range(3):
        r = src_ref[c] - apply(x0_ref[c], c)
        res_ref[c] = r
        r_own = own(r)
        v = apply(r, c)
        v_own = own(v)
        vk_ref[c, pl.ds(3, cx_n), pl.ds(0, cz_n)] = v[:, :cz_n]
        dots.append([(r_own, r_own), (r_own, v_own)])
    second = to_corners(vk_ref, vk_ref, 3, 2)
    for to, sx, sz in zip(corners, (1, 1, -1, -1), (1, -1, 1, -1)):
        (fx, _), (fz, tz) = side_x(sx, 1, 1, 1), side_z(sz, 1, 1)
        second.append(ship(res_ref, r_far, to, (fx, fz), (side_x(sx, 2, 1, 1)[1], tz)))
    second += to_z(vk_ref, vk_ref, 3, 1, 3)
    for sz in (1, -1):
        fz, tz = side_z(sz, 2, 2)
        second.append(
            ship(res_ref, r_far, north if sz > 0 else south,
                 (pl.ds(1, cx_n), fz), (pl.ds(2, cx_n), tz))
        )
    second += to_x(vk_ref, vk_ref, 3, 1, 3)
    for sx in (1, -1):
        fx, tx = side_x(sx, 1, 2, 2)[0], side_x(sx, 2, 2, 2)[1]
        z = pl.ds(0, cz_n)
        second.append(ship(res_ref, r_far, east if sx > 0 else west, (fx, z), (tx, z)))
    zero = jnp.zeros((8, ny), jnp.float32)
    sums_start(0, [p for d in dots for p in d + [(zero, zero)] * (PAD - 2)])

    aside = to_corners(code_ref, code_ref, 2, 1)
    aside += to_z(code_ref, code_ref, 2, 1, 2)
    aside += to_x(code_ref, code_ref, 2, 1, 2)
    aside.append(send(inv_ref, inv_w, side_s.at[0], side_r.at[0], east))
    aside.append(send(inv_ref, inv_e, side_s.at[1], side_r.at[1], west))

    arrive(second)
    m0, m1 = sums_end(0, 2)
    sigma = m1 / m0
    mine = (slot <= cz_n) | (slot == deep - 1)
    body_rows = slot < cz_n
    dots = []
    for c in range(3):
        s = sigma[c : c + 1]
        v = vk_ref[c]
        mid_r = jnp.where(mine, res_ref[c, pl.ds(1, cx_n)], r_far[c, pl.ds(2, cx_n)])
        lo_r = jnp.where(body_rows, res_ref[c, 0], r_far[c, 1])
        hi_r = jnp.where(body_rows, res_ref[c, cx_n + 1], r_far[c, cx_n + 2])
        r = jnp.concatenate(
            [r_far[c, pl.ds(0, 1)], lo_r[None], mid_r, hi_r[None], r_far[c, pl.ds(cx_n + 3, 1)]], 0
        )
        u = apply(v, c)
        v = v[1:-1]
        a1 = v - s * r
        a2 = (u - s * v) - s * a1
        a3 = apply(a2, c) - s * a2[1:-1]
        a4 = apply(a3, c) - s * a3[1:-1]
        r0, b1, b2, b3, b4 = own(r), own(a1), own(a2), own(a3), own(a4)
        dots += [
            (r0, b1), (b1, b1), (b1, b2), (b2, b2), (b2, b3), (b3, b3), (b3, b4), (b4, b4)
        ]
        a1_ref[c] = a1[1:-1]
        a2_ref[c] = a2[1:-1]
        a3_ref[c] = a3
    sums_start(1, dots)
    arrive(aside)
    for x in range(cx_n + 4):
        mark = code_ref[x] >= COARSE
        edge = floor | lid
        pd = jnp.where(edge, jnp.where(mark, 6.0, 5.0), 6.0)
        pd_ref[x] = pd
        share_ref[x] = jacobi_weight / pd
        cell_ref[x] = jnp.where(mark, code_ref[x] - COARSE, code_ref[x])
    mu = [m0] + sums_end(1, PAD)

    def times(p):
        out = [sigma * p[0]]
        for i in range(1, len(p)):
            out.append(p[i - 1] + sigma * p[i])
        return out + [p[-1]]

    def dot(p, q):
        total = 0.0
        for n in range(len(p) + len(q) - 1):
            terms = [p[i] * q[n - i] for i in range(len(p)) if 0 <= n - i < len(q)]
            total = total + sum(terms[1:], terms[0]) * mu[n]
        return total

    def against(p):
        return sum((p[i] * mu[i] for i in range(1, len(p))), p[0] * mu[0])

    alpha = m0 / (sigma * m0 + mu[1])
    s1 = [1.0 - alpha * sigma, -alpha]
    t1 = times(s1)
    omega = dot(s1, t1) / dot(t1, t1)
    rho_new = against(s1) - omega * against(t1)
    beta = (rho_new / m0) * (alpha / omega)
    r1 = [s1[0] - omega * t1[0], s1[1] - omega * t1[1], -omega * t1[2]]
    p2 = [r1[0] + beta * (1.0 - omega * sigma), r1[1] - beta * omega, r1[2]]
    v2 = times(p2)
    alpha2 = rho_new / against(v2)
    s2 = [r1[i] - alpha2 * v2[i] for i in range(3)] + [-alpha2 * v2[3]]
    t2 = times(s2)
    omega2 = dot(s2, t2) / dot(t2, t2)
    weight = [
        alpha + omega * s1[0] + alpha2 * p2[0] + omega2 * s2[0],
        omega * s1[1] + alpha2 * p2[1] + omega2 * s2[1],
        alpha2 * p2[2] + omega2 * s2[2],
        omega2 * s2[3],
    ]
    speed = []
    for c in range(3):
        w = [k[c : c + 1] for k in weight]
        field = x0_ref[c, pl.ds(1, cx_n + 2)] + w[0] * res_ref[c]
        field += w[1] * a1_ref[c] + w[2] * a2_ref[c] + w[3] * a3_ref[c]
        vel_ref[c] = field[1:-1, :cz_n]
        speed.append(field)
    ux, uz, uy = speed
    div = (ux[1:-1] - ux[:-2]) + (uz[1:-1] - z_roll(uz[1:-1], 1))
    uy = uy[1:-1]
    div = div + (uy - jnp.where(floor, 0.0, y_prev(uy)))
    share = share_ref[pl.ds(2, cx_n)]
    q = share * div
    q_ref[pl.ds(3, cx_n), pl.ds(0, cz_n)] = q[:, :cz_n]
    third = to_corners(q_ref, q_ref, 3, 2)
    third += to_z(q_ref, q_ref, 3, 1, 3)
    third += to_x(q_ref, q_ref, 3, 1, 3)

    def smooth(f):
        n = f.shape[0] - 2
        h = (n - cx_n) // 2
        g = f[1:-1]
        near = (f[2:] + f[:-2]) + (z_roll(g, 1) + z_roll(g, -1))
        near += jnp.where(lid, 0.0, y_next(g)) + jnp.where(floor, 0.0, y_prev(g))
        return pd_ref[pl.ds(2 - h, n)] * g - near

    def shares(h):
        return share_ref[pl.ds(2 - h, cx_n + 2 * h)]

    blank = jnp.zeros((2, deep, ny), jnp.float32)
    mine = jnp.where(body_rows, q, 0.0)
    first_cut = -smooth(jnp.concatenate([blank, mine, blank], 0))
    trace = jnp.concatenate(
        [first_cut[:1], first_cut[1:-1] + jnp.where(body_rows, div, 0.0), first_cut[-1:]], 0
    )
    full = jnp.concatenate([blank[:1], trace, blank[:1]], 0)
    full = full - smooth(jnp.concatenate([blank, shares(1) * trace, blank], 0))

    part = [[] for _ in range(6)]
    for m in range(COARSE):
        hit = jnp.where(cell_ref[...] == m, full, 0.0)
        flat = hit[:, :cz_n].reshape(-1, 8, ny)
        step = cz_n // 8
        top_rows = hit[:, cz_n:]
        part[0].append(jnp.sum(flat[: 2 * step], axis=0, keepdims=True))
        part[1].append(jnp.sum(flat[2 * step : -2 * step], axis=0, keepdims=True))
        part[2].append(jnp.sum(flat[-2 * step :], axis=0, keepdims=True))
        part[3].append(top_rows[1:2])
        part[4].append(jnp.sum(top_rows[2:-2], axis=0, keepdims=True))
        part[5].append(top_rows[-2:-1])
    part = [jnp.concatenate(p, 0) for p in part]
    upper_half = lax.broadcasted_iota(jnp.int32, (COARSE, 8, ny), 1) < 4

    def total_of(p):
        return jnp.sum(jnp.sum(p, axis=1), axis=1, keepdims=True)

    shape = (COARSE, lanes)
    spots = (south[1], gz, north[1])
    places = [
        lax.broadcasted_iota(jnp.int32, shape, 1)
        == lax.broadcasted_iota(jnp.int32, shape, 0) + spot * COARSE
        for spot in spots
    ]
    for k in range(3):
        cols = [
            total_of(jnp.where(upper_half, 0.0, part[3 + k])), total_of(part[k]),
            total_of(jnp.where(upper_half, part[3 + k], 0.0)),
        ]
        line = sum(
            jnp.where(place, jnp.broadcast_to(col, shape), 0.0)
            for place, col in zip(places, cols)
        )
        msg_c[k] = jnp.sum(line, axis=0, keepdims=True)
    scatter(msg_c, got_c, coarse_s, coarse_r, [at(o) for o in spread_to])

    arrive(third)
    ext = q_ref[...]
    q = 2.0 * ext[1:-1] - shares(2) * smooth(ext)
    q = q[1:-1] + ext[2:-2] - shares(1) * smooth(q)
    q = q[1:-1] + ext[3:-3] - shares(0) * smooth(q)

    pltpu.make_async_copy(got_c, got_c, coarse_r).wait()

    def restricted(t):
        rows_in = [
            got_c[spread_to.index(fold(-j, k)), t - j + 1]
            for j in (t - 1, t, t + 1) for k in range(n_gz) if fold(-j, k) != (0, 0)
        ]
        return sum(rows_in, msg_c[t + 1])

    def corrections(inv, coarse):
        out = []
        for spot in spots:
            block = inv[pl.ds(pl.multiple_of(spot * COARSE, COARSE), COARSE), :]
            col = jnp.sum(block * coarse[:, : block.shape[1]], axis=1, keepdims=True)
            out.append(jnp.broadcast_to(col, (COARSE, ny)))
        return out

    def lift(cell, pick):
        add = jnp.broadcast_to(pick(0), cell.shape)
        for m in range(1, COARSE):
            add = jnp.where(cell == m, pick(m), add)
        return add

    corr = [corrections(inv, restricted(t)) for inv, t in zip((inv_w, inv_ref, inv_e), (-1, 0, 1))]
    half = lax.broadcasted_iota(jnp.int32, (8, ny), 0) < 4
    spans = (pl.ds(0, 2), pl.ds(2, cx_n), pl.ds(cx_n + 2, 2))
    raised = []
    for k in range(3):
        cell = cell_ref[spans[k]]
        inside = lift(cell[:, :cz_n], lambda m: corr[k][1][m : m + 1])
        outside = lift(
            cell[:, cz_n:], lambda m: jnp.where(half, corr[k][2][m : m + 1], corr[k][0][m : m + 1])
        )
        raised.append(jnp.concatenate([inside, outside], 1))
    e = jnp.concatenate(raised, 0)
    e = e[1:-1] - shares(1) * smooth(e)
    e = e[1:-1] - shares(0) * smooth(e)
    out_ref[...] = (q + e)[:, :cz_n]
    for copy in pending:
        copy.wait_send()


def body(n_gx, n_gz, velocity_old, source, diag_coef, face_coef, bc_flags, coarse_map, coarse_inverse):
    cx_n, cz_n, ny = diag_coef.shape
    rows = cx_n * cz_n
    deep = cz_n + 8
    group = coarse_inverse.shape[1]
    lanes = -(-group // 128) * 128
    f32 = jnp.float32
    vmem = pltpu.VMEM
    dma = pltpu.SemaphoreType.DMA
    n_spread = min(5, n_gx) * n_gz - 1
    n_sum = n_gx * n_gz - 1 if n_gx * n_gz <= DIRECT else n_gx - 1

    def block(fields, halo):
        return vmem((fields, cx_n + 2 * halo, deep, ny), f32)

    scratch = [
        block(3, 2),
        block(3, 1),
        block(4, 3),
        vmem(bc_flags.shape, jnp.int32),
        vmem((rows, ny), jnp.int32),
        vmem(coarse_inverse.shape, f32),
        block(4, 2),
        block(3, 1),
        block(3, 2),
        block(3, 3),
        block(3, 1),
        block(3, 1),
        block(3, 1),
        vmem((cx_n + 4, deep, ny), jnp.int32),
        vmem((cx_n + 4, deep, ny), jnp.int32),
        vmem((cx_n + 4, deep, ny), f32),
        vmem((cx_n + 4, deep, ny), f32),
        vmem((cx_n + 6, deep, ny), f32),
        vmem(coarse_inverse.shape, f32),
        vmem(coarse_inverse.shape, f32),
        vmem((2, 1, 128), f32),
        vmem((2, n_sum, 1, 128), f32),
        vmem((2, 1, 128), f32),
        vmem((2, n_gz - 1, 1, 128), f32),
        vmem((3, 1, lanes), f32),
        vmem((n_spread, 3, 1, lanes), f32),
        dma((64,)),
        dma((64,)),
        dma((2, n_sum)),
        dma((2,)),
        dma((2, n_gz - 1)),
        dma((2,)),
        dma((n_spread,)),
        dma,
        dma((7,)),
        dma((2,)),
        dma((2,)),
    ]
    spec = pl.BlockSpec(memory_space=pltpu.VMEM)
    velocity, pressure = pl.pallas_call(
        functools.partial(kernel, (n_gx, n_gz, cx_n, cz_n, ny, lanes)),
        out_shape=(
            jax.ShapeDtypeStruct((3, cx_n, cz_n, ny), f32),
            jax.ShapeDtypeStruct((cx_n, cz_n, ny), f32),
        ),
        in_specs=[pl.BlockSpec(memory_space=pltpu.HBM)] * 7,
        out_specs=(spec, spec),
        scratch_shapes=scratch,
        compiler_params=pltpu.CompilerParams(
            collective_id=0, has_side_effects=True, vmem_limit_bytes=48 * 1024 * 1024
        ),
        name="corrector",
    )(
        *[
            pltpu.with_memory_space_constraint(a, pltpu.HBM)
            for a in (
                velocity_old,
                source,
                diag_coef,
                face_coef,
                bc_flags,
                coarse_map.reshape(rows, ny),
                coarse_inverse,
            )
        ]
    )
    return velocity, pressure


def solution(mesh):
    placed = (
        P(None, "gx", "gz", None),
        P(None, "gx", "gz", None),
        P("gx", "gz", None),
        P(None, "gx", "gz", None),
        P(None, "gx", "gz"),
        P("gx", "gz", None),
        P("gx", None),
    )
    return jax.shard_map(
        functools.partial(body, mesh.shape["gx"], mesh.shape["gz"]),
        mesh=mesh,
        in_specs=placed,
        out_specs=(P(None, "gx", "gz", None), P("gx", "gz", None)),
        check_vma=False,
    )
```

```python
import functools

import jax
import jax.numpy as jnp
from jax import lax
from jax.experimental import pallas as pl
from jax.experimental.pallas import tpu as pltpu
from jax.sharding import PartitionSpec as P

COARSE = 16
PAD = 8
DIRECT = 64

jacobi_weight = 2.0 / 3.0
MESH = pl.DeviceIdType.MESH


def kernel(
    dims,
    x0_in, src_in, diag_in, face_in, bc_in, map_in, inv_in,
    vel_ref, out_ref,
    x0_ref, src_ref, face_ref, bc_ref, map_ref, inv_ref,
    coef, res_ref, r_far, vk_ref, a1_ref, a2_ref, a3_ref,
    code_ref, cell_ref, pd_ref, share_ref, q_ref, inv_w, inv_e,
    msg, got, msg_z, got_z, msg_c, got_c,
    near_s, near_r, sum_s, sum_r, sum_sz, sum_rz, coarse_s, coarse_r,
    load_sem, side_s, side_r,
):
    n_gx, n_gz, cx_n, cz_n, ny, lanes = dims
    rows = cx_n * cz_n
    deep = x0_ref.shape[2]
    gx = lax.axis_index("gx")
    gz = lax.axis_index("gz")
    east = (lax.rem(gx + 1, n_gx), gz)
    west = (lax.rem(gx + n_gx - 1, n_gx), gz)
    north = (gx, lax.rem(gz + 1, n_gz))
    south = (gx, lax.rem(gz + n_gz - 1, n_gz))
    row_x = [(lax.rem(gx + d, n_gx), gz) for d in range(1, n_gx)]
    row_z = [(gx, lax.rem(gz + d, n_gz)) for d in range(1, n_gz)]
    direct = n_gx * n_gz <= DIRECT
    pending = []

    def send(src, dst, ssem, rsem, to):
        copy = pltpu.make_async_remote_copy(
            src_ref=src, dst_ref=dst, send_sem=ssem, recv_sem=rsem,
            device_id=to, device_id_type=MESH,
        )
        copy.start()
        pending.append(copy)
        return copy

    corners = [
        (east[0], north[1]), (east[0], south[1]), (west[0], north[1]), (west[0], south[1])
    ]

    def at(offset):
        return (lax.rem(gx + offset[0], n_gx), lax.rem(gz + offset[1], n_gz))

    def fold(d, k):
        return (d % n_gx, k % n_gz)

    around = {fold(d, k) for d in (-1, 0, 1) for k in (-1, 0, 1)} - {(0, 0)}
    spread_to = sorted({fold(d, k) for d in range(-2, 3) for k in range(n_gz)} - {(0, 0)})
    every = {(d, k) for d in range(n_gx) for k in range(n_gz)}
    if direct:
        sum_to = [
            (d, k)
            for k in sorted(range(n_gz), key=lambda k: -min(k, n_gz - k))
            for d in sorted(range(n_gx), key=lambda d: -min(d, n_gx - d))
            if d or k
        ]
        met = set(around)
        while True:
            seen = met | {fold(a + d, b + k) for a, b in around for d, k in met} | {(0, 0)}
            left = sorted(every - seen, key=lambda o: (min(o[1], n_gz - o[1]), o))
            if not left:
                break
            met |= {left[0], fold(-left[0][0], -left[0][1])}
        sum_to = [at(o) for o in sum_to]
    else:
        sum_to = row_x
        met = around | set(spread_to)
        met |= {(d, 0) for d in range(1, n_gx)} | {(0, k) for k in range(1, n_gz)}
    partners = [at(o) for o in sorted(around)] + [at(o) for o in sorted(met - around)]

    def inner(ref, halo):
        return ref.at[..., pl.ds(halo, cx_n), pl.ds(0, cz_n), :]

    loads = [
        pltpu.make_async_copy(a, b, load_sem.at[i])
        for i, (a, b) in enumerate(
            [
                (x0_in, inner(x0_ref, 2)), (face_in, inner(face_ref.at[pl.ds(0, 3)], 3)),
                (diag_in, inner(face_ref.at[3], 3)), (src_in, inner(src_ref, 1)),
                (bc_in, bc_ref), (map_in, map_ref), (inv_in, inv_ref),
            ]
        )
    ]
    for load in loads:
        load.start()
    barrier = pltpu.get_barrier_semaphore()
    for other in partners:
        pl.semaphore_signal(barrier, inc=1, device_id=other, device_id_type=MESH)
    for load in loads[:4]:
        load.wait()
    pl.semaphore_wait(barrier, len(partners))


    def side_x(sign, halo, a, b):
        if sign > 0:
            return pl.ds(halo + cx_n - b, b - a + 1), pl.ds(halo - b, b - a + 1)
        return pl.ds(halo + a - 1, b - a + 1), pl.ds(halo + cx_n + a - 1, b - a + 1)

    def side_z(sign, a, b):
        if sign > 0:
            return pl.ds(cz_n - b, b - a + 1), pl.ds(deep - b, b - a + 1)
        return pl.ds(a - 1, b - a + 1), pl.ds(cz_n + a - 1, b - a + 1)

    used = []

    def ship(src, dst, to, where_from, where_to):
        i = len(used)
        used.append(i)
        return send(
            src.at[(..., *where_from, slice(None))], dst.at[(..., *where_to, slice(None))],
            near_s.at[i], near_r.at[i], to,
        )

    def to_corners(src, dst, halo, n):
        out = []
        for to, sx, sz in zip(corners, (1, 1, -1, -1), (1, -1, 1, -1)):
            (fx, tx), (fz, tz) = side_x(sx, halo, 1, n), side_z(sz, 1, n)
            out.append(ship(src, dst, to, (fx, fz), (tx, tz)))
        return out

    def to_z(src, dst, halo, a, b, ways=(1, -1)):
        out = []
        for sz in ways:
            fz, tz = side_z(sz, a, b)
            x = pl.ds(halo, cx_n)
            out.append(ship(src, dst, north if sz > 0 else south, (x, fz), (x, tz)))
        return out

    def to_x(src, dst, halo, a, b, ways=(1, -1)):
        out = []
        for sx in ways:
            fx, tx = side_x(sx, halo, a, b)
            z = pl.ds(0, cz_n)
            out.append(ship(src, dst, east if sx > 0 else west, (fx, z), (tx, z)))
        return out

    first = to_corners(x0_ref, x0_ref, 2, 1)
    first += to_corners(face_ref, face_ref, 3, 2)
    first += to_z(x0_ref, x0_ref, 2, 1, 2)
    first += to_z(face_ref, face_ref, 3, 1, 2)
    first += to_z(face_ref.at[1], face_ref.at[1], 3, 3, 3, (1,))
    first += to_z(src_ref, src_ref, 1, 1, 1)
    first += to_x(x0_ref, x0_ref, 2, 1, 2)
    first += to_x(face_ref, face_ref, 3, 1, 2)
    first += to_x(face_ref.at[0], face_ref.at[0], 3, 3, 3, (1,))
    first += to_x(src_ref, src_ref, 1, 1, 1)

    def arrive(copies):
        for copy in copies:
            copy.wait_recv()

    level = lax.broadcasted_iota(jnp.int32, (rows, ny), 1)
    bottom = level == 0
    top = level == ny - 1
    def y_prev(f):
        return pltpu.roll(f, 1, f.ndim - 1)

    def y_next(f):
        return pltpu.roll(f, ny - 1, f.ndim - 1)

    eye = lax.broadcasted_iota(jnp.int32, (cz_n, cz_n), 0) == lax.broadcasted_iota(
        jnp.int32, (cz_n, cz_n), 1
    )

    def column(side):
        flags = bc_ref[side]
        parts = [
            jnp.sum(
                jnp.where(eye, jnp.broadcast_to(flags[i : i + 1], (cz_n, cz_n)), 0),
                axis=1, keepdims=True,
            )
            for i in range(cx_n)
        ]
        return jnp.broadcast_to(jnp.concatenate(parts, 0), (rows, ny))

    def scatter(msg, got, ssem, rsem, others):
        return [
            send(msg, got.at[d], ssem.at[d], rsem, to) for d, to in enumerate(others)
        ]

    def gathered(msg, got, rsem):
        pltpu.make_async_copy(got, got, rsem).wait()
        return msg[...] + jnp.sum(got[...], axis=0)


    def z_roll(f, shift):
        flat = f.reshape((-1,) + f.shape[-2:])
        return pltpu.roll(flat, shift % deep, 1).reshape(f.shape)

    def apply(f, c):
        h = (f.shape[0] - cx_n) // 2 - 1
        n = cx_n + 2 * h
        g = f[1:-1]
        total = coef[0, pl.ds(2 - h, n)] * g
        total -= face_ref[0, pl.ds(3 - h, n)] * f[2:] + face_ref[0, pl.ds(2 - h, n)] * f[:-2]
        total -= face_ref[1, pl.ds(3 - h, n)] * z_roll(g, -1) + coef[1, pl.ds(2 - h, n)] * z_roll(g, 1)
        total -= coef[2, pl.ds(2 - h, n)] * y_next(g) + coef[3, pl.ds(2 - h, n)] * y_prev(g)
        return total

    def own(f):
        h = (f.shape[0] - cx_n) // 2
        return f[h : h + cx_n, :cz_n].reshape(rows, ny)

    def pack(pairs):
        sums = [jnp.sum(a * b, axis=0, keepdims=True) for a, b in pairs]
        while len(sums) < 3 * PAD:
            sums.append(jnp.zeros_like(sums[0]))
        total = jnp.sum(jnp.concatenate(sums, 0), axis=1, keepdims=True)
        shape = (3 * PAD, 128)
        pick = lax.broadcasted_iota(jnp.int32, shape, 0) == lax.broadcasted_iota(
            jnp.int32, shape, 1
        )
        return jnp.sum(
            jnp.where(pick, jnp.broadcast_to(total, shape), 0.0), axis=0, keepdims=True
        )

    def sums_start(i, pairs):
        msg[i] = pack(pairs)
        scatter(msg.at[i], got.at[i], sum_s.at[i], sum_r.at[i], sum_to)

    def sums_end(i, count):
        total = gathered(msg.at[i], got.at[i], sum_r.at[i])
        if not direct:
            msg_z[i] = total
            scatter(msg_z.at[i], got_z.at[i], sum_sz.at[i], sum_rz.at[i], row_z)
            total = gathered(msg_z.at[i], got_z.at[i], sum_rz.at[i])
        shape = (8, 128)
        place = lax.broadcasted_iota(jnp.int32, shape, 0) * PAD
        lane = lax.broadcasted_iota(jnp.int32, shape, 1)
        wide = jnp.broadcast_to(total, shape)
        return [
            jnp.broadcast_to(
                jnp.sum(jnp.where(lane == place + k, wide, 0.0), axis=1, keepdims=True), shape
            )
            for k in range(count)
        ]

    slot = lax.broadcasted_iota(jnp.int32, (deep, ny), 0)
    floor = lax.broadcasted_iota(jnp.int32, (deep, ny), 1) == 0
    lid = lax.broadcasted_iota(jnp.int32, (deep, ny), 1) == ny - 1
    for load in loads[4:]:
        load.wait()
    flag = jnp.where(bottom, column(0), 0) + jnp.where(top, column(1), 0)
    code = map_ref[...] + COARSE * flag
    code_ref[pl.ds(2, cx_n), pl.ds(0, cz_n)] = code.reshape(cx_n, cz_n, ny)

    aside = to_corners(code_ref, code_ref, 2, 1)
    aside += to_z(code_ref, code_ref, 2, 1, 2)
    aside += to_x(code_ref, code_ref, 2, 1, 2)
    aside.append(send(inv_ref, inv_w, side_s.at[0], side_r.at[0], east))
    aside.append(send(inv_ref, inv_e, side_s.at[1], side_r.at[1], west))

    arrive(first)
    for x in range(cx_n + 4):
        cx, cx_low = face_ref[0, x + 1], face_ref[0, x]
        cz, cy = face_ref[1, x + 1], face_ref[2, x + 1]
        cz_low = pltpu.roll(cz, 1, 0)
        upper = jnp.where(lid, 0.0, cy)
        lower = jnp.where(floor, 0.0, y_prev(cy))
        wall = jnp.where(floor | lid, jnp.broadcast_to(cy[:, ny - 1 :], (deep, ny)), 0.0)
        coef[0, x] = (face_ref[3, x + 1] + (cx + cz)) + ((upper + lower) + wall) + (cx_low + cz_low)
        coef[1, x] = cz_low
        coef[2, x] = upper
        coef[3, x] = lower

    dots = []
    for c in range(3):
        r = src_ref[c] - apply(x0_ref[c], c)
        res_ref[c] = r
        r_own = own(r)
        v = apply(r, c)
        v_own = own(v)
        vk_ref[c, pl.ds(3, cx_n), pl.ds(0, cz_n)] = v[:, :cz_n]
        dots.append([(r_own, r_own), (r_own, v_own)])
    second = to_corners(vk_ref, vk_ref, 3, 2)
    for to, sx, sz in zip(corners, (1, 1, -1, -1), (1, -1, 1, -1)):
        (fx, _), (fz, tz) = side_x(sx, 1, 1, 1), side_z(sz, 1, 1)
        second.append(ship(res_ref, r_far, to, (fx, fz), (side_x(sx, 2, 1, 1)[1], tz)))
    zero = jnp.zeros((8, ny), jnp.float32)
    sums_start(0, [p for d in dots for p in d + [(zero, zero)] * (PAD - 2)])
    second += to_z(vk_ref, vk_ref, 3, 1, 3)
    for sz in (1, -1):
        fz, tz = side_z(sz, 2, 2)
        second.append(
            ship(res_ref, r_far, north if sz > 0 else south,
                 (pl.ds(1, cx_n), fz), (pl.ds(2, cx_n), tz))
        )
    second += to_x(vk_ref, vk_ref, 3, 1, 3)
    for sx in (1, -1):
        fx, tx = side_x(sx, 1, 2, 2)[0], side_x(sx, 2, 2, 2)[1]
        z = pl.ds(0, cz_n)
        second.append(ship(res_ref, r_far, east if sx > 0 else west, (fx, z), (tx, z)))

    arrive(second)
    m0, m1 = sums_end(0, 2)
    sigma = m1 / m0
    mine = (slot <= cz_n) | (slot == deep - 1)
    body_rows = slot < cz_n
    dots = []
    for c in range(3):
        s = sigma[c : c + 1]
        v = vk_ref[c]
        mid_r = jnp.where(mine, res_ref[c, pl.ds(1, cx_n)], r_far[c, pl.ds(2, cx_n)])
        lo_r = jnp.where(body_rows, res_ref[c, 0], r_far[c, 1])
        hi_r = jnp.where(body_rows, res_ref[c, cx_n + 1], r_far[c, cx_n + 2])
        r = jnp.concatenate(
            [r_far[c, pl.ds(0, 1)], lo_r[None], mid_r, hi_r[None], r_far[c, pl.ds(cx_n + 3, 1)]], 0
        )
        u = apply(v, c)
        v = v[1:-1]
        a1 = v - s * r
        a2 = (u - s * v) - s * a1
        a3 = apply(a2, c) - s * a2[1:-1]
        a4 = apply(a3, c) - s * a3[1:-1]
        r0, b1, b2, b3, b4 = own(r), own(a1), own(a2), own(a3), own(a4)
        dots += [
            (r0, b1), (b1, b1), (b1, b2), (b2, b2), (b2, b3), (b3, b3), (b3, b4), (b4, b4)
        ]
        a1_ref[c] = a1[1:-1]
        a2_ref[c] = a2[1:-1]
        a3_ref[c] = a3
    sums_start(1, dots)
    arrive(aside)
    for x in range(cx_n + 4):
        mark = code_ref[x] >= COARSE
        edge = floor | lid
        pd = jnp.where(edge, jnp.where(mark, 6.0, 5.0), 6.0)
        pd_ref[x] = pd
        share_ref[x] = jacobi_weight / pd
        cell_ref[x] = jnp.where(mark, code_ref[x] - COARSE, code_ref[x])
    mu = [m0] + sums_end(1, PAD)

    def times(p):
        out = [sigma * p[0]]
        for i in range(1, len(p)):
            out.append(p[i - 1] + sigma * p[i])
        return out + [p[-1]]

    def dot(p, q):
        total = 0.0
        for n in range(len(p) + len(q) - 1):
            terms = [p[i] * q[n - i] for i in range(len(p)) if 0 <= n - i < len(q)]
            total = total + sum(terms[1:], terms[0]) * mu[n]
        return total

    def against(p):
        return sum((p[i] * mu[i] for i in range(1, len(p))), p[0] * mu[0])

    alpha = m0 / (sigma * m0 + mu[1])
    s1 = [1.0 - alpha * sigma, -alpha]
    t1 = times(s1)
    omega = dot(s1, t1) / dot(t1, t1)
    rho_new = against(s1) - omega * against(t1)
    beta = (rho_new / m0) * (alpha / omega)
    r1 = [s1[0] - omega * t1[0], s1[1] - omega * t1[1], -omega * t1[2]]
    p2 = [r1[0] + beta * (1.0 - omega * sigma), r1[1] - beta * omega, r1[2]]
    v2 = times(p2)
    alpha2 = rho_new / against(v2)
    s2 = [r1[i] - alpha2 * v2[i] for i in range(3)] + [-alpha2 * v2[3]]
    t2 = times(s2)
    omega2 = dot(s2, t2) / dot(t2, t2)
    weight = [
        alpha + omega * s1[0] + alpha2 * p2[0] + omega2 * s2[0],
        omega * s1[1] + alpha2 * p2[1] + omega2 * s2[1],
        alpha2 * p2[2] + omega2 * s2[2],
        omega2 * s2[3],
    ]
    speed = []
    for c in range(3):
        w = [k[c : c + 1] for k in weight]
        field = x0_ref[c, pl.ds(1, cx_n + 2)] + w[0] * res_ref[c]
        field += w[1] * a1_ref[c] + w[2] * a2_ref[c] + w[3] * a3_ref[c]
        vel_ref[c] = field[1:-1, :cz_n]
        speed.append(field)
    ux, uz, uy = speed
    div = (ux[1:-1] - ux[:-2]) + (uz[1:-1] - z_roll(uz[1:-1], 1))
    uy = uy[1:-1]
    div = div + (uy - jnp.where(floor, 0.0, y_prev(uy)))
    share = share_ref[pl.ds(2, cx_n)]
    q = share * div
    q_ref[pl.ds(3, cx_n), pl.ds(0, cz_n)] = q[:, :cz_n]
    third = to_corners(q_ref, q_ref, 3, 2)
    third += to_z(q_ref, q_ref, 3, 1, 3)
    third += to_x(q_ref, q_ref, 3, 1, 3)

    def smooth(f):
        n = f.shape[0] - 2
        h = (n - cx_n) // 2
        g = f[1:-1]
        near = (f[2:] + f[:-2]) + (z_roll(g, 1) + z_roll(g, -1))
        near += jnp.where(lid, 0.0, y_next(g)) + jnp.where(floor, 0.0, y_prev(g))
        return pd_ref[pl.ds(2 - h, n)] * g - near

    def shares(h):
        return share_ref[pl.ds(2 - h, cx_n + 2 * h)]

    blank = jnp.zeros((2, deep, ny), jnp.float32)
    mine = jnp.where(body_rows, q, 0.0)
    first_cut = -smooth(jnp.concatenate([blank, mine, blank], 0))
    trace = jnp.concatenate(
        [first_cut[:1], first_cut[1:-1] + jnp.where(body_rows, div, 0.0), first_cut[-1:]], 0
    )
    full = jnp.concatenate([blank[:1], trace, blank[:1]], 0)
    full = full - smooth(jnp.concatenate([blank, shares(1) * trace, blank], 0))

    part = [[] for _ in range(6)]
    for m in range(COARSE):
        hit = jnp.where(cell_ref[...] == m, full, 0.0)
        flat = hit[:, :cz_n].reshape(-1, 8, ny)
        step = cz_n // 8
        top_rows = hit[:, cz_n:]
        part[0].append(jnp.sum(flat[: 2 * step], axis=0, keepdims=True))
        part[1].append(jnp.sum(flat[2 * step : -2 * step], axis=0, keepdims=True))
        part[2].append(jnp.sum(flat[-2 * step :], axis=0, keepdims=True))
        part[3].append(top_rows[1:2])
        part[4].append(jnp.sum(top_rows[2:-2], axis=0, keepdims=True))
        part[5].append(top_rows[-2:-1])
    part = [jnp.concatenate(p, 0) for p in part]
    upper_half = lax.broadcasted_iota(jnp.int32, (COARSE, 8, ny), 1) < 4

    def total_of(p):
        return jnp.sum(jnp.sum(p, axis=1), axis=1, keepdims=True)

    shape = (COARSE, lanes)
    spots = (south[1], gz, north[1])
    places = [
        lax.broadcasted_iota(jnp.int32, shape, 1)
        == lax.broadcasted_iota(jnp.int32, shape, 0) + spot * COARSE
        for spot in spots
    ]
    for k in range(3):
        cols = [
            total_of(jnp.where(upper_half, 0.0, part[3 + k])), total_of(part[k]),
            total_of(jnp.where(upper_half, part[3 + k], 0.0)),
        ]
        line = sum(
            jnp.where(place, jnp.broadcast_to(col, shape), 0.0)
            for place, col in zip(places, cols)
        )
        msg_c[k] = jnp.sum(line, axis=0, keepdims=True)
    scatter(msg_c, got_c, coarse_s, coarse_r, [at(o) for o in spread_to])

    arrive(third)
    ext = q_ref[...]
    q = 2.0 * ext[1:-1] - shares(2) * smooth(ext)
    q = q[1:-1] + ext[2:-2] - shares(1) * smooth(q)
    q = q[1:-1] + ext[3:-3] - shares(0) * smooth(q)

    pltpu.make_async_copy(got_c, got_c, coarse_r).wait()

    def restricted(t):
        rows_in = [
            got_c[spread_to.index(fold(-j, k)), t - j + 1]
            for j in (t - 1, t, t + 1) for k in range(n_gz) if fold(-j, k) != (0, 0)
        ]
        return sum(rows_in, msg_c[t + 1])

    def corrections(inv, coarse):
        out = []
        for spot in spots:
            block = inv[pl.ds(pl.multiple_of(spot * COARSE, COARSE), COARSE), :]
            col = jnp.sum(block * coarse[:, : block.shape[1]], axis=1, keepdims=True)
            out.append(jnp.broadcast_to(col, (COARSE, ny)))
        return out

    def lift(cell, pick):
        add = jnp.broadcast_to(pick(0), cell.shape)
        for m in range(1, COARSE):
            add = jnp.where(cell == m, pick(m), add)
        return add

    corr = [corrections(inv, restricted(t)) for inv, t in zip((inv_w, inv_ref, inv_e), (-1, 0, 1))]
    half = lax.broadcasted_iota(jnp.int32, (8, ny), 0) < 4
    spans = (pl.ds(0, 2), pl.ds(2, cx_n), pl.ds(cx_n + 2, 2))
    raised = []
    for k in range(3):
        cell = cell_ref[spans[k]]
        inside = lift(cell[:, :cz_n], lambda m: corr[k][1][m : m + 1])
        outside = lift(
            cell[:, cz_n:], lambda m: jnp.where(half, corr[k][2][m : m + 1], corr[k][0][m : m + 1])
        )
        raised.append(jnp.concatenate([inside, outside], 1))
    e = jnp.concatenate(raised, 0)
    e = e[1:-1] - shares(1) * smooth(e)
    e = e[1:-1] - shares(0) * smooth(e)
    out_ref[...] = (q + e)[:, :cz_n]
    for copy in pending:
        copy.wait_send()


def body(n_gx, n_gz, velocity_old, source, diag_coef, face_coef, bc_flags, coarse_map, coarse_inverse):
    cx_n, cz_n, ny = diag_coef.shape
    rows = cx_n * cz_n
    deep = cz_n + 8
    group = coarse_inverse.shape[1]
    lanes = -(-group // 128) * 128
    f32 = jnp.float32
    vmem = pltpu.VMEM
    dma = pltpu.SemaphoreType.DMA
    n_spread = min(5, n_gx) * n_gz - 1
    n_sum = n_gx * n_gz - 1 if n_gx * n_gz <= DIRECT else n_gx - 1

    def block(fields, halo):
        return vmem((fields, cx_n + 2 * halo, deep, ny), f32)

    scratch = [
        block(3, 2),
        block(3, 1),
        block(4, 3),
        vmem(bc_flags.shape, jnp.int32),
        vmem((rows, ny), jnp.int32),
        vmem(coarse_inverse.shape, f32),
        block(4, 2),
        block(3, 1),
        block(3, 2),
        block(3, 3),
        block(3, 1),
        block(3, 1),
        block(3, 1),
        vmem((cx_n + 4, deep, ny), jnp.int32),
        vmem((cx_n + 4, deep, ny), jnp.int32),
        vmem((cx_n + 4, deep, ny), f32),
        vmem((cx_n + 4, deep, ny), f32),
        vmem((cx_n + 6, deep, ny), f32),
        vmem(coarse_inverse.shape, f32),
        vmem(coarse_inverse.shape, f32),
        vmem((2, 1, 128), f32),
        vmem((2, n_sum, 1, 128), f32),
        vmem((2, 1, 128), f32),
        vmem((2, n_gz - 1, 1, 128), f32),
        vmem((3, 1, lanes), f32),
        vmem((n_spread, 3, 1, lanes), f32),
        dma((64,)),
        dma((64,)),
        dma((2, n_sum)),
        dma((2,)),
        dma((2, n_gz - 1)),
        dma((2,)),
        dma((n_spread,)),
        dma,
        dma((7,)),
        dma((2,)),
        dma((2,)),
    ]
    spec = pl.BlockSpec(memory_space=pltpu.VMEM)
    velocity, pressure = pl.pallas_call(
        functools.partial(kernel, (n_gx, n_gz, cx_n, cz_n, ny, lanes)),
        out_shape=(
            jax.ShapeDtypeStruct((3, cx_n, cz_n, ny), f32),
            jax.ShapeDtypeStruct((cx_n, cz_n, ny), f32),
        ),
        in_specs=[pl.BlockSpec(memory_space=pltpu.HBM)] * 7,
        out_specs=(spec, spec),
        scratch_shapes=scratch,
        compiler_params=pltpu.CompilerParams(
            collective_id=0, has_side_effects=True, vmem_limit_bytes=48 * 1024 * 1024
        ),
        name="corrector",
    )(
        *[
            pltpu.with_memory_space_constraint(a, pltpu.HBM)
            for a in (
                velocity_old,
                source,
                diag_coef,
                face_coef,
                bc_flags,
                coarse_map.reshape(rows, ny),
                coarse_inverse,
            )
        ]
    )
    return velocity, pressure


def solution(mesh):
    placed = (
        P(None, "gx", "gz", None),
        P(None, "gx", "gz", None),
        P("gx", "gz", None),
        P(None, "gx", "gz", None),
        P(None, "gx", "gz"),
        P("gx", "gz", None),
        P("gx", None),
    )
    return jax.shard_map(
        functools.partial(body, mesh.shape["gx"], mesh.shape["gz"]),
        mesh=mesh,
        in_specs=placed,
        out_specs=(P(None, "gx", "gz", None), P("gx", "gz", None)),
        check_vma=False,
    )
```

```python
import functools

import jax
import jax.numpy as jnp
from jax import lax
from jax.experimental import pallas as pl
from jax.experimental.pallas import tpu as pltpu
from jax.sharding import PartitionSpec as P

COARSE = 16
PAD = 8
DIRECT = 64

jacobi_weight = 2.0 / 3.0
MESH = pl.DeviceIdType.MESH


def kernel(
    dims,
    x0_in, src_in, diag_in, face_in, bc_in, map_in, inv_in,
    vel_ref, out_ref,
    x0_ref, src_ref, face_ref, bc_ref, map_ref, inv_ref,
    x0_late, src_late, face_late,
    coef, res_ref, v_ref, vk_ref, a1_ref, a2_ref, a3_ref,
    code_ref, cell_ref, pd_ref, share_ref, q_ref, inv_w, inv_e,
    msg, got, msg_z, got_z, msg_c, got_c,
    near_s, near_r, sum_s, sum_r, sum_sz, sum_rz, coarse_s, coarse_r,
    load_sem, side_s, side_r,
):
    n_gx, n_gz, cx_n, cz_n, ny, lanes = dims
    rows = cx_n * cz_n
    deep = x0_ref.shape[2]
    gx = lax.axis_index("gx")
    gz = lax.axis_index("gz")
    east = (lax.rem(gx + 1, n_gx), gz)
    west = (lax.rem(gx + n_gx - 1, n_gx), gz)
    north = (gx, lax.rem(gz + 1, n_gz))
    south = (gx, lax.rem(gz + n_gz - 1, n_gz))
    row_x = [(lax.rem(gx + d, n_gx), gz) for d in range(1, n_gx)]
    row_z = [(gx, lax.rem(gz + d, n_gz)) for d in range(1, n_gz)]
    direct = n_gx * n_gz <= DIRECT
    pending = []

    def send(src, dst, ssem, rsem, to):
        copy = pltpu.make_async_remote_copy(
            src_ref=src, dst_ref=dst, send_sem=ssem, recv_sem=rsem,
            device_id=to, device_id_type=MESH,
        )
        copy.start()
        pending.append(copy)
        return copy

    corners = [
        (east[0], north[1]), (east[0], south[1]), (west[0], north[1]), (west[0], south[1])
    ]

    def at(offset):
        return (lax.rem(gx + offset[0], n_gx), lax.rem(gz + offset[1], n_gz))

    def fold(d, k):
        return (d % n_gx, k % n_gz)

    around = {fold(d, k) for d in (-1, 0, 1) for k in (-1, 0, 1)} - {(0, 0)}
    spread_to = sorted({fold(d, k) for d in range(-2, 3) for k in range(n_gz)} - {(0, 0)})
    every = {(d, k) for d in range(n_gx) for k in range(n_gz)}
    if direct:
        sum_to = [
            (d, k)
            for k in sorted(range(n_gz), key=lambda k: -min(k, n_gz - k))
            for d in sorted(range(n_gx), key=lambda d: -min(d, n_gx - d))
            if d or k
        ]
        met = set(around)
        while True:
            seen = met | {fold(a + d, b + k) for a, b in around for d, k in met} | {(0, 0)}
            left = sorted(every - seen, key=lambda o: (min(o[1], n_gz - o[1]), o))
            if not left:
                break
            met |= {left[0], fold(-left[0][0], -left[0][1])}
        sum_to = [at(o) for o in sum_to]
    else:
        sum_to = row_x
        met = around | set(spread_to)
        met |= {(d, 0) for d in range(1, n_gx)} | {(0, k) for k in range(1, n_gz)}
    partners = [at(o) for o in sorted(around)] + [at(o) for o in sorted(met - around)]

    def inner(ref, halo):
        return ref.at[..., pl.ds(halo, cx_n), pl.ds(0, cz_n), :]

    loads = [
        pltpu.make_async_copy(a, b, load_sem.at[i])
        for i, (a, b) in enumerate(
            [
                (x0_in, inner(x0_ref, 3)), (face_in, inner(face_ref.at[pl.ds(0, 3)], 3)),
                (diag_in, inner(face_ref.at[3], 3)), (src_in, inner(src_ref, 2)),
                (bc_in, bc_ref), (map_in, map_ref), (inv_in, inv_ref),
            ]
        )
    ]
    for load in loads:
        load.start()
    barrier = pltpu.get_barrier_semaphore()
    for other in partners:
        pl.semaphore_signal(barrier, inc=1, device_id=other, device_id_type=MESH)
    for load in loads[:4]:
        load.wait()
    pl.semaphore_wait(barrier, len(partners))


    def side_x(sign, halo, a, b):
        if sign > 0:
            return pl.ds(halo + cx_n - b, b - a + 1), pl.ds(halo - b, b - a + 1)
        return pl.ds(halo + a - 1, b - a + 1), pl.ds(halo + cx_n + a - 1, b - a + 1)

    def side_z(sign, a, b, base=0):
        if sign > 0:
            return pl.ds(cz_n - b, b - a + 1), pl.ds(deep - b - base, b - a + 1)
        return pl.ds(a - 1, b - a + 1), pl.ds(cz_n + a - 1 - base, b - a + 1)

    used = []

    def ship(src, dst, to, where_from, where_to):
        i = len(used)
        used.append(i)
        return send(
            src.at[(..., *where_from, slice(None))], dst.at[(..., *where_to, slice(None))],
            near_s.at[i], near_r.at[i], to,
        )

    def to_corners(src, dst, halo, n, base=0):
        out = []
        for to, sx, sz in zip(corners, (1, 1, -1, -1), (1, -1, 1, -1)):
            (fx, tx), (fz, tz) = side_x(sx, halo, 1, n), side_z(sz, 1, n, base)
            out.append(ship(src, dst, to, (fx, fz), (tx, tz)))
        return out

    def to_z(src, dst, halo, a, b, ways=(1, -1), base=0):
        out = []
        for sz in ways:
            fz, tz = side_z(sz, a, b, base)
            x = pl.ds(halo, cx_n)
            out.append(ship(src, dst, north if sz > 0 else south, (x, fz), (x, tz)))
        return out

    def to_x(src, dst, halo, a, b, ways=(1, -1)):
        out = []
        for sx in ways:
            fx, tx = side_x(sx, halo, a, b)
            z = pl.ds(0, cz_n)
            out.append(ship(src, dst, east if sx > 0 else west, (fx, z), (tx, z)))
        return out

    both = pl.ds(0, 2)
    first = to_corners(x0_ref, x0_ref, 3, 1)
    first += to_corners(face_ref.at[both], face_ref.at[both], 3, 1)
    first += to_z(x0_ref, x0_ref, 3, 1, 2)
    first += to_z(face_ref, face_ref, 3, 1, 1)
    first += to_z(face_ref.at[1], face_ref.at[1], 3, 2, 2, (1,))
    first += to_z(src_ref, src_ref, 2, 1, 1)
    first += to_x(x0_ref, x0_ref, 3, 1, 2)
    first += to_x(face_ref, face_ref, 3, 1, 1)
    first += to_x(face_ref.at[0], face_ref.at[0], 3, 2, 2, (1,))
    first += to_x(src_ref, src_ref, 2, 1, 1)

    rest = pl.ds(1, 3)
    late = to_corners(x0_ref, x0_late, 3, 2, cz_n)
    late += to_corners(face_ref, face_late, 3, 2, cz_n)
    late += to_corners(src_ref, src_late, 2, 1, cz_n)
    late += to_z(x0_ref, x0_late, 3, 3, 3, base=cz_n)
    late += to_z(src_ref, src_late, 2, 2, 2, base=cz_n)
    late += to_z(face_ref, face_late, 3, 2, 2, base=cz_n)
    late += to_z(face_ref.at[1], face_late.at[1], 3, 3, 3, (1,), base=cz_n)
    late += to_x(x0_ref, x0_ref, 3, 3, 3)
    late += to_x(src_ref, src_ref, 2, 2, 2)
    late += to_x(face_ref.at[rest], face_ref.at[rest], 3, 2, 2, (1,))
    late += to_x(face_ref.at[0], face_ref.at[0], 3, 3, 3, (1,))
    late += to_x(face_ref, face_ref, 3, 2, 2, (-1,))

    def arrive(copies):
        for copy in copies:
            copy.wait_recv()

    level = lax.broadcasted_iota(jnp.int32, (rows, ny), 1)
    bottom = level == 0
    top = level == ny - 1
    def y_prev(f):
        return pltpu.roll(f, 1, f.ndim - 1)

    def y_next(f):
        return pltpu.roll(f, ny - 1, f.ndim - 1)

    eye = lax.broadcasted_iota(jnp.int32, (cz_n, cz_n), 0) == lax.broadcasted_iota(
        jnp.int32, (cz_n, cz_n), 1
    )

    def column(side):
        flags = bc_ref[side]
        parts = [
            jnp.sum(
                jnp.where(eye, jnp.broadcast_to(flags[i : i + 1], (cz_n, cz_n)), 0),
                axis=1, keepdims=True,
            )
            for i in range(cx_n)
        ]
        return jnp.broadcast_to(jnp.concatenate(parts, 0), (rows, ny))

    def scatter(msg, got, ssem, rsem, others):
        return [
            send(msg, got.at[d], ssem.at[d], rsem, to) for d, to in enumerate(others)
        ]

    def gathered(msg, got, rsem):
        pltpu.make_async_copy(got, got, rsem).wait()
        return msg[...] + jnp.sum(got[...], axis=0)


    def z_roll(f, shift):
        flat = f.reshape((-1,) + f.shape[-2:])
        return pltpu.roll(flat, shift % deep, 1).reshape(f.shape)

    def apply(f, c):
        h = (f.shape[0] - cx_n) // 2 - 1
        n = cx_n + 2 * h
        g = f[1:-1]
        total = coef[0, pl.ds(2 - h, n)] * g
        total -= face_ref[0, pl.ds(3 - h, n)] * f[2:] + face_ref[0, pl.ds(2 - h, n)] * f[:-2]
        total -= face_ref[1, pl.ds(3 - h, n)] * z_roll(g, -1) + coef[1, pl.ds(2 - h, n)] * z_roll(g, 1)
        total -= coef[2, pl.ds(2 - h, n)] * y_next(g) + coef[3, pl.ds(2 - h, n)] * y_prev(g)
        return total

    def own(f):
        h = (f.shape[0] - cx_n) // 2
        return f[h : h + cx_n, :cz_n].reshape(rows, ny)

    def pack(pairs):
        sums = [jnp.sum(a * b, axis=0, keepdims=True) for a, b in pairs]
        while len(sums) < 3 * PAD:
            sums.append(jnp.zeros_like(sums[0]))
        total = jnp.sum(jnp.concatenate(sums, 0), axis=1, keepdims=True)
        shape = (3 * PAD, 128)
        pick = lax.broadcasted_iota(jnp.int32, shape, 0) == lax.broadcasted_iota(
            jnp.int32, shape, 1
        )
        return jnp.sum(
            jnp.where(pick, jnp.broadcast_to(total, shape), 0.0), axis=0, keepdims=True
        )

    def sums_start(i, pairs):
        msg[i] = pack(pairs)
        scatter(msg.at[i], got.at[i], sum_s.at[i], sum_r.at[i], sum_to)

    def sums_end(i, count):
        total = gathered(msg.at[i], got.at[i], sum_r.at[i])
        if not direct:
            msg_z[i] = total
            scatter(msg_z.at[i], got_z.at[i], sum_sz.at[i], sum_rz.at[i], row_z)
            total = gathered(msg_z.at[i], got_z.at[i], sum_rz.at[i])
        shape = (8, 128)
        place = lax.broadcasted_iota(jnp.int32, shape, 0) * PAD
        lane = lax.broadcasted_iota(jnp.int32, shape, 1)
        wide = jnp.broadcast_to(total, shape)
        return [
            jnp.broadcast_to(
                jnp.sum(jnp.where(lane == place + k, wide, 0.0), axis=1, keepdims=True), shape
            )
            for k in range(count)
        ]

    slot = lax.broadcasted_iota(jnp.int32, (deep, ny), 0)
    floor = lax.broadcasted_iota(jnp.int32, (deep, ny), 1) == 0
    lid = lax.broadcasted_iota(jnp.int32, (deep, ny), 1) == ny - 1
    for load in loads[4:]:
        load.wait()
    flag = jnp.where(bottom, column(0), 0) + jnp.where(top, column(1), 0)
    code = map_ref[...] + COARSE * flag
    code_ref[pl.ds(2, cx_n), pl.ds(0, cz_n)] = code.reshape(cx_n, cz_n, ny)

    aside = to_corners(code_ref, code_ref, 2, 1)
    aside += to_z(code_ref, code_ref, 2, 1, 2)
    aside += to_x(code_ref, code_ref, 2, 1, 2)
    aside.append(send(inv_ref, inv_w, side_s.at[0], side_r.at[0], east))
    aside.append(send(inv_ref, inv_e, side_s.at[1], side_r.at[1], west))

    arrive(first)

    def prepare(low, high):
        for x in range(low, high):
            cx, cx_low = face_ref[0, x + 1], face_ref[0, x]
            cz, cy = face_ref[1, x + 1], face_ref[2, x + 1]
            cz_low = pltpu.roll(cz, 1, 0)
            upper = jnp.where(lid, 0.0, cy)
            lower = jnp.where(floor, 0.0, y_prev(cy))
            wall = jnp.where(floor | lid, jnp.broadcast_to(cy[:, ny - 1 :], (deep, ny)), 0.0)
            total = (face_ref[3, x + 1] + (cx + cz)) + ((upper + lower) + wall)
            coef[0, x] = total + (cx_low + cz_low)
            coef[1, x] = cz_low
            coef[2, x] = upper
            coef[3, x] = lower

    prepare(1, cx_n + 3)
    dots = []
    for c in range(3):
        r = src_ref[c, pl.ds(1, cx_n + 2)] - apply(x0_ref[c, pl.ds(1, cx_n + 4)], c)
        r_own = own(r)
        v = apply(r, c)
        v_own = own(v)
        vk_ref[c, pl.ds(3, cx_n), pl.ds(0, cz_n)] = v[:, :cz_n]
        dots.append([(r_own, r_own), (r_own, v_own)])
    second = to_corners(vk_ref, vk_ref, 3, 2)
    zero = jnp.zeros((8, ny), jnp.float32)
    sums_start(0, [p for d in dots for p in d + [(zero, zero)] * (PAD - 2)])
    second += to_z(vk_ref, vk_ref, 3, 2, 3)
    second += to_x(vk_ref, vk_ref, 3, 2, 3)

    arrive(late)
    beyond = pl.ds(cz_n, 8)
    nearest = (slot[cz_n:] == cz_n) | (slot[cz_n:] == deep - 1)
    farthest = (slot[cz_n:] == cz_n + 2) | (slot[cz_n:] == deep - 3)
    middle = pl.ds(3, cx_n)
    for f in range(4):
        face_ref[f, middle, beyond] = jnp.where(
            nearest, face_ref[f, middle, beyond], face_late[f, middle]
        )
        for x in (1, cx_n + 3):
            face_ref[f, pl.ds(x, 2), beyond] = face_late[f, pl.ds(x, 2)]
    prepare(0, cx_n + 4)
    inside = pl.ds(2, cx_n)
    for c in range(3):
        x0_ref[c, middle, beyond] = jnp.where(
            farthest, x0_late[c, middle], x0_ref[c, middle, beyond]
        )
        for x in (1, cx_n + 3):
            x0_ref[c, pl.ds(x, 2), beyond] = x0_late[c, pl.ds(x, 2)]
        src_ref[c, inside, beyond] = jnp.where(
            nearest, src_ref[c, inside, beyond], src_late[c, inside]
        )
        for x in (1, cx_n + 2):
            src_ref[c, x, beyond] = src_late[c, x]
        r = src_ref[c] - apply(x0_ref[c], c)
        res_ref[c] = r
        v_ref[c] = apply(r, c)

    arrive(second)
    m0, m1 = sums_end(0, 2)
    sigma = m1 / m0
    mine = (slot <= cz_n) | (slot == deep - 1)
    body_rows = slot < cz_n
    dots = []
    for c in range(3):
        s = sigma[c : c + 1]
        mid = jnp.where(mine, v_ref[c, pl.ds(1, cx_n)], vk_ref[c, pl.ds(3, cx_n)])
        low = jnp.where(body_rows, v_ref[c, 0], vk_ref[c, 2])
        high = jnp.where(body_rows, v_ref[c, cx_n + 1], vk_ref[c, cx_n + 3])
        v = jnp.concatenate(
            [vk_ref[c, pl.ds(0, 2)], low[None], mid, high[None], vk_ref[c, pl.ds(cx_n + 4, 2)]], 0
        )
        r = res_ref[c]
        u = apply(v, c)
        v = v[1:-1]
        a1 = v - s * r
        a2 = (u - s * v) - s * a1
        a3 = apply(a2, c) - s * a2[1:-1]
        a4 = apply(a3, c) - s * a3[1:-1]
        r0, b1, b2, b3, b4 = own(r), own(a1), own(a2), own(a3), own(a4)
        dots += [
            (r0, b1), (b1, b1), (b1, b2), (b2, b2), (b2, b3), (b3, b3), (b3, b4), (b4, b4)
        ]
        a1_ref[c] = a1[1:-1]
        a2_ref[c] = a2[1:-1]
        a3_ref[c] = a3
    sums_start(1, dots)
    arrive(aside)
    for x in range(cx_n + 4):
        mark = code_ref[x] >= COARSE
        edge = floor | lid
        pd = jnp.where(edge, jnp.where(mark, 6.0, 5.0), 6.0)
        pd_ref[x] = pd
        share_ref[x] = jacobi_weight / pd
        cell_ref[x] = jnp.where(mark, code_ref[x] - COARSE, code_ref[x])
    mu = [m0] + sums_end(1, PAD)

    def times(p):
        out = [sigma * p[0]]
        for i in range(1, len(p)):
            out.append(p[i - 1] + sigma * p[i])
        return out + [p[-1]]

    def dot(p, q):
        total = 0.0
        for n in range(len(p) + len(q) - 1):
            terms = [p[i] * q[n - i] for i in range(len(p)) if 0 <= n - i < len(q)]
            total = total + sum(terms[1:], terms[0]) * mu[n]
        return total

    def against(p):
        return sum((p[i] * mu[i] for i in range(1, len(p))), p[0] * mu[0])

    alpha = m0 / (sigma * m0 + mu[1])
    s1 = [1.0 - alpha * sigma, -alpha]
    t1 = times(s1)
    omega = dot(s1, t1) / dot(t1, t1)
    rho_new = against(s1) - omega * against(t1)
    beta = (rho_new / m0) * (alpha / omega)
    r1 = [s1[0] - omega * t1[0], s1[1] - omega * t1[1], -omega * t1[2]]
    p2 = [r1[0] + beta * (1.0 - omega * sigma), r1[1] - beta * omega, r1[2]]
    v2 = times(p2)
    alpha2 = rho_new / against(v2)
    s2 = [r1[i] - alpha2 * v2[i] for i in range(3)] + [-alpha2 * v2[3]]
    t2 = times(s2)
    omega2 = dot(s2, t2) / dot(t2, t2)
    weight = [
        alpha + omega * s1[0] + alpha2 * p2[0] + omega2 * s2[0],
        omega * s1[1] + alpha2 * p2[1] + omega2 * s2[1],
        alpha2 * p2[2] + omega2 * s2[2],
        omega2 * s2[3],
    ]
    speed = []
    for c in range(3):
        w = [k[c : c + 1] for k in weight]
        field = x0_ref[c, pl.ds(2, cx_n + 2)] + w[0] * res_ref[c, pl.ds(1, cx_n + 2)]
        field += w[1] * a1_ref[c] + w[2] * a2_ref[c] + w[3] * a3_ref[c]
        vel_ref[c] = field[1:-1, :cz_n]
        speed.append(field)
    ux, uz, uy = speed
    div = (ux[1:-1] - ux[:-2]) + (uz[1:-1] - z_roll(uz[1:-1], 1))
    uy = uy[1:-1]
    div = div + (uy - jnp.where(floor, 0.0, y_prev(uy)))
    share = share_ref[pl.ds(2, cx_n)]
    q = share * div
    q_ref[pl.ds(3, cx_n), pl.ds(0, cz_n)] = q[:, :cz_n]
    third = to_corners(q_ref, q_ref, 3, 2)
    third += to_z(q_ref, q_ref, 3, 1, 3)
    third += to_x(q_ref, q_ref, 3, 1, 3)

    def smooth(f):
        n = f.shape[0] - 2
        h = (n - cx_n) // 2
        g = f[1:-1]
        near = (f[2:] + f[:-2]) + (z_roll(g, 1) + z_roll(g, -1))
        near += jnp.where(lid, 0.0, y_next(g)) + jnp.where(floor, 0.0, y_prev(g))
        return pd_ref[pl.ds(2 - h, n)] * g - near

    def shares(h):
        return share_ref[pl.ds(2 - h, cx_n + 2 * h)]

    blank = jnp.zeros((2, deep, ny), jnp.float32)
    mine = jnp.where(body_rows, q, 0.0)
    first_cut = -smooth(jnp.concatenate([blank, mine, blank], 0))
    trace = jnp.concatenate(
        [first_cut[:1], first_cut[1:-1] + jnp.where(body_rows, div, 0.0), first_cut[-1:]], 0
    )
    full = jnp.concatenate([blank[:1], trace, blank[:1]], 0)
    full = full - smooth(jnp.concatenate([blank, shares(1) * trace, blank], 0))

    part = [[] for _ in range(6)]
    for m in range(COARSE):
        hit = jnp.where(cell_ref[...] == m, full, 0.0)
        flat = hit[:, :cz_n].reshape(-1, 8, ny)
        step = cz_n // 8
        top_rows = hit[:, cz_n:]
        part[0].append(jnp.sum(flat[: 2 * step], axis=0, keepdims=True))
        part[1].append(jnp.sum(flat[2 * step : -2 * step], axis=0, keepdims=True))
        part[2].append(jnp.sum(flat[-2 * step :], axis=0, keepdims=True))
        part[3].append(top_rows[1:2])
        part[4].append(jnp.sum(top_rows[2:-2], axis=0, keepdims=True))
        part[5].append(top_rows[-2:-1])
    part = [jnp.concatenate(p, 0) for p in part]
    upper_half = lax.broadcasted_iota(jnp.int32, (COARSE, 8, ny), 1) < 4

    def total_of(p):
        return jnp.sum(jnp.sum(p, axis=1), axis=1, keepdims=True)

    shape = (COARSE, lanes)
    spots = (south[1], gz, north[1])
    places = [
        lax.broadcasted_iota(jnp.int32, shape, 1)
        == lax.broadcasted_iota(jnp.int32, shape, 0) + spot * COARSE
        for spot in spots
    ]
    for k in range(3):
        cols = [
            total_of(jnp.where(upper_half, 0.0, part[3 + k])), total_of(part[k]),
            total_of(jnp.where(upper_half, part[3 + k], 0.0)),
        ]
        line = sum(
            jnp.where(place, jnp.broadcast_to(col, shape), 0.0)
            for place, col in zip(places, cols)
        )
        msg_c[k] = jnp.sum(line, axis=0, keepdims=True)
    scatter(msg_c, got_c, coarse_s, coarse_r, [at(o) for o in spread_to])

    arrive(third)
    ext = q_ref[...]
    q = 2.0 * ext[1:-1] - shares(2) * smooth(ext)
    q = q[1:-1] + ext[2:-2] - shares(1) * smooth(q)
    q = q[1:-1] + ext[3:-3] - shares(0) * smooth(q)

    pltpu.make_async_copy(got_c, got_c, coarse_r).wait()

    def restricted(t):
        rows_in = [
            got_c[spread_to.index(fold(-j, k)), t - j + 1]
            for j in (t - 1, t, t + 1) for k in range(n_gz) if fold(-j, k) != (0, 0)
        ]
        return sum(rows_in, msg_c[t + 1])

    def corrections(inv, coarse):
        out = []
        for spot in spots:
            block = inv[pl.ds(pl.multiple_of(spot * COARSE, COARSE), COARSE), :]
            col = jnp.sum(block * coarse[:, : block.shape[1]], axis=1, keepdims=True)
            out.append(jnp.broadcast_to(col, (COARSE, ny)))
        return out

    def lift(cell, pick):
        add = jnp.broadcast_to(pick(0), cell.shape)
        for m in range(1, COARSE):
            add = jnp.where(cell == m, pick(m), add)
        return add

    corr = [corrections(inv, restricted(t)) for inv, t in zip((inv_w, inv_ref, inv_e), (-1, 0, 1))]
    half = lax.broadcasted_iota(jnp.int32, (8, ny), 0) < 4
    spans = (pl.ds(0, 2), pl.ds(2, cx_n), pl.ds(cx_n + 2, 2))
    raised = []
    for k in range(3):
        cell = cell_ref[spans[k]]
        inside = lift(cell[:, :cz_n], lambda m: corr[k][1][m : m + 1])
        outside = lift(
            cell[:, cz_n:], lambda m: jnp.where(half, corr[k][2][m : m + 1], corr[k][0][m : m + 1])
        )
        raised.append(jnp.concatenate([inside, outside], 1))
    e = jnp.concatenate(raised, 0)
    e = e[1:-1] - shares(1) * smooth(e)
    e = e[1:-1] - shares(0) * smooth(e)
    out_ref[...] = (q + e)[:, :cz_n]
    for copy in pending:
        copy.wait_send()


def put(a_ref, b_ref, a_out, b_out, sem):
    copies = [
        pltpu.make_async_copy(a_ref, a_out, sem.at[0]), pltpu.make_async_copy(b_ref, b_out, sem.at[1])
    ]
    for copy in copies:
        copy.start()
    for copy in copies:
        copy.wait()


def body(n_gx, n_gz, velocity_old, source, diag_coef, face_coef, bc_flags, coarse_map, coarse_inverse):
    cx_n, cz_n, ny = diag_coef.shape
    rows = cx_n * cz_n
    deep = cz_n + 8
    group = coarse_inverse.shape[1]
    lanes = -(-group // 128) * 128
    f32 = jnp.float32
    vmem = pltpu.VMEM
    dma = pltpu.SemaphoreType.DMA
    n_spread = min(5, n_gx) * n_gz - 1
    n_sum = n_gx * n_gz - 1 if n_gx * n_gz <= DIRECT else n_gx - 1

    def block(fields, halo):
        return vmem((fields, cx_n + 2 * halo, deep, ny), f32)

    scratch = [
        block(3, 3),
        block(3, 2),
        block(4, 3),
        vmem(bc_flags.shape, jnp.int32),
        vmem((rows, ny), jnp.int32),
        vmem(coarse_inverse.shape, f32),
        vmem((3, cx_n + 6, 8, ny), f32),
        vmem((3, cx_n + 4, 8, ny), f32),
        vmem((4, cx_n + 6, 8, ny), f32),
        block(4, 2),
        block(3, 2),
        block(3, 1),
        block(3, 3),
        block(3, 1),
        block(3, 1),
        block(3, 1),
        vmem((cx_n + 4, deep, ny), jnp.int32),
        vmem((cx_n + 4, deep, ny), jnp.int32),
        vmem((cx_n + 4, deep, ny), f32),
        vmem((cx_n + 4, deep, ny), f32),
        vmem((cx_n + 6, deep, ny), f32),
        vmem(coarse_inverse.shape, f32),
        vmem(coarse_inverse.shape, f32),
        vmem((2, 1, 128), f32),
        vmem((2, n_sum, 1, 128), f32),
        vmem((2, 1, 128), f32),
        vmem((2, n_gz - 1, 1, 128), f32),
        vmem((3, 1, lanes), f32),
        vmem((n_spread, 3, 1, lanes), f32),
        dma((96,)),
        dma((96,)),
        dma((2, n_sum)),
        dma((2,)),
        dma((2, n_gz - 1)),
        dma((2,)),
        dma((n_spread,)),
        dma,
        dma((7,)),
        dma((2,)),
        dma((2,)),
    ]
    spec = pl.BlockSpec(memory_space=pltpu.VMEM)
    velocity, pressure = pl.pallas_call(
        functools.partial(kernel, (n_gx, n_gz, cx_n, cz_n, ny, lanes)),
        out_shape=(
            jax.ShapeDtypeStruct((3, cx_n, cz_n, ny), f32),
            jax.ShapeDtypeStruct((cx_n, cz_n, ny), f32),
        ),
        in_specs=[pl.BlockSpec(memory_space=pltpu.HBM)] * 7,
        out_specs=(spec, spec),
        scratch_shapes=scratch,
        compiler_params=pltpu.CompilerParams(
            collective_id=0, has_side_effects=True, vmem_limit_bytes=48 * 1024 * 1024
        ),
        name="corrector",
    )(
        *[
            pltpu.with_memory_space_constraint(a, pltpu.HBM)
            for a in (
                velocity_old,
                source,
                diag_coef,
                face_coef,
                bc_flags,
                coarse_map.reshape(rows, ny),
                coarse_inverse,
            )
        ]
    )
    velocity, pressure = pl.pallas_call(
        put,
        out_shape=(
            jax.ShapeDtypeStruct(velocity.shape, f32),
            jax.ShapeDtypeStruct(pressure.shape, f32),
        ),
        in_specs=[spec, spec],
        out_specs=[pl.BlockSpec(memory_space=pltpu.HBM)] * 2,
        scratch_shapes=[dma((2,))],
        name="put",
    )(*[pltpu.with_memory_space_constraint(a, pltpu.VMEM) for a in (velocity, pressure)])
    return velocity, pressure


def solution(mesh):
    placed = (
        P(None, "gx", "gz", None),
        P(None, "gx", "gz", None),
        P("gx", "gz", None),
        P(None, "gx", "gz", None),
        P(None, "gx", "gz"),
        P("gx", "gz", None),
        P("gx", None),
    )
    return jax.shard_map(
        functools.partial(body, mesh.shape["gx"], mesh.shape["gz"]),
        mesh=mesh,
        in_specs=placed,
        out_specs=(P(None, "gx", "gz", None), P("gx", "gz", None)),
        check_vma=False,
    )
```

```python
import functools
import math

import jax
import jax.numpy as jnp
from jax import lax
from jax.experimental import pallas as pl
from jax.experimental.pallas import tpu as pltpu
from jax.sharding import PartitionSpec as P

COARSE = 16
PAD = 8
DIRECT = 64

jacobi_weight = 2.0 / 3.0
MESH = pl.DeviceIdType.MESH


def kernel(
    dims,
    x0_in, src_in, diag_in, face_in, bc_in, map_in, inv_in,
    vel_ref, out_ref,
    x0_ref, src_ref, face_ref, bc_ref, map_ref, inv_ref,
    x0_late, src_late, face_late,
    coef, res_ref, v_ref, vk_ref, a1_ref, a2_ref, a3_ref,
    code_ref, cell_ref, pd_ref, share_ref, q_ref, inv_w, inv_e,
    msg, got, msg_z, got_z, msg_c, got_c,
    tally, near_s, near_r, sum_sem, coarse_sem, load_sem, side_s, side_r,
):
    n_gx, n_gz, cx_n, cz_n, ny, lanes = dims
    rows = cx_n * cz_n
    deep = x0_ref.shape[2]
    gx = lax.axis_index("gx")
    gz = lax.axis_index("gz")
    east = (lax.rem(gx + 1, n_gx), gz)
    west = (lax.rem(gx + n_gx - 1, n_gx), gz)
    north = (gx, lax.rem(gz + 1, n_gz))
    south = (gx, lax.rem(gz + n_gz - 1, n_gz))
    row_x = [(lax.rem(gx + d, n_gx), gz) for d in range(1, n_gx)]
    row_z = [(gx, lax.rem(gz + d, n_gz)) for d in range(1, n_gz)]
    direct = n_gx * n_gz <= DIRECT

    def send(src, dst, ssem, rsem, to):
        copy = pltpu.make_async_remote_copy(
            src_ref=src, dst_ref=dst, send_sem=ssem, recv_sem=rsem,
            device_id=to, device_id_type=MESH,
        )
        copy.start()
        return copy

    def settle(sem, count):
        span = tally.at[pl.ds(0, count)]
        pltpu.make_async_copy(span, span, sem).wait()

    corners = [
        (east[0], north[1]), (east[0], south[1]), (west[0], north[1]), (west[0], south[1])
    ]

    def at(offset):
        return (lax.rem(gx + offset[0], n_gx), lax.rem(gz + offset[1], n_gz))

    def fold(d, k):
        return (d % n_gx, k % n_gz)

    around = {fold(d, k) for d in (-1, 0, 1) for k in (-1, 0, 1)} - {(0, 0)}
    spread_to = sorted({fold(d, k) for d in range(-2, 3) for k in range(n_gz)} - {(0, 0)})
    every = {(d, k) for d in range(n_gx) for k in range(n_gz)}
    if direct:
        sum_to = [
            (d, k)
            for k in sorted(range(n_gz), key=lambda k: -min(k, n_gz - k))
            for d in sorted(range(n_gx), key=lambda d: -min(d, n_gx - d))
            if d or k
        ]
        met = set(around)
        while True:
            seen = met | {fold(a + d, b + k) for a, b in around for d, k in met} | {(0, 0)}
            left = sorted(every - seen, key=lambda o: (min(o[1], n_gz - o[1]), o))
            if not left:
                break
            met |= {left[0], fold(-left[0][0], -left[0][1])}
        sum_to = [at(o) for o in sum_to]
    else:
        sum_to = row_x
        met = around | set(spread_to)
        met |= {(d, 0) for d in range(1, n_gx)} | {(0, k) for k in range(1, n_gz)}
    near_first = sorted(around, key=lambda o: (o[0] == 0) + (o[1] == 0) * 2)
    partners = [at(o) for o in near_first] + [at(o) for o in sorted(met - around)]

    def inner(ref, halo):
        return ref.at[..., pl.ds(halo, cx_n), pl.ds(0, cz_n), :]

    loads = [
        pltpu.make_async_copy(a, b, load_sem.at[max(0, i - 3)])
        for i, (a, b) in enumerate(
            [
                (x0_in, inner(x0_ref, 3)), (face_in, inner(face_ref.at[pl.ds(0, 3)], 3)),
                (diag_in, inner(face_ref.at[3], 3)), (src_in, inner(src_ref, 2)),
                (bc_in, bc_ref), (map_in, map_ref), (inv_in, inv_ref),
            ]
        )
    ]
    barrier = pltpu.get_barrier_semaphore()
    for other in partners:
        pl.semaphore_signal(barrier, inc=1, device_id=other, device_id_type=MESH)
    for load in loads:
        load.start()
    settle(load_sem.at[0], 10 * rows)
    pl.semaphore_wait(barrier, len(partners))


    def side_x(sign, halo, a, b):
        if sign > 0:
            return pl.ds(halo + cx_n - b, b - a + 1), pl.ds(halo - b, b - a + 1)
        return pl.ds(halo + a - 1, b - a + 1), pl.ds(halo + cx_n + a - 1, b - a + 1)

    def side_z(sign, a, b, base=0):
        if sign > 0:
            return pl.ds(cz_n - b, b - a + 1), pl.ds(deep - b - base, b - a + 1)
        return pl.ds(a - 1, b - a + 1), pl.ds(cz_n + a - 1 - base, b - a + 1)

    lots = []

    def ship(src, dst, to, where_from, where_to):
        target = dst.at[(..., *where_to, slice(None))]
        lots[-1] += math.prod(target.shape[:-1])
        i = len(lots) - 1
        send(src.at[(..., *where_from, slice(None))], target, near_s.at[i], near_r.at[i], to)

    def arrive(i):
        settle(near_r.at[i], lots[i])

    def to_corners(src, dst, halo, n, base=0):
        for to, sx, sz in zip(corners, (1, 1, -1, -1), (1, -1, 1, -1)):
            (fx, tx), (fz, tz) = side_x(sx, halo, 1, n), side_z(sz, 1, n, base)
            ship(src, dst, to, (fx, fz), (tx, tz))

    def to_z(src, dst, halo, a, b, ways=(1, -1), base=0):
        for sz in ways:
            fz, tz = side_z(sz, a, b, base)
            x = pl.ds(halo, cx_n)
            ship(src, dst, north if sz > 0 else south, (x, fz), (x, tz))

    def to_x(src, dst, halo, a, b, ways=(1, -1)):
        for sx in ways:
            fx, tx = side_x(sx, halo, a, b)
            z = pl.ds(0, cz_n)
            ship(src, dst, east if sx > 0 else west, (fx, z), (tx, z))

    both = pl.ds(0, 2)
    lots.append(0)
    to_corners(x0_ref, x0_ref, 3, 1)
    to_corners(face_ref.at[both], face_ref.at[both], 3, 1)
    to_z(x0_ref, x0_ref, 3, 1, 2)
    to_z(face_ref, face_ref, 3, 1, 1)
    to_z(face_ref.at[1], face_ref.at[1], 3, 2, 2, (1,))
    to_z(src_ref, src_ref, 2, 1, 1)
    to_x(x0_ref, x0_ref, 3, 1, 2)
    to_x(face_ref, face_ref, 3, 1, 1)
    to_x(face_ref.at[0], face_ref.at[0], 3, 2, 2, (1,))
    to_x(src_ref, src_ref, 2, 1, 1)

    rest = pl.ds(1, 3)
    lots.append(0)
    to_corners(x0_ref, x0_late, 3, 2, cz_n)
    to_corners(face_ref, face_late, 3, 2, cz_n)
    to_corners(src_ref, src_late, 2, 1, cz_n)
    to_z(x0_ref, x0_late, 3, 3, 3, base=cz_n)
    to_z(src_ref, src_late, 2, 2, 2, base=cz_n)
    to_z(face_ref, face_late, 3, 2, 2, base=cz_n)
    to_z(face_ref.at[1], face_late.at[1], 3, 3, 3, (1,), base=cz_n)
    to_x(x0_ref, x0_ref, 3, 3, 3)
    to_x(src_ref, src_ref, 2, 2, 2)
    to_x(face_ref.at[rest], face_ref.at[rest], 3, 2, 2, (1,))
    to_x(face_ref.at[0], face_ref.at[0], 3, 3, 3, (1,))
    to_x(face_ref, face_ref, 3, 2, 2, (-1,))

    level = lax.broadcasted_iota(jnp.int32, (rows, ny), 1)
    bottom = level == 0
    top = level == ny - 1
    def y_prev(f):
        return pltpu.roll(f, 1, f.ndim - 1)

    def y_next(f):
        return pltpu.roll(f, ny - 1, f.ndim - 1)

    eye = lax.broadcasted_iota(jnp.int32, (cz_n, cz_n), 0) == lax.broadcasted_iota(
        jnp.int32, (cz_n, cz_n), 1
    )

    def column(side):
        flags = bc_ref[side]
        parts = [
            jnp.sum(
                jnp.where(eye, jnp.broadcast_to(flags[i : i + 1], (cz_n, cz_n)), 0),
                axis=1, keepdims=True,
            )
            for i in range(cx_n)
        ]
        return jnp.broadcast_to(jnp.concatenate(parts, 0), (rows, ny))

    def scatter(msg, got, sem, others):
        for d, to in enumerate(others):
            send(msg, got.at[d], sem.at[0], sem.at[1], to)

    def gathered(msg, got, sem):
        for k in range(2):
            pltpu.make_async_copy(got, got, sem.at[k]).wait()
        return msg[...] + jnp.sum(got[...], axis=0)

    def z_roll(f, shift):
        flat = f.reshape((-1,) + f.shape[-2:])
        return pltpu.roll(flat, shift % deep, 1).reshape(f.shape)

    def apply(f):
        h = (f.shape[0] - cx_n) // 2 - 1
        n = cx_n + 2 * h
        g = f[1:-1]
        flux_x = face_ref[0, pl.ds(2 - h, n + 1)] * (f[:-1] - f[1:])
        flux_z = face_ref[1, pl.ds(3 - h, n)] * (g - z_roll(g, -1))
        flux_y = coef[1, pl.ds(2 - h, n)] * (g - y_next(g))
        total = coef[0, pl.ds(2 - h, n)] * g + (flux_x[1:] - flux_x[:-1])
        return total + (flux_z - z_roll(flux_z, 1)) + (flux_y - y_prev(flux_y))

    def own(f):
        h = (f.shape[0] - cx_n) // 2
        return f[h : h + cx_n, :cz_n].reshape(rows, ny)

    def pack(pairs):
        sums = [jnp.sum(a * b, axis=0, keepdims=True) for a, b in pairs]
        while len(sums) < 3 * PAD:
            sums.append(jnp.zeros_like(sums[0]))
        total = jnp.sum(jnp.concatenate(sums, 0), axis=1, keepdims=True)
        shape = (3 * PAD, 128)
        pick = lax.broadcasted_iota(jnp.int32, shape, 0) == lax.broadcasted_iota(
            jnp.int32, shape, 1
        )
        return jnp.sum(
            jnp.where(pick, jnp.broadcast_to(total, shape), 0.0), axis=0, keepdims=True
        )

    def sums_start(i, pairs):
        msg[i] = pack(pairs)
        scatter(msg.at[i], got.at[i], sum_sem.at[i, 0], sum_to)

    def sums_end(i, count):
        total = gathered(msg.at[i], got.at[i], sum_sem.at[i, 0])
        if not direct:
            msg_z[i] = total
            scatter(msg_z.at[i], got_z.at[i], sum_sem.at[i, 1], row_z)
            total = gathered(msg_z.at[i], got_z.at[i], sum_sem.at[i, 1])
        shape = (8, 128)
        place = lax.broadcasted_iota(jnp.int32, shape, 0) * PAD
        lane = lax.broadcasted_iota(jnp.int32, shape, 1)
        wide = jnp.broadcast_to(total, shape)
        return [
            jnp.broadcast_to(
                jnp.sum(jnp.where(lane == place + k, wide, 0.0), axis=1, keepdims=True), shape
            )
            for k in range(count)
        ]

    slot = lax.broadcasted_iota(jnp.int32, (deep, ny), 0)
    floor = lax.broadcasted_iota(jnp.int32, (deep, ny), 1) == 0
    lid = lax.broadcasted_iota(jnp.int32, (deep, ny), 1) == ny - 1
    for load in loads[4:]:
        load.wait()
    flag = jnp.where(bottom, column(0), 0) + jnp.where(top, column(1), 0)
    code = map_ref[...] + COARSE * flag
    code_ref[pl.ds(2, cx_n), pl.ds(0, cz_n)] = code.reshape(cx_n, cz_n, ny)

    lots.append(0)
    to_corners(code_ref, code_ref, 2, 1)
    to_z(code_ref, code_ref, 2, 1, 2)
    to_x(code_ref, code_ref, 2, 1, 2)
    blocks = [
        send(inv_ref, inv_w, side_s.at[0], side_r.at[0], east),
        send(inv_ref, inv_e, side_s.at[1], side_r.at[1], west),
    ]

    arrive(0)

    def prepare(low, high):
        for x in range(low, high):
            cy = face_ref[2, x + 1]
            wall = jnp.where(floor | lid, jnp.broadcast_to(cy[:, ny - 1 :], (deep, ny)), 0.0)
            coef[0, x] = face_ref[3, x + 1] + wall
            coef[1, x] = jnp.where(lid, 0.0, cy)

    prepare(1, cx_n + 3)
    dots = []
    for c in range(3):
        r = src_ref[c, pl.ds(1, cx_n + 2)] - apply(x0_ref[c, pl.ds(1, cx_n + 4)])
        r_own = own(r)
        v = apply(r)
        v_own = own(v)
        vk_ref[c, pl.ds(3, cx_n), pl.ds(0, cz_n)] = v[:, :cz_n]
        dots.append([(r_own, r_own), (r_own, v_own)])
    lots.append(0)
    to_corners(vk_ref, vk_ref, 3, 2)
    zero = jnp.zeros((8, ny), jnp.float32)
    sums_start(0, [p for d in dots for p in d + [(zero, zero)] * (PAD - 2)])
    to_z(vk_ref, vk_ref, 3, 2, 3)
    to_x(vk_ref, vk_ref, 3, 2, 3)

    arrive(1)
    beyond = pl.ds(cz_n, 8)
    nearest = (slot[cz_n:] == cz_n) | (slot[cz_n:] == deep - 1)
    farthest = (slot[cz_n:] == cz_n + 2) | (slot[cz_n:] == deep - 3)
    middle = pl.ds(3, cx_n)
    for f in range(4):
        face_ref[f, middle, beyond] = jnp.where(
            nearest, face_ref[f, middle, beyond], face_late[f, middle]
        )
        for x in (1, cx_n + 3):
            face_ref[f, pl.ds(x, 2), beyond] = face_late[f, pl.ds(x, 2)]
    prepare(0, cx_n + 4)
    inside = pl.ds(2, cx_n)
    for c in range(3):
        x0_ref[c, middle, beyond] = jnp.where(
            farthest, x0_late[c, middle], x0_ref[c, middle, beyond]
        )
        for x in (1, cx_n + 3):
            x0_ref[c, pl.ds(x, 2), beyond] = x0_late[c, pl.ds(x, 2)]
        src_ref[c, inside, beyond] = jnp.where(
            nearest, src_ref[c, inside, beyond], src_late[c, inside]
        )
        for x in (1, cx_n + 2):
            src_ref[c, x, beyond] = src_late[c, x]
        r = src_ref[c] - apply(x0_ref[c])
        res_ref[c] = r
        v_ref[c] = apply(r)

    arrive(3)
    m0, m1 = sums_end(0, 2)
    sigma = m1 / m0
    mine = (slot <= cz_n) | (slot == deep - 1)
    body_rows = slot < cz_n
    dots = []
    for c in range(3):
        s = sigma[c : c + 1]
        mid = jnp.where(mine, v_ref[c, pl.ds(1, cx_n)], vk_ref[c, pl.ds(3, cx_n)])
        low = jnp.where(body_rows, v_ref[c, 0], vk_ref[c, 2])
        high = jnp.where(body_rows, v_ref[c, cx_n + 1], vk_ref[c, cx_n + 3])
        v = jnp.concatenate(
            [vk_ref[c, pl.ds(0, 2)], low[None], mid, high[None], vk_ref[c, pl.ds(cx_n + 4, 2)]], 0
        )
        r = res_ref[c]
        u = apply(v)
        v = v[1:-1]
        a1 = v - s * r
        a2 = (u - s * v) - s * a1
        a3 = apply(a2) - s * a2[1:-1]
        a4 = apply(a3) - s * a3[1:-1]
        r0, b1, b2, b3, b4 = own(r), own(a1), own(a2), own(a3), own(a4)
        dots += [
            (r0, b1), (b1, b1), (b1, b2), (b2, b2), (b2, b3), (b3, b3), (b3, b4), (b4, b4)
        ]
        a1_ref[c] = a1[1:-1]
        a2_ref[c] = a2[1:-1]
        a3_ref[c] = a3
    sums_start(1, dots)
    arrive(2)
    for block in blocks:
        block.wait()
    for x in range(cx_n + 4):
        mark = code_ref[x] >= COARSE
        edge = floor | lid
        pd = jnp.where(edge, jnp.where(mark, 6.0, 5.0), 6.0)
        pd_ref[x] = pd
        share_ref[x] = jacobi_weight / pd
        cell_ref[x] = jnp.where(mark, code_ref[x] - COARSE, code_ref[x])
    mu = [m0] + sums_end(1, PAD)

    def times(p):
        out = [sigma * p[0]]
        for i in range(1, len(p)):
            out.append(p[i - 1] + sigma * p[i])
        return out + [p[-1]]

    def dot(p, q):
        total = 0.0
        for n in range(len(p) + len(q) - 1):
            terms = [p[i] * q[n - i] for i in range(len(p)) if 0 <= n - i < len(q)]
            total = total + sum(terms[1:], terms[0]) * mu[n]
        return total

    def against(p):
        return sum((p[i] * mu[i] for i in range(1, len(p))), p[0] * mu[0])

    alpha = m0 / (sigma * m0 + mu[1])
    s1 = [1.0 - alpha * sigma, -alpha]
    t1 = times(s1)
    omega = dot(s1, t1) / dot(t1, t1)
    rho_new = against(s1) - omega * against(t1)
    beta = (rho_new / m0) * (alpha / omega)
    r1 = [s1[0] - omega * t1[0], s1[1] - omega * t1[1], -omega * t1[2]]
    p2 = [r1[0] + beta * (1.0 - omega * sigma), r1[1] - beta * omega, r1[2]]
    v2 = times(p2)
    alpha2 = rho_new / against(v2)
    s2 = [r1[i] - alpha2 * v2[i] for i in range(3)] + [-alpha2 * v2[3]]
    t2 = times(s2)
    omega2 = dot(s2, t2) / dot(t2, t2)
    weight = [
        alpha + omega * s1[0] + alpha2 * p2[0] + omega2 * s2[0],
        omega * s1[1] + alpha2 * p2[1] + omega2 * s2[1],
        alpha2 * p2[2] + omega2 * s2[2],
        omega2 * s2[3],
    ]
    speed = []
    for c in range(3):
        w = [k[c : c + 1] for k in weight]
        field = x0_ref[c, pl.ds(2, cx_n + 2)] + w[0] * res_ref[c, pl.ds(1, cx_n + 2)]
        field += w[1] * a1_ref[c] + w[2] * a2_ref[c] + w[3] * a3_ref[c]
        vel_ref[c] = field[1:-1, :cz_n]
        speed.append(field)
    ux, uz, uy = speed
    div = (ux[1:-1] - ux[:-2]) + (uz[1:-1] - z_roll(uz[1:-1], 1))
    uy = uy[1:-1]
    div = div + (uy - jnp.where(floor, 0.0, y_prev(uy)))
    share = share_ref[pl.ds(2, cx_n)]
    q = share * div
    q_ref[pl.ds(3, cx_n), pl.ds(0, cz_n)] = q[:, :cz_n]
    lots.append(0)
    to_corners(q_ref, q_ref, 3, 2)
    to_z(q_ref, q_ref, 3, 1, 3)
    to_x(q_ref, q_ref, 3, 1, 3)

    def smooth(f):
        n = f.shape[0] - 2
        h = (n - cx_n) // 2
        g = f[1:-1]
        near = (f[2:] + f[:-2]) + (z_roll(g, 1) + z_roll(g, -1))
        near += jnp.where(lid, 0.0, y_next(g)) + jnp.where(floor, 0.0, y_prev(g))
        return pd_ref[pl.ds(2 - h, n)] * g - near

    def shares(h):
        return share_ref[pl.ds(2 - h, cx_n + 2 * h)]

    blank = jnp.zeros((2, deep, ny), jnp.float32)
    mine = jnp.where(body_rows, q, 0.0)
    first_cut = -smooth(jnp.concatenate([blank, mine, blank], 0))
    trace = jnp.concatenate(
        [first_cut[:1], first_cut[1:-1] + jnp.where(body_rows, div, 0.0), first_cut[-1:]], 0
    )
    full = jnp.concatenate([blank[:1], trace, blank[:1]], 0)
    full = full - smooth(jnp.concatenate([blank, shares(1) * trace, blank], 0))

    part = [[] for _ in range(6)]
    for m in range(COARSE):
        hit = jnp.where(cell_ref[...] == m, full, 0.0)
        flat = hit[:, :cz_n].reshape(-1, 8, ny)
        step = cz_n // 8
        top_rows = hit[:, cz_n:]
        part[0].append(jnp.sum(flat[: 2 * step], axis=0, keepdims=True))
        part[1].append(jnp.sum(flat[2 * step : -2 * step], axis=0, keepdims=True))
        part[2].append(jnp.sum(flat[-2 * step :], axis=0, keepdims=True))
        part[3].append(top_rows[1:2])
        part[4].append(jnp.sum(top_rows[2:-2], axis=0, keepdims=True))
        part[5].append(top_rows[-2:-1])
    part = [jnp.concatenate(p, 0) for p in part]
    upper_half = lax.broadcasted_iota(jnp.int32, (COARSE, 8, ny), 1) < 4

    def total_of(p):
        return jnp.sum(jnp.sum(p, axis=1), axis=1, keepdims=True)

    shape = (COARSE, lanes)
    spots = (south[1], gz, north[1])
    places = [
        lax.broadcasted_iota(jnp.int32, shape, 1)
        == lax.broadcasted_iota(jnp.int32, shape, 0) + spot * COARSE
        for spot in spots
    ]
    for k in range(3):
        cols = [
            total_of(jnp.where(upper_half, 0.0, part[3 + k])), total_of(part[k]),
            total_of(jnp.where(upper_half, part[3 + k], 0.0)),
        ]
        line = sum(
            jnp.where(place, jnp.broadcast_to(col, shape), 0.0)
            for place, col in zip(places, cols)
        )
        msg_c[k] = jnp.sum(line, axis=0, keepdims=True)
    scatter(msg_c, got_c, coarse_sem, [at(o) for o in spread_to])

    for i in range(4):
        settle(near_s.at[i], lots[i])
    arrive(4)
    ext = q_ref[...]
    q = 2.0 * ext[1:-1] - shares(2) * smooth(ext)
    q = q[1:-1] + ext[2:-2] - shares(1) * smooth(q)
    q = q[1:-1] + ext[3:-3] - shares(0) * smooth(q)

    settle(near_s.at[4], lots[4])
    for k in range(2):
        pltpu.make_async_copy(got_c, got_c, coarse_sem.at[k]).wait()

    def restricted(t):
        rows_in = [
            got_c[spread_to.index(fold(-j, k)), t - j + 1]
            for j in (t - 1, t, t + 1) for k in range(n_gz) if fold(-j, k) != (0, 0)
        ]
        return sum(rows_in, msg_c[t + 1])

    def corrections(inv, coarse):
        out = []
        for spot in spots:
            block = inv[pl.ds(pl.multiple_of(spot * COARSE, COARSE), COARSE), :]
            col = jnp.sum(block * coarse[:, : block.shape[1]], axis=1, keepdims=True)
            out.append(jnp.broadcast_to(col, (COARSE, ny)))
        return out

    def lift(cell, pick):
        add = jnp.broadcast_to(pick(0), cell.shape)
        for m in range(1, COARSE):
            add = jnp.where(cell == m, pick(m), add)
        return add

    corr = [corrections(inv, restricted(t)) for inv, t in zip((inv_w, inv_ref, inv_e), (-1, 0, 1))]
    half = lax.broadcasted_iota(jnp.int32, (8, ny), 0) < 4
    spans = (pl.ds(0, 2), pl.ds(2, cx_n), pl.ds(cx_n + 2, 2))
    raised = []
    for k in range(3):
        cell = cell_ref[spans[k]]
        inside = lift(cell[:, :cz_n], lambda m: corr[k][1][m : m + 1])
        outside = lift(
            cell[:, cz_n:], lambda m: jnp.where(half, corr[k][2][m : m + 1], corr[k][0][m : m + 1])
        )
        raised.append(jnp.concatenate([inside, outside], 1))
    e = jnp.concatenate(raised, 0)
    e = e[1:-1] - shares(1) * smooth(e)
    e = e[1:-1] - shares(0) * smooth(e)
    out_ref[...] = (q + e)[:, :cz_n]


def put(a_ref, b_ref, a_out, b_out, sem):
    copies = [
        pltpu.make_async_copy(a_ref, a_out, sem.at[0]), pltpu.make_async_copy(b_ref, b_out, sem.at[1])
    ]
    for copy in copies:
        copy.start()
    for copy in copies:
        copy.wait()


def body(n_gx, n_gz, velocity_old, source, diag_coef, face_coef, bc_flags, coarse_map, coarse_inverse):
    cx_n, cz_n, ny = diag_coef.shape
    rows = cx_n * cz_n
    deep = cz_n + 8
    group = coarse_inverse.shape[1]
    lanes = -(-group // 128) * 128
    f32 = jnp.float32
    vmem = pltpu.VMEM
    dma = pltpu.SemaphoreType.DMA
    n_spread = min(5, n_gx) * n_gz - 1
    n_sum = n_gx * n_gz - 1 if n_gx * n_gz <= DIRECT else n_gx - 1

    def block(fields, halo):
        return vmem((fields, cx_n + 2 * halo, deep, ny), f32)

    scratch = [
        block(3, 3),
        block(3, 2),
        block(4, 3),
        vmem(bc_flags.shape, jnp.int32),
        vmem((rows, ny), jnp.int32),
        vmem(coarse_inverse.shape, f32),
        vmem((3, cx_n + 6, 8, ny), f32),
        vmem((3, cx_n + 4, 8, ny), f32),
        vmem((4, cx_n + 6, 8, ny), f32),
        block(2, 2),
        block(3, 2),
        block(3, 1),
        block(3, 3),
        block(3, 1),
        block(3, 1),
        block(3, 1),
        vmem((cx_n + 4, deep, ny), jnp.int32),
        vmem((cx_n + 4, deep, ny), jnp.int32),
        vmem((cx_n + 4, deep, ny), f32),
        vmem((cx_n + 4, deep, ny), f32),
        vmem((cx_n + 6, deep, ny), f32),
        vmem(coarse_inverse.shape, f32),
        vmem(coarse_inverse.shape, f32),
        vmem((2, 1, 128), f32),
        vmem((2, n_sum, 1, 128), f32),
        vmem((2, 1, 128), f32),
        vmem((2, n_gz - 1, 1, 128), f32),
        vmem((3, 1, lanes), f32),
        vmem((n_spread, 3, 1, lanes), f32),
        vmem((2048, ny), f32),
        dma((5,)),
        dma((5,)),
        dma((2, 2, 2) if n_sum < n_gx * n_gz - 1 else (2, 1, 2)),
        dma((2,)),
        dma((4,)),
        dma((2,)),
        dma((2,)),
    ]
    spec = pl.BlockSpec(memory_space=pltpu.VMEM)
    velocity, pressure = pl.pallas_call(
        functools.partial(kernel, (n_gx, n_gz, cx_n, cz_n, ny, lanes)),
        out_shape=(
            jax.ShapeDtypeStruct((3, cx_n, cz_n, ny), f32),
            jax.ShapeDtypeStruct((cx_n, cz_n, ny), f32),
        ),
        in_specs=[pl.BlockSpec(memory_space=pltpu.HBM)] * 7,
        out_specs=(spec, spec),
        scratch_shapes=scratch,
        compiler_params=pltpu.CompilerParams(
            collective_id=0, has_side_effects=True, vmem_limit_bytes=48 * 1024 * 1024
        ),
        name="corrector",
    )(
        *[
            pltpu.with_memory_space_constraint(a, pltpu.HBM)
            for a in (
                velocity_old,
                source,
                diag_coef,
                face_coef,
                bc_flags,
                coarse_map.reshape(rows, ny),
                coarse_inverse,
            )
        ]
    )
    velocity, pressure = pl.pallas_call(
        put,
        out_shape=(
            jax.ShapeDtypeStruct(velocity.shape, f32),
            jax.ShapeDtypeStruct(pressure.shape, f32),
        ),
        in_specs=[spec, spec],
        out_specs=[pl.BlockSpec(memory_space=pltpu.HBM)] * 2,
        scratch_shapes=[dma((2,))],
        name="put",
    )(*[pltpu.with_memory_space_constraint(a, pltpu.VMEM) for a in (velocity, pressure)])
    return velocity, pressure


def solution(mesh):
    placed = (
        P(None, "gx", "gz", None),
        P(None, "gx", "gz", None),
        P("gx", "gz", None),
        P(None, "gx", "gz", None),
        P(None, "gx", "gz"),
        P("gx", "gz", None),
        P("gx", None),
    )
    return jax.shard_map(
        functools.partial(body, mesh.shape["gx"], mesh.shape["gz"]),
        mesh=mesh,
        in_specs=placed,
        out_specs=(P(None, "gx", "gz", None), P("gx", "gz", None)),
        check_vma=False,
    )
```

```python
import functools
import math

import jax
import jax.numpy as jnp
from jax import lax
from jax.experimental import pallas as pl
from jax.experimental.pallas import tpu as pltpu
from jax.sharding import PartitionSpec as P

COARSE = 16
PAD = 8
DIRECT = 64

jacobi_weight = 2.0 / 3.0
MESH = pl.DeviceIdType.MESH


def kernel(
    dims,
    x0_in, src_in, diag_in, face_in, bc_in, map_in, inv_in,
    vel_ref, out_ref,
    x0_ref, src_ref, face_ref, bc_ref, map_ref, inv_ref,
    x0_late, rho_ref, rho_late, edge_ref,
    coef, res_ref, v_ref, vk_ref, a1_ref, a2_ref, a3_ref,
    code_ref, cell_ref, pd_ref, share_ref, q_ref, inv_w, inv_e,
    msg, got, msg_z, got_z, msg_c, got_c,
    tally, near_s, near_r, sum_sem, coarse_sem, load_sem, side_s, side_r,
):
    n_gx, n_gz, cx_n, cz_n, ny, lanes = dims
    rows = cx_n * cz_n
    deep = x0_ref.shape[2]
    gx = lax.axis_index("gx")
    gz = lax.axis_index("gz")
    east = (lax.rem(gx + 1, n_gx), gz)
    west = (lax.rem(gx + n_gx - 1, n_gx), gz)
    north = (gx, lax.rem(gz + 1, n_gz))
    south = (gx, lax.rem(gz + n_gz - 1, n_gz))
    row_x = [(lax.rem(gx + d, n_gx), gz) for d in range(1, n_gx)]
    row_z = [(gx, lax.rem(gz + d, n_gz)) for d in range(1, n_gz)]
    direct = n_gx * n_gz <= DIRECT

    def send(src, dst, ssem, rsem, to):
        copy = pltpu.make_async_remote_copy(
            src_ref=src, dst_ref=dst, send_sem=ssem, recv_sem=rsem,
            device_id=to, device_id_type=MESH,
        )
        copy.start()
        return copy

    def settle(sem, count):
        span = tally.at[pl.ds(0, count)]
        pltpu.make_async_copy(span, span, sem).wait()

    corners = [
        (east[0], north[1]), (east[0], south[1]), (west[0], north[1]), (west[0], south[1])
    ]

    def at(offset):
        return (lax.rem(gx + offset[0], n_gx), lax.rem(gz + offset[1], n_gz))

    def fold(d, k):
        return (d % n_gx, k % n_gz)

    around = {fold(d, k) for d in (-1, 0, 1) for k in (-1, 0, 1)} - {(0, 0)}
    spread_to = sorted({fold(d, k) for d in range(-2, 3) for k in range(n_gz)} - {(0, 0)})
    every = {(d, k) for d in range(n_gx) for k in range(n_gz)}
    if direct:
        sum_to = [
            (d, k)
            for k in sorted(range(n_gz), key=lambda k: -min(k, n_gz - k))
            for d in sorted(range(n_gx), key=lambda d: -min(d, n_gx - d))
            if d or k
        ]
        met = set(around)
        while True:
            seen = met | {fold(a + d, b + k) for a, b in around for d, k in met} | {(0, 0)}
            left = sorted(every - seen, key=lambda o: (min(o[1], n_gz - o[1]), o))
            if not left:
                break
            met |= {left[0], fold(-left[0][0], -left[0][1])}
        sum_to = [at(o) for o in sum_to]
    else:
        sum_to = row_x
        met = around | set(spread_to)
        met |= {(d, 0) for d in range(1, n_gx)} | {(0, k) for k in range(1, n_gz)}
    near_first = sorted(around, key=lambda o: (o[0] == 0) + (o[1] == 0) * 2)
    partners = [at(o) for o in near_first] + [at(o) for o in sorted(met - around)]

    def inner(ref, halo):
        return ref.at[..., pl.ds(halo, cx_n), pl.ds(0, cz_n), :]

    loads = [
        pltpu.make_async_copy(a, b, load_sem.at[max(0, i - 3)])
        for i, (a, b) in enumerate(
            [
                (x0_in, inner(x0_ref, 2)), (face_in, inner(face_ref.at[pl.ds(0, 3)], 3)),
                (diag_in, inner(face_ref.at[3], 3)), (src_in, src_ref),
                (bc_in, bc_ref), (map_in, map_ref), (inv_in, inv_ref),
            ]
        )
    ]
    barrier = pltpu.get_barrier_semaphore()
    for other in partners:
        pl.semaphore_signal(barrier, inc=1, device_id=other, device_id_type=MESH)
    for load in loads:
        load.start()
    settle(load_sem.at[0], 10 * rows)
    pl.semaphore_wait(barrier, len(partners))


    def side_x(sign, halo, a, b):
        if sign > 0:
            return pl.ds(halo + cx_n - b, b - a + 1), pl.ds(halo - b, b - a + 1)
        return pl.ds(halo + a - 1, b - a + 1), pl.ds(halo + cx_n + a - 1, b - a + 1)

    def side_z(sign, a, b):
        if sign > 0:
            return pl.ds(cz_n - b, b - a + 1), pl.ds(deep - b, b - a + 1)
        return pl.ds(a - 1, b - a + 1), pl.ds(cz_n + a - 1, b - a + 1)

    lots = []

    def ship(src, dst, to, where_from, where_to):
        target = dst.at[(..., *where_to, slice(None))]
        lots[-1] += math.prod(target.shape[:-1])
        i = len(lots) - 1
        send(src.at[(..., *where_from, slice(None))], target, near_s.at[i], near_r.at[i], to)

    def arrive(i):
        settle(near_r.at[i], lots[i])

    def to_corners(src, dst, halo, n, land=None):
        land = halo if land is None else land
        for to, sx, sz in zip(corners, (1, 1, -1, -1), (1, -1, 1, -1)):
            fz, tz = side_z(sz, 1, n)
            ship(src, dst, to, (side_x(sx, halo, 1, n)[0], fz), (side_x(sx, land, 1, n)[1], tz))

    def to_z(src, dst, halo, a, b, ways=(1, -1), land=None, start=0, size=cx_n):
        land = halo if land is None else land
        for sz in ways:
            fz, tz = side_z(sz, a, b)
            where_from, where_to = (pl.ds(halo + start, size), fz), (pl.ds(land + start, size), tz)
            ship(src, dst, north if sz > 0 else south, where_from, where_to)

    def to_x(src, dst, halo, a, b, ways=(1, -1), land=None, start=0, size=cz_n):
        land = halo if land is None else land
        for sx in ways:
            fx, tx = side_x(sx, halo, a, b)[0], side_x(sx, land, a, b)[1]
            z = pl.ds(start, size)
            ship(src, dst, east if sx > 0 else west, (fx, z), (tx, z))

    both = pl.ds(0, 2)
    lots.append(0)
    to_corners(x0_ref, x0_ref, 2, 1)
    to_corners(face_ref.at[both], edge_ref, 3, 1, land=1)
    to_z(x0_ref, x0_ref, 2, 1, 1)
    to_z(face_ref.at[1], edge_ref.at[1], 3, 1, 1, (1,), land=1)
    to_z(face_ref.at[0], edge_ref.at[0], 3, 1, 1, land=1, start=cx_n - 1, size=1)
    to_x(x0_ref, x0_ref, 2, 1, 1)
    to_x(face_ref.at[0], edge_ref.at[0], 3, 1, 1, (1,), land=1)
    to_x(face_ref.at[1], edge_ref.at[1], 3, 1, 1, land=1, start=cz_n - 1, size=1)

    level = lax.broadcasted_iota(jnp.int32, (rows, ny), 1)
    bottom = level == 0
    top = level == ny - 1
    def y_prev(f):
        return pltpu.roll(f, 1, f.ndim - 1)

    def y_next(f):
        return pltpu.roll(f, ny - 1, f.ndim - 1)

    own_z = pl.ds(0, cz_n)
    own_x = pl.ds(3, cx_n)
    shelf = lax.broadcasted_iota(jnp.int32, (cz_n, ny), 0)
    ends = lax.broadcasted_iota(jnp.int32, (cz_n, ny), 1)
    cy = face_ref[2, own_x, own_z]
    rim = (ends == 0) | (ends == ny - 1)
    main = face_ref[3, own_x, own_z] + jnp.where(rim, jnp.broadcast_to(cy[..., ny - 1 :], cy.shape), 0.0)
    rise = jnp.where(ends == ny - 1, 0.0, cy)

    def within(f):
        none = jnp.zeros((1, cz_n, ny), jnp.float32)
        flux_x = face_ref[0, pl.ds(3, cx_n - 1), own_z] * (f[:-1] - f[1:])
        flux_x = jnp.concatenate([none, flux_x, none], 0)
        flux_z = face_ref[1, own_x, own_z] * (f - pltpu.roll(f, cz_n - 1, 1))
        flux_z = jnp.where(shelf == cz_n - 1, 0.0, flux_z)
        flux_y = rise * (f - y_next(f))
        total = main * f + (flux_x[1:] - flux_x[:-1])
        return total + (flux_z - pltpu.roll(flux_z, 1, 1)) + (flux_y - y_prev(flux_y))

    for c in range(3):
        rho_ref[c, pl.ds(1, cx_n), own_z] = src_ref[c] - within(x0_ref[c, pl.ds(2, cx_n), own_z])
    to_z(rho_ref, rho_ref, 1, 1, 1)
    to_x(rho_ref, rho_ref, 1, 1, 1)

    lots.append(0)
    to_corners(x0_ref, x0_late, 2, 2)
    to_corners(face_ref, face_ref, 3, 2)
    to_corners(rho_ref, rho_late, 1, 1, land=2)
    to_z(rho_ref, rho_late, 1, 2, 2, land=2)
    for x in (0, cx_n - 1):
        to_z(x0_ref, x0_late, 2, 2, 2, start=x, size=1)
    to_z(face_ref, face_ref, 3, 1, 2)
    to_z(face_ref.at[1], face_ref.at[1], 3, 3, 3, (1,))
    to_x(rho_ref, rho_late, 1, 2, 2, land=2)
    for z in (0, cz_n - 1):
        to_x(x0_ref, x0_late, 2, 2, 2, start=z, size=1)
    to_x(face_ref, face_ref, 3, 1, 2)
    to_x(face_ref.at[0], face_ref.at[0], 3, 3, 3, (1,))

    eye = lax.broadcasted_iota(jnp.int32, (cz_n, cz_n), 0) == lax.broadcasted_iota(
        jnp.int32, (cz_n, cz_n), 1
    )

    def column(side):
        flags = bc_ref[side]
        parts = [
            jnp.sum(
                jnp.where(eye, jnp.broadcast_to(flags[i : i + 1], (cz_n, cz_n)), 0),
                axis=1, keepdims=True,
            )
            for i in range(cx_n)
        ]
        return jnp.broadcast_to(jnp.concatenate(parts, 0), (rows, ny))

    def scatter(msg, got, sem, others):
        for d, to in enumerate(others):
            send(msg, got.at[d], sem.at[0], sem.at[1], to)

    def gathered(msg, got, sem):
        for k in range(2):
            pltpu.make_async_copy(got, got, sem.at[k]).wait()
        return msg[...] + jnp.sum(got[...], axis=0)

    def z_roll(f, shift):
        flat = f.reshape((-1,) + f.shape[-2:])
        return pltpu.roll(flat, shift % deep, 1).reshape(f.shape)

    def apply(f):
        h = (f.shape[0] - cx_n) // 2 - 1
        n = cx_n + 2 * h
        g = f[1:-1]
        flux_x = face_ref[0, pl.ds(2 - h, n + 1)] * (f[:-1] - f[1:])
        flux_z = face_ref[1, pl.ds(3 - h, n)] * (g - z_roll(g, -1))
        flux_y = coef[1, pl.ds(2 - h, n)] * (g - y_next(g))
        total = coef[0, pl.ds(2 - h, n)] * g + (flux_x[1:] - flux_x[:-1])
        return total + (flux_z - z_roll(flux_z, 1)) + (flux_y - y_prev(flux_y))

    def own(f):
        h = (f.shape[0] - cx_n) // 2
        return f[h : h + cx_n, :cz_n].reshape(rows, ny)

    def pack(pairs):
        sums = [jnp.sum(a * b, axis=0, keepdims=True) for a, b in pairs]
        while len(sums) < 3 * PAD:
            sums.append(jnp.zeros_like(sums[0]))
        total = jnp.sum(jnp.concatenate(sums, 0), axis=1, keepdims=True)
        shape = (3 * PAD, 128)
        pick = lax.broadcasted_iota(jnp.int32, shape, 0) == lax.broadcasted_iota(
            jnp.int32, shape, 1
        )
        return jnp.sum(
            jnp.where(pick, jnp.broadcast_to(total, shape), 0.0), axis=0, keepdims=True
        )

    def sums_start(i, pairs):
        msg[i] = pack(pairs)
        scatter(msg.at[i], got.at[i], sum_sem.at[i, 0], sum_to)

    def sums_end(i, count):
        total = gathered(msg.at[i], got.at[i], sum_sem.at[i, 0])
        if not direct:
            msg_z[i] = total
            scatter(msg_z.at[i], got_z.at[i], sum_sem.at[i, 1], row_z)
            total = gathered(msg_z.at[i], got_z.at[i], sum_sem.at[i, 1])
        shape = (8, 128)
        place = lax.broadcasted_iota(jnp.int32, shape, 0) * PAD
        lane = lax.broadcasted_iota(jnp.int32, shape, 1)
        wide = jnp.broadcast_to(total, shape)
        return [
            jnp.broadcast_to(
                jnp.sum(jnp.where(lane == place + k, wide, 0.0), axis=1, keepdims=True), shape
            )
            for k in range(count)
        ]

    slot = lax.broadcasted_iota(jnp.int32, (deep, ny), 0)
    floor = lax.broadcasted_iota(jnp.int32, (deep, ny), 1) == 0
    lid = lax.broadcasted_iota(jnp.int32, (deep, ny), 1) == ny - 1
    for load in loads[4:]:
        load.wait()
    flag = jnp.where(bottom, column(0), 0) + jnp.where(top, column(1), 0)
    code = map_ref[...] + COARSE * flag
    code_ref[pl.ds(2, cx_n), pl.ds(0, cz_n)] = code.reshape(cx_n, cz_n, ny)

    lots.append(0)
    to_corners(code_ref, code_ref, 2, 1)
    to_z(code_ref, code_ref, 2, 1, 2)
    to_x(code_ref, code_ref, 2, 1, 2)
    blocks = [
        send(inv_ref, inv_w, side_s.at[0], side_r.at[0], east),
        send(inv_ref, inv_e, side_s.at[1], side_r.at[1], west),
    ]

    arrive(0)

    def prepare(low, high):
        for x in range(low, high):
            cy = face_ref[2, x + 1]
            wall = jnp.where(floor | lid, jnp.broadcast_to(cy[:, ny - 1 :], (deep, ny)), 0.0)
            coef[0, x] = face_ref[3, x + 1] + wall
            coef[1, x] = jnp.where(lid, 0.0, cy)

    seam = (slot == cz_n - 1) | (slot == deep - 1)

    def mend(part, f, coef_w, coef_e, coef_z):
        flux_w, flux_e = coef_w * (f[0] - f[1]), coef_e * (f[-2] - f[-1])
        flux_z = jnp.where(seam, coef_z * (f - z_roll(f, -1)), 0.0)
        part = part - (flux_z - z_roll(flux_z, 1))
        return jnp.concatenate(
            [
                (part[0] - flux_w)[None], (part[1] + flux_w)[None], part[2:-2],
                (part[-2] - flux_e)[None], (part[-1] + flux_e)[None],
            ], 0,
        )

    tail = pl.ds(cz_n, 8)
    coef_w = edge_ref[0, 0]
    coef_e = jnp.concatenate([face_ref[0, cx_n + 2, own_z], edge_ref[0, cx_n, tail]], 0)
    coef_z = jnp.concatenate(
        [edge_ref[1, pl.ds(0, 1), own_z], face_ref[1, own_x, own_z], edge_ref[1, pl.ds(cx_n + 1, 1), own_z]], 0
    )
    coef_z = jnp.concatenate([coef_z, edge_ref[1, :, tail]], 1)
    dots = []
    for c in range(3):
        r = mend(rho_ref[c], x0_ref[c, pl.ds(1, cx_n + 2)], coef_w, coef_e, coef_z)
        r_own = own(r)
        v = jnp.concatenate([-within(r[1:-1, :cz_n]), jnp.zeros((cx_n, 8, ny), jnp.float32)], 1)
        none = jnp.zeros((1, deep, ny), jnp.float32)
        v = -mend(jnp.concatenate([none, v, none], 0), r, coef_w, coef_e, coef_z)
        v_own = own(v)
        vk_ref[c, pl.ds(3, cx_n), own_z] = v[1:-1, :cz_n]
        dots.append([(r_own, r_own), (r_own, v_own)])
    lots.append(0)
    to_corners(vk_ref, vk_ref, 3, 2)
    zero = jnp.zeros((8, ny), jnp.float32)
    sums_start(0, [p for d in dots for p in d + [(zero, zero)] * (PAD - 2)])
    to_z(vk_ref, vk_ref, 3, 2, 3)
    to_x(vk_ref, vk_ref, 3, 2, 3)

    arrive(1)
    prepare(0, cx_n + 4)
    mine = (slot <= cz_n) | (slot == deep - 1)
    body_rows = slot < cz_n

    def widen(near, far):
        n = near.shape[0] - 2
        mid = jnp.where(mine, near[1:-1], far[2:-2])
        low = jnp.where(body_rows, near[0], far[1])
        high = jnp.where(body_rows, near[n + 1], far[n + 2])
        return jnp.concatenate([far[:1], low[None], mid, high[None], far[-1:]], 0)

    coef_w, coef_e = face_ref[0, 2], face_ref[0, cx_n + 2]
    coef_z = face_ref[1, pl.ds(1, cx_n + 4)]
    for c in range(3):
        r = widen(rho_ref[c], rho_late[c])
        f = widen(x0_ref[c, pl.ds(1, cx_n + 2)], x0_late[c])
        flux_w, flux_e = coef_w * (f[1] - f[2]), coef_e * (f[-3] - f[-2])
        flux_z = jnp.where(seam, coef_z * (f - z_roll(f, -1)), 0.0)
        r = r - (flux_z - z_roll(flux_z, 1))
        r = jnp.concatenate(
            [
                r[:1], (r[1] - flux_w)[None], (r[2] + flux_w)[None], r[3:-3],
                (r[-3] - flux_e)[None], (r[-2] + flux_e)[None], r[-1:],
            ], 0,
        )
        res_ref[c] = r
        v_ref[c] = apply(r)

    arrive(3)
    m0, m1 = sums_end(0, 2)
    sigma = m1 / m0
    dots = []
    for c in range(3):
        s = sigma[c : c + 1]
        mid = jnp.where(mine, v_ref[c, pl.ds(1, cx_n)], vk_ref[c, pl.ds(3, cx_n)])
        low = jnp.where(body_rows, v_ref[c, 0], vk_ref[c, 2])
        high = jnp.where(body_rows, v_ref[c, cx_n + 1], vk_ref[c, cx_n + 3])
        v = jnp.concatenate(
            [vk_ref[c, pl.ds(0, 2)], low[None], mid, high[None], vk_ref[c, pl.ds(cx_n + 4, 2)]], 0
        )
        r = res_ref[c]
        u = apply(v)
        v = v[1:-1]
        a1 = v - s * r
        a2 = (u - s * v) - s * a1
        a3 = apply(a2) - s * a2[1:-1]
        a4 = apply(a3) - s * a3[1:-1]
        r0, b1, b2, b3, b4 = own(r), own(a1), own(a2), own(a3), own(a4)
        dots += [
            (r0, b1), (b1, b1), (b1, b2), (b2, b2), (b2, b3), (b3, b3), (b3, b4), (b4, b4)
        ]
        a1_ref[c] = a1[1:-1]
        a2_ref[c] = a2[1:-1]
        a3_ref[c] = a3
    sums_start(1, dots)
    arrive(2)
    for block in blocks:
        block.wait()
    for x in range(cx_n + 4):
        mark = code_ref[x] >= COARSE
        edge = floor | lid
        pd = jnp.where(edge, jnp.where(mark, 6.0, 5.0), 6.0)
        pd_ref[x] = pd
        share_ref[x] = jacobi_weight / pd
        cell_ref[x] = jnp.where(mark, code_ref[x] - COARSE, code_ref[x])
    mu = [m0] + sums_end(1, PAD)

    def times(p):
        out = [sigma * p[0]]
        for i in range(1, len(p)):
            out.append(p[i - 1] + sigma * p[i])
        return out + [p[-1]]

    def dot(p, q):
        total = 0.0
        for n in range(len(p) + len(q) - 1):
            terms = [p[i] * q[n - i] for i in range(len(p)) if 0 <= n - i < len(q)]
            total = total + sum(terms[1:], terms[0]) * mu[n]
        return total

    def against(p):
        return sum((p[i] * mu[i] for i in range(1, len(p))), p[0] * mu[0])

    alpha = m0 / (sigma * m0 + mu[1])
    s1 = [1.0 - alpha * sigma, -alpha]
    t1 = times(s1)
    omega = dot(s1, t1) / dot(t1, t1)
    rho_new = against(s1) - omega * against(t1)
    beta = (rho_new / m0) * (alpha / omega)
    r1 = [s1[0] - omega * t1[0], s1[1] - omega * t1[1], -omega * t1[2]]
    p2 = [r1[0] + beta * (1.0 - omega * sigma), r1[1] - beta * omega, r1[2]]
    v2 = times(p2)
    alpha2 = rho_new / against(v2)
    s2 = [r1[i] - alpha2 * v2[i] for i in range(3)] + [-alpha2 * v2[3]]
    t2 = times(s2)
    omega2 = dot(s2, t2) / dot(t2, t2)
    weight = [
        alpha + omega * s1[0] + alpha2 * p2[0] + omega2 * s2[0],
        omega * s1[1] + alpha2 * p2[1] + omega2 * s2[1],
        alpha2 * p2[2] + omega2 * s2[2],
        omega2 * s2[3],
    ]
    speed = []
    for c in range(3):
        w = [k[c : c + 1] for k in weight]
        field = x0_ref[c, pl.ds(1, cx_n + 2)] + w[0] * res_ref[c, pl.ds(1, cx_n + 2)]
        field += w[1] * a1_ref[c] + w[2] * a2_ref[c] + w[3] * a3_ref[c]
        vel_ref[c] = field[1:-1, :cz_n]
        speed.append(field)
    ux, uz, uy = speed
    div = (ux[1:-1] - ux[:-2]) + (uz[1:-1] - z_roll(uz[1:-1], 1))
    uy = uy[1:-1]
    div = div + (uy - jnp.where(floor, 0.0, y_prev(uy)))
    share = share_ref[pl.ds(2, cx_n)]
    q = share * div
    q_ref[pl.ds(3, cx_n), pl.ds(0, cz_n)] = q[:, :cz_n]
    lots.append(0)
    to_corners(q_ref, q_ref, 3, 2)
    to_z(q_ref, q_ref, 3, 1, 3)
    to_x(q_ref, q_ref, 3, 1, 3)

    def smooth(f):
        n = f.shape[0] - 2
        h = (n - cx_n) // 2
        g = f[1:-1]
        near = (f[2:] + f[:-2]) + (z_roll(g, 1) + z_roll(g, -1))
        near += jnp.where(lid, 0.0, y_next(g)) + jnp.where(floor, 0.0, y_prev(g))
        return pd_ref[pl.ds(2 - h, n)] * g - near

    def shares(h):
        return share_ref[pl.ds(2 - h, cx_n + 2 * h)]

    blank = jnp.zeros((2, deep, ny), jnp.float32)
    mine = jnp.where(body_rows, q, 0.0)
    first_cut = -smooth(jnp.concatenate([blank, mine, blank], 0))
    trace = jnp.concatenate(
        [first_cut[:1], first_cut[1:-1] + jnp.where(body_rows, div, 0.0), first_cut[-1:]], 0
    )
    full = jnp.concatenate([blank[:1], trace, blank[:1]], 0)
    full = full - smooth(jnp.concatenate([blank, shares(1) * trace, blank], 0))

    part = [[] for _ in range(6)]
    for m in range(COARSE):
        hit = jnp.where(cell_ref[...] == m, full, 0.0)
        flat = hit[:, :cz_n].reshape(-1, 8, ny)
        step = cz_n // 8
        top_rows = hit[:, cz_n:]
        part[0].append(jnp.sum(flat[: 2 * step], axis=0, keepdims=True))
        part[1].append(jnp.sum(flat[2 * step : -2 * step], axis=0, keepdims=True))
        part[2].append(jnp.sum(flat[-2 * step :], axis=0, keepdims=True))
        part[3].append(top_rows[1:2])
        part[4].append(jnp.sum(top_rows[2:-2], axis=0, keepdims=True))
        part[5].append(top_rows[-2:-1])
    part = [jnp.concatenate(p, 0) for p in part]
    upper_half = lax.broadcasted_iota(jnp.int32, (COARSE, 8, ny), 1) < 4

    def total_of(p):
        return jnp.sum(jnp.sum(p, axis=1), axis=1, keepdims=True)

    shape = (COARSE, lanes)
    spots = (south[1], gz, north[1])
    places = [
        lax.broadcasted_iota(jnp.int32, shape, 1)
        == lax.broadcasted_iota(jnp.int32, shape, 0) + spot * COARSE
        for spot in spots
    ]
    for k in range(3):
        cols = [
            total_of(jnp.where(upper_half, 0.0, part[3 + k])), total_of(part[k]),
            total_of(jnp.where(upper_half, part[3 + k], 0.0)),
        ]
        line = sum(
            jnp.where(place, jnp.broadcast_to(col, shape), 0.0)
            for place, col in zip(places, cols)
        )
        msg_c[k] = jnp.sum(line, axis=0, keepdims=True)
    scatter(msg_c, got_c, coarse_sem, [at(o) for o in spread_to])

    for i in range(4):
        settle(near_s.at[i], lots[i])
    arrive(4)
    ext = q_ref[...]
    q = 2.0 * ext[1:-1] - shares(2) * smooth(ext)
    q = q[1:-1] + ext[2:-2] - shares(1) * smooth(q)
    q = q[1:-1] + ext[3:-3] - shares(0) * smooth(q)

    settle(near_s.at[4], lots[4])
    for k in range(2):
        pltpu.make_async_copy(got_c, got_c, coarse_sem.at[k]).wait()

    def restricted(t):
        rows_in = [
            got_c[spread_to.index(fold(-j, k)), t - j + 1]
            for j in (t - 1, t, t + 1) for k in range(n_gz) if fold(-j, k) != (0, 0)
        ]
        return sum(rows_in, msg_c[t + 1])

    def corrections(inv, coarse):
        out = []
        for spot in spots:
            block = inv[pl.ds(pl.multiple_of(spot * COARSE, COARSE), COARSE), :]
            col = jnp.sum(block * coarse[:, : block.shape[1]], axis=1, keepdims=True)
            out.append(jnp.broadcast_to(col, (COARSE, ny)))
        return out

    def lift(cell, pick):
        add = jnp.broadcast_to(pick(0), cell.shape)
        for m in range(1, COARSE):
            add = jnp.where(cell == m, pick(m), add)
        return add

    corr = [corrections(inv, restricted(t)) for inv, t in zip((inv_w, inv_ref, inv_e), (-1, 0, 1))]
    half = lax.broadcasted_iota(jnp.int32, (8, ny), 0) < 4
    spans = (pl.ds(0, 2), pl.ds(2, cx_n), pl.ds(cx_n + 2, 2))
    raised = []
    for k in range(3):
        cell = cell_ref[spans[k]]
        inside = lift(cell[:, :cz_n], lambda m: corr[k][1][m : m + 1])
        outside = lift(
            cell[:, cz_n:], lambda m: jnp.where(half, corr[k][2][m : m + 1], corr[k][0][m : m + 1])
        )
        raised.append(jnp.concatenate([inside, outside], 1))
    e = jnp.concatenate(raised, 0)
    e = e[1:-1] - shares(1) * smooth(e)
    e = e[1:-1] - shares(0) * smooth(e)
    out_ref[...] = (q + e)[:, :cz_n]


def put(a_ref, b_ref, a_out, b_out, sem):
    copies = [
        pltpu.make_async_copy(a_ref, a_out, sem.at[0]), pltpu.make_async_copy(b_ref, b_out, sem.at[1])
    ]
    for copy in copies:
        copy.start()
    for copy in copies:
        copy.wait()


def body(n_gx, n_gz, velocity_old, source, diag_coef, face_coef, bc_flags, coarse_map, coarse_inverse):
    cx_n, cz_n, ny = diag_coef.shape
    rows = cx_n * cz_n
    deep = cz_n + 8
    group = coarse_inverse.shape[1]
    lanes = -(-group // 128) * 128
    f32 = jnp.float32
    vmem = pltpu.VMEM
    dma = pltpu.SemaphoreType.DMA
    n_spread = min(5, n_gx) * n_gz - 1
    n_sum = n_gx * n_gz - 1 if n_gx * n_gz <= DIRECT else n_gx - 1

    def block(fields, halo):
        return vmem((fields, cx_n + 2 * halo, deep, ny), f32)

    scratch = [
        block(3, 2),
        vmem((3, cx_n, cz_n, ny), f32),
        block(4, 3),
        vmem(bc_flags.shape, jnp.int32),
        vmem((rows, ny), jnp.int32),
        vmem(coarse_inverse.shape, f32),
        block(3, 2),
        block(3, 1),
        block(3, 2),
        block(2, 1),
        block(2, 2),
        block(3, 2),
        block(3, 1),
        block(3, 3),
        block(3, 1),
        block(3, 1),
        block(3, 1),
        vmem((cx_n + 4, deep, ny), jnp.int32),
        vmem((cx_n + 4, deep, ny), jnp.int32),
        vmem((cx_n + 4, deep, ny), f32),
        vmem((cx_n + 4, deep, ny), f32),
        vmem((cx_n + 6, deep, ny), f32),
        vmem(coarse_inverse.shape, f32),
        vmem(coarse_inverse.shape, f32),
        vmem((2, 1, 128), f32),
        vmem((2, n_sum, 1, 128), f32),
        vmem((2, 1, 128), f32),
        vmem((2, n_gz - 1, 1, 128), f32),
        vmem((3, 1, lanes), f32),
        vmem((n_spread, 3, 1, lanes), f32),
        vmem((2048, ny), f32),
        dma((5,)),
        dma((5,)),
        dma((2, 2, 2) if n_sum < n_gx * n_gz - 1 else (2, 1, 2)),
        dma((2,)),
        dma((4,)),
        dma((2,)),
        dma((2,)),
    ]
    spec = pl.BlockSpec(memory_space=pltpu.VMEM)
    velocity, pressure = pl.pallas_call(
        functools.partial(kernel, (n_gx, n_gz, cx_n, cz_n, ny, lanes)),
        out_shape=(
            jax.ShapeDtypeStruct((3, cx_n, cz_n, ny), f32),
            jax.ShapeDtypeStruct((cx_n, cz_n, ny), f32),
        ),
        in_specs=[pl.BlockSpec(memory_space=pltpu.HBM)] * 7,
        out_specs=(spec, spec),
        scratch_shapes=scratch,
        compiler_params=pltpu.CompilerParams(
            collective_id=0, has_side_effects=True, vmem_limit_bytes=48 * 1024 * 1024
        ),
        name="corrector",
    )(
        *[
            pltpu.with_memory_space_constraint(a, pltpu.HBM)
            for a in (
                velocity_old,
                source,
                diag_coef,
                face_coef,
                bc_flags,
                coarse_map.reshape(rows, ny),
                coarse_inverse,
            )
        ]
    )
    velocity, pressure = pl.pallas_call(
        put,
        out_shape=(
            jax.ShapeDtypeStruct(velocity.shape, f32),
            jax.ShapeDtypeStruct(pressure.shape, f32),
        ),
        in_specs=[spec, spec],
        out_specs=[pl.BlockSpec(memory_space=pltpu.HBM)] * 2,
        scratch_shapes=[dma((2,))],
        name="put",
    )(*[pltpu.with_memory_space_constraint(a, pltpu.VMEM) for a in (velocity, pressure)])
    return velocity, pressure


def solution(mesh):
    placed = (
        P(None, "gx", "gz", None),
        P(None, "gx", "gz", None),
        P("gx", "gz", None),
        P(None, "gx", "gz", None),
        P(None, "gx", "gz"),
        P("gx", "gz", None),
        P("gx", None),
    )
    return jax.shard_map(
        functools.partial(body, mesh.shape["gx"], mesh.shape["gz"]),
        mesh=mesh,
        in_specs=placed,
        out_specs=(P(None, "gx", "gz", None), P("gx", "gz", None)),
        check_vma=False,
    )
```

```python
import functools
import math

import jax
import jax.numpy as jnp
from jax import lax
from jax.experimental import pallas as pl
from jax.experimental.pallas import tpu as pltpu
from jax.sharding import PartitionSpec as P

COARSE = 16
PAD = 8
DIRECT = 64

jacobi_weight = 2.0 / 3.0
MESH = pl.DeviceIdType.MESH


def kernel(
    dims,
    x0_in, src_in, diag_in, face_in, bc_in, map_in, inv_in,
    vel_ref, out_ref,
    x0_ref, src_ref, face_ref, bc_ref, map_ref, inv_ref,
    x0_late, rho_ref, rho_late, edge_ref,
    coef, res_ref, v_ref, vk_ref, a1_ref, a2_ref, a3_ref,
    code_ref, cell_ref, pd_ref, share_ref, q_ref, inv_side,
    msg, got, msg_z, got_z, msg_c, got_c,
    tally, sent, near_r, sum_sem, coarse_sem, load_sem, side_s, side_r,
):
    n_gx, n_gz, cx_n, cz_n, ny, lanes = dims
    rows = cx_n * cz_n
    deep = x0_ref.shape[2]
    gx = lax.axis_index("gx")
    gz = lax.axis_index("gz")
    east = (lax.rem(gx + 1, n_gx), gz)
    west = (lax.rem(gx + n_gx - 1, n_gx), gz)
    north = (gx, lax.rem(gz + 1, n_gz))
    south = (gx, lax.rem(gz + n_gz - 1, n_gz))
    row_x = [(lax.rem(gx + d, n_gx), gz) for d in range(1, n_gx)]
    row_z = [(gx, lax.rem(gz + d, n_gz)) for d in range(1, n_gz)]
    direct = n_gx * n_gz <= DIRECT

    def send(src, dst, ssem, rsem, to):
        copy = pltpu.make_async_remote_copy(
            src_ref=src, dst_ref=dst, send_sem=ssem, recv_sem=rsem,
            device_id=to, device_id_type=MESH,
        )
        copy.start()
        return copy

    def settle(sem, count):
        span = tally.at[pl.ds(0, count)]
        pltpu.make_async_copy(span, span, sem).wait()

    corners = [
        (east[0], north[1]), (east[0], south[1]), (west[0], north[1]), (west[0], south[1])
    ]

    def at(offset):
        return (lax.rem(gx + offset[0], n_gx), lax.rem(gz + offset[1], n_gz))

    def fold(d, k):
        return (d % n_gx, k % n_gz)

    around = {fold(d, k) for d in (-1, 0, 1) for k in (-1, 0, 1)} - {(0, 0)}
    spread_to = sorted({fold(d, k) for d in range(-2, 3) for k in range(n_gz)} - {(0, 0)})
    every = {(d, k) for d in range(n_gx) for k in range(n_gz)}
    if direct:
        sum_to = [
            (d, k)
            for k in sorted(range(n_gz), key=lambda k: -min(k, n_gz - k))
            for d in sorted(range(n_gx), key=lambda d: -min(d, n_gx - d))
            if d or k
        ]
        met = set(around)
        while True:
            seen = met | {fold(a + d, b + k) for a, b in around for d, k in met} | {(0, 0)}
            left = sorted(every - seen, key=lambda o: (min(o[1], n_gz - o[1]), o))
            if not left:
                break
            met |= {left[0], fold(-left[0][0], -left[0][1])}
        sum_to = [at(o) for o in sum_to]
    else:
        sum_to = row_x
        met = around | set(spread_to)
        met |= {(d, 0) for d in range(1, n_gx)} | {(0, k) for k in range(1, n_gz)}
    near_first = sorted(around, key=lambda o: (o[0] == 0) + (o[1] == 0) * 2)
    partners = [at(o) for o in near_first] + [at(o) for o in sorted(met - around)]

    def inner(ref, halo):
        return ref.at[..., pl.ds(halo, cx_n), pl.ds(0, cz_n), :]

    loads = [
        pltpu.make_async_copy(a, b, load_sem.at[max(0, i - 4)])
        for i, (a, b) in enumerate(
            [
                (x0_in, inner(x0_ref, 2)), (face_in, inner(face_ref.at[pl.ds(0, 3)], 3)),
                (diag_in, inner(face_ref.at[3], 3)), (src_in, src_ref),
                (map_in, map_ref), (bc_in, bc_ref), (inv_in, inv_ref),
            ]
        )
    ]
    barrier = pltpu.get_barrier_semaphore()
    for other in partners:
        pl.semaphore_signal(barrier, inc=1, device_id=other, device_id_type=MESH)
    for load in loads:
        load.start()
    settle(load_sem.at[0], 11 * rows)
    pl.semaphore_wait(barrier, len(partners))


    def side_x(sign, halo, a, b):
        if sign > 0:
            return pl.ds(halo + cx_n - b, b - a + 1), pl.ds(halo - b, b - a + 1)
        return pl.ds(halo + a - 1, b - a + 1), pl.ds(halo + cx_n + a - 1, b - a + 1)

    def side_z(sign, a, b):
        if sign > 0:
            return pl.ds(cz_n - b, b - a + 1), pl.ds(deep - b, b - a + 1)
        return pl.ds(a - 1, b - a + 1), pl.ds(cz_n + a - 1, b - a + 1)

    lots = []
    extra = []

    def ship(src, dst, to, where_from, where_to):
        target = dst.at[(..., *where_to, slice(None))]
        lots[-1] += math.prod(target.shape[:-1])
        i = len(lots) - 1
        send(src.at[(..., *where_from, slice(None))], target, sent.at[0], near_r.at[i], to)

    def arrive(i):
        settle(near_r.at[i], lots[i])

    def to_corners(src, dst, halo, n, land=None):
        land = halo if land is None else land
        for to, sx, sz in zip(corners, (1, 1, -1, -1), (1, -1, 1, -1)):
            fz, tz = side_z(sz, 1, n)
            ship(src, dst, to, (side_x(sx, halo, 1, n)[0], fz), (side_x(sx, land, 1, n)[1], tz))

    def to_z(src, dst, halo, a, b, ways=(1, -1), land=None, start=0, size=cx_n):
        land = halo if land is None else land
        for sz in ways:
            fz, tz = side_z(sz, a, b)
            where_from, where_to = (pl.ds(halo + start, size), fz), (pl.ds(land + start, size), tz)
            ship(src, dst, north if sz > 0 else south, where_from, where_to)

    def to_x(src, dst, halo, a, b, ways=(1, -1), land=None, start=0, size=cz_n):
        land = halo if land is None else land
        for sx in ways:
            fx, tx = side_x(sx, halo, a, b)[0], side_x(sx, land, a, b)[1]
            z = pl.ds(start, size)
            ship(src, dst, east if sx > 0 else west, (fx, z), (tx, z))

    both = pl.ds(0, 2)
    lots.append(0)
    to_corners(x0_ref, x0_ref, 2, 1)
    to_corners(face_ref.at[both], edge_ref, 3, 1, land=1)
    to_z(x0_ref, x0_ref, 2, 1, 1)
    to_z(face_ref.at[1], edge_ref.at[1], 3, 1, 1, (1,), land=1)
    to_z(face_ref.at[0], edge_ref.at[0], 3, 1, 1, land=1, start=cx_n - 1, size=1)
    to_x(x0_ref, x0_ref, 2, 1, 1)
    to_x(face_ref.at[0], edge_ref.at[0], 3, 1, 1, (1,), land=1)
    to_x(face_ref.at[1], edge_ref.at[1], 3, 1, 1, land=1, start=cz_n - 1, size=1)

    level = lax.broadcasted_iota(jnp.int32, (rows, ny), 1)
    bottom = level == 0
    top = level == ny - 1
    def y_prev(f):
        return pltpu.roll(f, 1, f.ndim - 1)

    def y_next(f):
        return pltpu.roll(f, ny - 1, f.ndim - 1)

    own_z = pl.ds(0, cz_n)
    own_x = pl.ds(3, cx_n)
    shelf = lax.broadcasted_iota(jnp.int32, (cz_n, ny), 0)
    ends = lax.broadcasted_iota(jnp.int32, (cz_n, ny), 1)
    cy = face_ref[2, own_x, own_z]
    rim = (ends == 0) | (ends == ny - 1)
    main = face_ref[3, own_x, own_z] + jnp.where(rim, jnp.broadcast_to(cy[..., ny - 1 :], cy.shape), 0.0)
    rise = jnp.where(ends == ny - 1, 0.0, cy)

    def within(f):
        none = jnp.zeros((1, cz_n, ny), jnp.float32)
        flux_x = face_ref[0, pl.ds(3, cx_n - 1), own_z] * (f[:-1] - f[1:])
        flux_x = jnp.concatenate([none, flux_x, none], 0)
        flux_z = face_ref[1, own_x, own_z] * (f - pltpu.roll(f, cz_n - 1, 1))
        flux_z = jnp.where(shelf == cz_n - 1, 0.0, flux_z)
        flux_y = rise * (f - y_next(f))
        total = main * f + (flux_x[1:] - flux_x[:-1])
        return total + (flux_z - pltpu.roll(flux_z, 1, 1)) + (flux_y - y_prev(flux_y))

    for c in range(3):
        rho_ref[c, pl.ds(1, cx_n), own_z] = src_ref[c] - within(x0_ref[c, pl.ds(2, cx_n), own_z])
    to_z(rho_ref, rho_ref, 1, 1, 1)
    to_x(rho_ref, rho_ref, 1, 1, 1)

    lots.append(0)
    to_corners(x0_ref, x0_late, 2, 2)
    to_corners(face_ref, face_ref, 3, 2)
    to_corners(rho_ref, rho_late, 1, 1, land=2)
    to_z(rho_ref, rho_late, 1, 2, 2, land=2)
    for x in (0, cx_n - 1):
        to_z(x0_ref, x0_late, 2, 2, 2, start=x, size=1)
    to_z(face_ref, face_ref, 3, 1, 2)
    to_z(face_ref.at[1], face_ref.at[1], 3, 3, 3, (1,))
    to_x(rho_ref, rho_late, 1, 2, 2, land=2)
    for z in (0, cz_n - 1):
        to_x(x0_ref, x0_late, 2, 2, 2, start=z, size=1)
    to_x(face_ref, face_ref, 3, 1, 2)
    to_x(face_ref.at[0], face_ref.at[0], 3, 3, 3, (1,))

    eye = lax.broadcasted_iota(jnp.int32, (cz_n, cz_n), 0) == lax.broadcasted_iota(
        jnp.int32, (cz_n, cz_n), 1
    )

    def column(side):
        flags = bc_ref[side]
        parts = [
            jnp.sum(
                jnp.where(eye, jnp.broadcast_to(flags[i : i + 1], (cz_n, cz_n)), 0),
                axis=1, keepdims=True,
            )
            for i in range(cx_n)
        ]
        return jnp.broadcast_to(jnp.concatenate(parts, 0), (rows, ny))

    def scatter(msg, got, sem, others):
        for d, to in enumerate(others):
            send(msg, got.at[d], sent.at[0], sem, to)
        extra.append(math.prod(got.shape) // ny)

    def gathered(msg, got, sem):
        pltpu.make_async_copy(got, got, sem).wait()
        return msg[...] + jnp.sum(got[...], axis=0)

    def z_roll(f, shift):
        flat = f.reshape((-1,) + f.shape[-2:])
        return pltpu.roll(flat, shift % deep, 1).reshape(f.shape)

    def apply(f):
        h = (f.shape[0] - cx_n) // 2 - 1
        n = cx_n + 2 * h
        g = f[1:-1]
        flux_x = face_ref[0, pl.ds(2 - h, n + 1)] * (f[:-1] - f[1:])
        flux_z = face_ref[1, pl.ds(3 - h, n)] * (g - z_roll(g, -1))
        flux_y = coef[1, pl.ds(2 - h, n)] * (g - y_next(g))
        total = coef[0, pl.ds(2 - h, n)] * g + (flux_x[1:] - flux_x[:-1])
        return total + (flux_z - z_roll(flux_z, 1)) + (flux_y - y_prev(flux_y))

    def own(f):
        h = (f.shape[0] - cx_n) // 2
        return f[h : h + cx_n, :cz_n].reshape(rows, ny)

    def pack(pairs):
        sums = [jnp.sum(a * b, axis=0, keepdims=True) for a, b in pairs]
        while len(sums) < 3 * PAD:
            sums.append(jnp.zeros_like(sums[0]))
        total = jnp.sum(jnp.concatenate(sums, 0), axis=1, keepdims=True)
        shape = (3 * PAD, 128)
        pick = lax.broadcasted_iota(jnp.int32, shape, 0) == lax.broadcasted_iota(
            jnp.int32, shape, 1
        )
        return jnp.sum(
            jnp.where(pick, jnp.broadcast_to(total, shape), 0.0), axis=0, keepdims=True
        )

    def sums_start(i, pairs):
        msg[i] = pack(pairs)
        scatter(msg.at[i], got.at[i], sum_sem.at[i, 0], sum_to)

    def sums_end(i, count):
        total = gathered(msg.at[i], got.at[i], sum_sem.at[i, 0])
        if not direct:
            msg_z[i] = total
            scatter(msg_z.at[i], got_z.at[i], sum_sem.at[i, 1], row_z)
            total = gathered(msg_z.at[i], got_z.at[i], sum_sem.at[i, 1])
        shape = (8, 128)
        place = lax.broadcasted_iota(jnp.int32, shape, 0) * PAD
        lane = lax.broadcasted_iota(jnp.int32, shape, 1)
        wide = jnp.broadcast_to(total, shape)
        return [
            jnp.broadcast_to(
                jnp.sum(jnp.where(lane == place + k, wide, 0.0), axis=1, keepdims=True), shape
            )
            for k in range(count)
        ]

    slot = lax.broadcasted_iota(jnp.int32, (deep, ny), 0)
    floor = lax.broadcasted_iota(jnp.int32, (deep, ny), 1) == 0
    lid = lax.broadcasted_iota(jnp.int32, (deep, ny), 1) == ny - 1
    for load in loads[5:]:
        load.wait()
    flag = jnp.where(bottom, column(0), 0) + jnp.where(top, column(1), 0)
    code = map_ref[...] + COARSE * flag
    code_ref[pl.ds(2, cx_n), pl.ds(0, cz_n)] = code.reshape(cx_n, cz_n, ny)

    lots.append(0)
    to_corners(code_ref, code_ref, 2, 1)
    to_z(code_ref, code_ref, 2, 1, 2)
    to_x(code_ref, code_ref, 2, 1, 2)
    for k, to in enumerate((east, west)):
        send(inv_ref, inv_side.at[k], side_s.at[0], side_r.at[0], to)

    arrive(0)

    def prepare(low, high):
        for x in range(low, high):
            cy = face_ref[2, x + 1]
            wall = jnp.where(floor | lid, jnp.broadcast_to(cy[:, ny - 1 :], (deep, ny)), 0.0)
            coef[0, x] = face_ref[3, x + 1] + wall
            coef[1, x] = jnp.where(lid, 0.0, cy)

    seam = (slot == cz_n - 1) | (slot == deep - 1)

    def mend(part, f, coef_w, coef_e, coef_z):
        flux_w, flux_e = coef_w * (f[0] - f[1]), coef_e * (f[-2] - f[-1])
        flux_z = jnp.where(seam, coef_z * (f - z_roll(f, -1)), 0.0)
        part = part - (flux_z - z_roll(flux_z, 1))
        return jnp.concatenate(
            [
                (part[0] - flux_w)[None], (part[1] + flux_w)[None], part[2:-2],
                (part[-2] - flux_e)[None], (part[-1] + flux_e)[None],
            ], 0,
        )

    tail = pl.ds(cz_n, 8)
    coef_w = edge_ref[0, 0]
    coef_e = jnp.concatenate([face_ref[0, cx_n + 2, own_z], edge_ref[0, cx_n, tail]], 0)
    coef_z = jnp.concatenate(
        [edge_ref[1, pl.ds(0, 1), own_z], face_ref[1, own_x, own_z], edge_ref[1, pl.ds(cx_n + 1, 1), own_z]], 0
    )
    coef_z = jnp.concatenate([coef_z, edge_ref[1, :, tail]], 1)
    dots = []
    for c in range(3):
        r = mend(rho_ref[c], x0_ref[c, pl.ds(1, cx_n + 2)], coef_w, coef_e, coef_z)
        r_own = own(r)
        v = jnp.concatenate([-within(r[1:-1, :cz_n]), jnp.zeros((cx_n, 8, ny), jnp.float32)], 1)
        none = jnp.zeros((1, deep, ny), jnp.float32)
        v = -mend(jnp.concatenate([none, v, none], 0), r, coef_w, coef_e, coef_z)
        v_own = own(v)
        vk_ref[c, pl.ds(3, cx_n), own_z] = v[1:-1, :cz_n]
        dots.append([(r_own, r_own), (r_own, v_own)])
    zero = jnp.zeros((8, ny), jnp.float32)
    sums_start(0, [p for d in dots for p in d + [(zero, zero)] * (PAD - 2)])
    lots.append(0)
    to_corners(vk_ref, vk_ref, 3, 2)
    to_z(vk_ref, vk_ref, 3, 2, 3)
    to_x(vk_ref, vk_ref, 3, 2, 3)

    arrive(1)
    prepare(0, cx_n + 4)
    mine = (slot <= cz_n) | (slot == deep - 1)
    body_rows = slot < cz_n

    def widen(near, far):
        n = near.shape[0] - 2
        mid = jnp.where(mine, near[1:-1], far[2:-2])
        low = jnp.where(body_rows, near[0], far[1])
        high = jnp.where(body_rows, near[n + 1], far[n + 2])
        return jnp.concatenate([far[:1], low[None], mid, high[None], far[-1:]], 0)

    coef_w, coef_e = face_ref[0, 2], face_ref[0, cx_n + 2]
    coef_z = face_ref[1, pl.ds(1, cx_n + 4)]
    for c in range(3):
        r = widen(rho_ref[c], rho_late[c])
        f = widen(x0_ref[c, pl.ds(1, cx_n + 2)], x0_late[c])
        flux_w, flux_e = coef_w * (f[1] - f[2]), coef_e * (f[-3] - f[-2])
        flux_z = jnp.where(seam, coef_z * (f - z_roll(f, -1)), 0.0)
        r = r - (flux_z - z_roll(flux_z, 1))
        r = jnp.concatenate(
            [
                r[:1], (r[1] - flux_w)[None], (r[2] + flux_w)[None], r[3:-3],
                (r[-3] - flux_e)[None], (r[-2] + flux_e)[None], r[-1:],
            ], 0,
        )
        res_ref[c] = r
        v_ref[c] = apply(r)

    arrive(3)
    m0, m1 = sums_end(0, 2)
    sigma = m1 / m0
    dots = []
    for c in range(3):
        s = sigma[c : c + 1]
        mid = jnp.where(mine, v_ref[c, pl.ds(1, cx_n)], vk_ref[c, pl.ds(3, cx_n)])
        low = jnp.where(body_rows, v_ref[c, 0], vk_ref[c, 2])
        high = jnp.where(body_rows, v_ref[c, cx_n + 1], vk_ref[c, cx_n + 3])
        v = jnp.concatenate(
            [vk_ref[c, pl.ds(0, 2)], low[None], mid, high[None], vk_ref[c, pl.ds(cx_n + 4, 2)]], 0
        )
        r = res_ref[c]
        u = apply(v)
        v = v[1:-1]
        a1 = v - s * r
        a2 = (u - s * v) - s * a1
        a3 = apply(a2) - s * a2[1:-1]
        a4 = apply(a3) - s * a3[1:-1]
        r0, b1, b2, b3, b4 = own(r), own(a1), own(a2), own(a3), own(a4)
        dots += [
            (r0, b1), (b1, b1), (b1, b2), (b2, b2), (b2, b3), (b3, b3), (b3, b4), (b4, b4)
        ]
        a1_ref[c] = a1[1:-1]
        a2_ref[c] = a2[1:-1]
        a3_ref[c] = a3
    sums_start(1, dots)
    arrive(2)
    for sem in (side_s, side_r):
        pltpu.make_async_copy(inv_side, inv_side, sem.at[0]).wait()
    for x in range(cx_n + 4):
        mark = code_ref[x] >= COARSE
        edge = floor | lid
        pd = jnp.where(edge, jnp.where(mark, 6.0, 5.0), 6.0)
        pd_ref[x] = pd
        share_ref[x] = jacobi_weight / pd
        cell_ref[x] = jnp.where(mark, code_ref[x] - COARSE, code_ref[x])
    mu = [m0] + sums_end(1, PAD)

    def times(p):
        out = [sigma * p[0]]
        for i in range(1, len(p)):
            out.append(p[i - 1] + sigma * p[i])
        return out + [p[-1]]

    def dot(p, q):
        total = 0.0
        for n in range(len(p) + len(q) - 1):
            terms = [p[i] * q[n - i] for i in range(len(p)) if 0 <= n - i < len(q)]
            total = total + sum(terms[1:], terms[0]) * mu[n]
        return total

    def against(p):
        return sum((p[i] * mu[i] for i in range(1, len(p))), p[0] * mu[0])

    alpha = m0 / (sigma * m0 + mu[1])
    s1 = [1.0 - alpha * sigma, -alpha]
    t1 = times(s1)
    omega = dot(s1, t1) / dot(t1, t1)
    rho_new = against(s1) - omega * against(t1)
    beta = (rho_new / m0) * (alpha / omega)
    r1 = [s1[0] - omega * t1[0], s1[1] - omega * t1[1], -omega * t1[2]]
    p2 = [r1[0] + beta * (1.0 - omega * sigma), r1[1] - beta * omega, r1[2]]
    v2 = times(p2)
    alpha2 = rho_new / against(v2)
    s2 = [r1[i] - alpha2 * v2[i] for i in range(3)] + [-alpha2 * v2[3]]
    t2 = times(s2)
    omega2 = dot(s2, t2) / dot(t2, t2)
    weight = [
        alpha + omega * s1[0] + alpha2 * p2[0] + omega2 * s2[0],
        omega * s1[1] + alpha2 * p2[1] + omega2 * s2[1],
        alpha2 * p2[2] + omega2 * s2[2],
        omega2 * s2[3],
    ]
    speed = []
    for c in range(3):
        w = [k[c : c + 1] for k in weight]
        field = x0_ref[c, pl.ds(1, cx_n + 2)] + w[0] * res_ref[c, pl.ds(1, cx_n + 2)]
        field += w[1] * a1_ref[c] + w[2] * a2_ref[c] + w[3] * a3_ref[c]
        vel_ref[c] = field[1:-1, :cz_n]
        speed.append(field)
    ux, uz, uy = speed
    div = (ux[1:-1] - ux[:-2]) + (uz[1:-1] - z_roll(uz[1:-1], 1))
    uy = uy[1:-1]
    div = div + (uy - jnp.where(floor, 0.0, y_prev(uy)))
    share = share_ref[pl.ds(2, cx_n)]
    q = share * div
    q_ref[pl.ds(3, cx_n), pl.ds(0, cz_n)] = q[:, :cz_n]
    lots.append(0)
    to_corners(q_ref, q_ref, 3, 2)
    to_z(q_ref, q_ref, 3, 1, 3)
    to_x(q_ref, q_ref, 3, 1, 3)

    def smooth(f):
        n = f.shape[0] - 2
        h = (n - cx_n) // 2
        g = f[1:-1]
        near = (f[2:] + f[:-2]) + (z_roll(g, 1) + z_roll(g, -1))
        near += jnp.where(lid, 0.0, y_next(g)) + jnp.where(floor, 0.0, y_prev(g))
        return pd_ref[pl.ds(2 - h, n)] * g - near

    def shares(h):
        return share_ref[pl.ds(2 - h, cx_n + 2 * h)]

    blank = jnp.zeros((2, deep, ny), jnp.float32)
    mine = jnp.where(body_rows, q, 0.0)
    first_cut = -smooth(jnp.concatenate([blank, mine, blank], 0))
    trace = jnp.concatenate(
        [first_cut[:1], first_cut[1:-1] + jnp.where(body_rows, div, 0.0), first_cut[-1:]], 0
    )
    full = jnp.concatenate([blank[:1], trace, blank[:1]], 0)
    full = full - smooth(jnp.concatenate([blank, shares(1) * trace, blank], 0))

    part = [[] for _ in range(6)]
    for m in range(COARSE):
        hit = jnp.where(cell_ref[...] == m, full, 0.0)
        flat = hit[:, :cz_n].reshape(-1, 8, ny)
        step = cz_n // 8
        top_rows = hit[:, cz_n:]
        part[0].append(jnp.sum(flat[: 2 * step], axis=0, keepdims=True))
        part[1].append(jnp.sum(flat[2 * step : -2 * step], axis=0, keepdims=True))
        part[2].append(jnp.sum(flat[-2 * step :], axis=0, keepdims=True))
        part[3].append(top_rows[1:2])
        part[4].append(jnp.sum(top_rows[2:-2], axis=0, keepdims=True))
        part[5].append(top_rows[-2:-1])
    part = [jnp.concatenate(p, 0) for p in part]
    upper_half = lax.broadcasted_iota(jnp.int32, (COARSE, 8, ny), 1) < 4

    def total_of(p):
        return jnp.sum(jnp.sum(p, axis=1), axis=1, keepdims=True)

    shape = (COARSE, lanes)
    spots = (south[1], gz, north[1])
    places = [
        lax.broadcasted_iota(jnp.int32, shape, 1)
        == lax.broadcasted_iota(jnp.int32, shape, 0) + spot * COARSE
        for spot in spots
    ]
    for k in range(3):
        cols = [
            total_of(jnp.where(upper_half, 0.0, part[3 + k])), total_of(part[k]),
            total_of(jnp.where(upper_half, part[3 + k], 0.0)),
        ]
        line = sum(
            jnp.where(place, jnp.broadcast_to(col, shape), 0.0)
            for place, col in zip(places, cols)
        )
        msg_c[k] = jnp.sum(line, axis=0, keepdims=True)
    scatter(msg_c, got_c, coarse_sem.at[0], [at(o) for o in spread_to])

    arrive(4)
    ext = q_ref[...]
    q = 2.0 * ext[1:-1] - shares(2) * smooth(ext)
    q = q[1:-1] + ext[2:-2] - shares(1) * smooth(q)
    q = q[1:-1] + ext[3:-3] - shares(0) * smooth(q)

    pltpu.make_async_copy(got_c, got_c, coarse_sem.at[0]).wait()
    settle(sent.at[0], sum(lots) + sum(extra))

    def restricted(t):
        rows_in = [
            got_c[spread_to.index(fold(-j, k)), t - j + 1]
            for j in (t - 1, t, t + 1) for k in range(n_gz) if fold(-j, k) != (0, 0)
        ]
        return sum(rows_in, msg_c[t + 1])

    def corrections(inv, coarse):
        out = []
        for spot in spots:
            block = inv[pl.ds(pl.multiple_of(spot * COARSE, COARSE), COARSE), :]
            col = jnp.sum(block * coarse[:, : block.shape[1]], axis=1, keepdims=True)
            out.append(jnp.broadcast_to(col, (COARSE, ny)))
        return out

    def lift(cell, table):
        flat = cell.reshape(-1, 8, ny)
        picked = []
        for t in range(flat.shape[0]):
            index = flat[t]
            low = jnp.bitwise_and(index, 7)
            value = jnp.take_along_axis(table[:8], low, axis=0)
            for m in range(8, COARSE, 8):
                value = jnp.where(index >= m, jnp.take_along_axis(table[m : m + 8], low, axis=0), value)
            picked.append(value[None])
        return jnp.concatenate(picked, 0).reshape(cell.shape)

    corr = [corrections(inv, restricted(t)) for inv, t in zip((inv_side.at[0], inv_ref, inv_side.at[1]), (-1, 0, 1))]
    half = lax.broadcasted_iota(jnp.int32, (8, ny), 0) < 4
    spans = (pl.ds(0, 2), pl.ds(2, cx_n), pl.ds(cx_n + 2, 2))
    raised = []
    for k in range(3):
        cell = cell_ref[spans[k]]
        inside = lift(cell[:, :cz_n], corr[k][1])
        outside = jnp.where(
            half, lift(cell[:, cz_n:], corr[k][2]), lift(cell[:, cz_n:], corr[k][0])
        )
        raised.append(jnp.concatenate([inside, outside], 1))
    e = jnp.concatenate(raised, 0)
    e = e[1:-1] - shares(1) * smooth(e)
    e = e[1:-1] - shares(0) * smooth(e)
    out_ref[...] = (q + e)[:, :cz_n]


def put(a_ref, b_ref, a_out, b_out, sem):
    copies = [
        pltpu.make_async_copy(a_ref, a_out, sem.at[0]), pltpu.make_async_copy(b_ref, b_out, sem.at[1])
    ]
    for copy in copies:
        copy.start()
    for copy in copies:
        copy.wait()


def body(n_gx, n_gz, velocity_old, source, diag_coef, face_coef, bc_flags, coarse_map, coarse_inverse):
    cx_n, cz_n, ny = diag_coef.shape
    rows = cx_n * cz_n
    deep = cz_n + 8
    group = coarse_inverse.shape[1]
    lanes = -(-group // 128) * 128
    f32 = jnp.float32
    vmem = pltpu.VMEM
    dma = pltpu.SemaphoreType.DMA
    n_spread = min(5, n_gx) * n_gz - 1
    n_sum = n_gx * n_gz - 1 if n_gx * n_gz <= DIRECT else n_gx - 1

    def block(fields, halo):
        return vmem((fields, cx_n + 2 * halo, deep, ny), f32)

    scratch = [
        block(3, 2),
        vmem((3, cx_n, cz_n, ny), f32),
        block(4, 3),
        vmem(bc_flags.shape, jnp.int32),
        vmem((rows, ny), jnp.int32),
        vmem(coarse_inverse.shape, f32),
        block(3, 2),
        block(3, 1),
        block(3, 2),
        block(2, 1),
        block(2, 2),
        block(3, 2),
        block(3, 1),
        block(3, 3),
        block(3, 1),
        block(3, 1),
        block(3, 1),
        vmem((cx_n + 4, deep, ny), jnp.int32),
        vmem((cx_n + 4, deep, ny), jnp.int32),
        vmem((cx_n + 4, deep, ny), f32),
        vmem((cx_n + 4, deep, ny), f32),
        vmem((cx_n + 6, deep, ny), f32),
        vmem((2,) + coarse_inverse.shape, f32),
        vmem((2, 1, 128), f32),
        vmem((2, n_sum, 1, 128), f32),
        vmem((2, 1, 128), f32),
        vmem((2, n_gz - 1, 1, 128), f32),
        vmem((3, 1, lanes), f32),
        vmem((n_spread, 3, 1, lanes), f32),
        vmem((4096, ny), f32),
        dma((1,)),
        dma((5,)),
        dma((2, 2) if n_sum < n_gx * n_gz - 1 else (2, 1)),
        dma((1,)),
        dma((3,)),
        dma((1,)),
        dma((1,)),
    ]
    spec = pl.BlockSpec(memory_space=pltpu.VMEM)
    velocity, pressure = pl.pallas_call(
        functools.partial(kernel, (n_gx, n_gz, cx_n, cz_n, ny, lanes)),
        out_shape=(
            jax.ShapeDtypeStruct((3, cx_n, cz_n, ny), f32),
            jax.ShapeDtypeStruct((cx_n, cz_n, ny), f32),
        ),
        in_specs=[pl.BlockSpec(memory_space=pltpu.HBM)] * 7,
        out_specs=(spec, spec),
        scratch_shapes=scratch,
        compiler_params=pltpu.CompilerParams(
            collective_id=0, has_side_effects=True, vmem_limit_bytes=48 * 1024 * 1024
        ),
        name="corrector",
    )(
        *[
            pltpu.with_memory_space_constraint(a, pltpu.HBM)
            for a in (
                velocity_old,
                source,
                diag_coef,
                face_coef,
                bc_flags,
                coarse_map.reshape(rows, ny),
                coarse_inverse,
            )
        ]
    )
    velocity, pressure = pl.pallas_call(
        put,
        out_shape=(
            jax.ShapeDtypeStruct(velocity.shape, f32),
            jax.ShapeDtypeStruct(pressure.shape, f32),
        ),
        in_specs=[spec, spec],
        out_specs=[pl.BlockSpec(memory_space=pltpu.HBM)] * 2,
        scratch_shapes=[dma((2,))],
        name="put",
    )(*[pltpu.with_memory_space_constraint(a, pltpu.VMEM) for a in (velocity, pressure)])
    return velocity, pressure


def solution(mesh):
    placed = (
        P(None, "gx", "gz", None),
        P(None, "gx", "gz", None),
        P("gx", "gz", None),
        P(None, "gx", "gz", None),
        P(None, "gx", "gz"),
        P("gx", "gz", None),
        P("gx", None),
    )
    return jax.shard_map(
        functools.partial(body, mesh.shape["gx"], mesh.shape["gz"]),
        mesh=mesh,
        in_specs=placed,
        out_specs=(P(None, "gx", "gz", None), P("gx", "gz", None)),
        check_vma=False,
    )
```

```python
import functools
import math

import jax
import jax.numpy as jnp
from jax import lax
from jax.experimental import pallas as pl
from jax.experimental.pallas import tpu as pltpu
from jax.sharding import PartitionSpec as P

COARSE = 16
PAD = 8
DIRECT = 64

jacobi_weight = 2.0 / 3.0
MESH = pl.DeviceIdType.MESH


def kernel(
    dims,
    x0_in, src_in, diag_in, face_in, bc_in, map_in, inv_in,
    vel_ref, out_ref,
    x0_ref, src_ref, face_ref, bc_ref, map_ref, inv_ref,
    x0_late, rho_ref, rho_late, edge_ref,
    coef, res_ref, v_ref, vk_ref, a1_ref, a2_ref, a3_ref,
    code_ref, cell_ref, pd_ref, share_ref, q_ref, inv_side,
    msg, got, msg_z, got_z, msg_c, got_c,
    tally, sent, near_r, sum_sem, coarse_sem, load_sem, side_s, side_r,
):
    n_gx, n_gz, cx_n, cz_n, ny, lanes = dims
    rows = cx_n * cz_n
    deep = x0_ref.shape[2]
    gx = lax.axis_index("gx")
    gz = lax.axis_index("gz")
    east = (lax.rem(gx + 1, n_gx), gz)
    west = (lax.rem(gx + n_gx - 1, n_gx), gz)
    north = (gx, lax.rem(gz + 1, n_gz))
    south = (gx, lax.rem(gz + n_gz - 1, n_gz))
    row_x = [(lax.rem(gx + d, n_gx), gz) for d in range(1, n_gx)]
    row_z = [(gx, lax.rem(gz + d, n_gz)) for d in range(1, n_gz)]
    direct = n_gx * n_gz <= DIRECT

    def send(src, dst, ssem, rsem, to):
        copy = pltpu.make_async_remote_copy(
            src_ref=src, dst_ref=dst, send_sem=ssem, recv_sem=rsem,
            device_id=to, device_id_type=MESH,
        )
        copy.start()
        return copy

    def settle(sem, count):
        span = tally.at[pl.ds(0, count)]
        pltpu.make_async_copy(span, span, sem).wait()

    corners = [
        (east[0], north[1]), (east[0], south[1]), (west[0], north[1]), (west[0], south[1])
    ]

    def at(offset):
        return (lax.rem(gx + offset[0], n_gx), lax.rem(gz + offset[1], n_gz))

    def fold(d, k):
        return (d % n_gx, k % n_gz)

    around = {fold(d, k) for d in (-1, 0, 1) for k in (-1, 0, 1)} - {(0, 0)}
    spread_to = sorted({fold(d, k) for d in range(-2, 3) for k in range(n_gz)} - {(0, 0)}, key=lambda o: (o[1] == 0, min(o[1], n_gz - o[1]), -min(o[0], n_gx - o[0])))
    every = {(d, k) for d in range(n_gx) for k in range(n_gz)}
    if direct:
        sum_to = [
            (d, k)
            for k in sorted(range(n_gz), key=lambda k: (k == 0, min(k, n_gz - k)))
            for d in sorted(range(n_gx), key=lambda d: (d == 0, d % 4 == 0, d % 2))
            if d or k
        ]
        met = set(around)

        def known(extra):
            reach = met | extra
            return reach | {fold(a + d, b + k) for a, b in around for d, k in reach} | {(0, 0)}

        while every - known(set()):
            pairs = [{o, fold(-o[0], -o[1])} for o in sorted(every - met - {(0, 0)})]
            gain = len(known(set()))
            met |= max(pairs, key=lambda p: (len(known(p)) - gain) / len(p))
        sum_to = [at(o) for o in sum_to]
    else:
        sum_to = row_x
        met = around | set(spread_to)
        met |= {(d, 0) for d in range(1, n_gx)} | {(0, k) for k in range(1, n_gz)}
    near_first = sorted(around, key=lambda o: (o[0] == 0) + (o[1] == 0) * 2)
    partners = [at(o) for o in near_first] + [at(o) for o in sorted(met - around)]

    def inner(ref, halo):
        return ref.at[..., pl.ds(halo, cx_n), pl.ds(0, cz_n), :]

    loads = [
        pltpu.make_async_copy(a, b, load_sem.at[max(0, i - 4)])
        for i, (a, b) in enumerate(
            [
                (x0_in, inner(x0_ref, 2)), (face_in, inner(face_ref.at[pl.ds(0, 3)], 3)),
                (diag_in, inner(face_ref.at[3], 3)), (src_in, src_ref),
                (map_in, map_ref), (bc_in, bc_ref), (inv_in, inv_ref),
            ]
        )
    ]
    barrier = pltpu.get_barrier_semaphore()
    for other in partners:
        pl.semaphore_signal(barrier, inc=1, device_id=other, device_id_type=MESH)
    for load in loads:
        load.start()
    settle(load_sem.at[0], 11 * rows)
    pl.semaphore_wait(barrier, len(partners))


    def side_x(sign, halo, a, b):
        if sign > 0:
            return pl.ds(halo + cx_n - b, b - a + 1), pl.ds(halo - b, b - a + 1)
        return pl.ds(halo + a - 1, b - a + 1), pl.ds(halo + cx_n + a - 1, b - a + 1)

    def side_z(sign, a, b):
        if sign > 0:
            return pl.ds(cz_n - b, b - a + 1), pl.ds(deep - b, b - a + 1)
        return pl.ds(a - 1, b - a + 1), pl.ds(cz_n + a - 1, b - a + 1)

    lots = []
    extra = []

    def ship(src, dst, to, where_from, where_to):
        target = dst.at[(..., *where_to, slice(None))]
        lots[-1] += math.prod(target.shape[:-1])
        i = len(lots) - 1
        send(src.at[(..., *where_from, slice(None))], target, sent.at[0], near_r.at[i], to)

    def arrive(i):
        settle(near_r.at[i], lots[i])

    def to_corners(src, dst, halo, n, land=None):
        land = halo if land is None else land
        for to, sx, sz in zip(corners, (1, 1, -1, -1), (1, -1, 1, -1)):
            fz, tz = side_z(sz, 1, n)
            ship(src, dst, to, (side_x(sx, halo, 1, n)[0], fz), (side_x(sx, land, 1, n)[1], tz))

    def to_z(src, dst, halo, a, b, ways=(1, -1), land=None, start=0, size=cx_n):
        land = halo if land is None else land
        for sz in ways:
            fz, tz = side_z(sz, a, b)
            where_from, where_to = (pl.ds(halo + start, size), fz), (pl.ds(land + start, size), tz)
            ship(src, dst, north if sz > 0 else south, where_from, where_to)

    def to_x(src, dst, halo, a, b, ways=(1, -1), land=None, start=0, size=cz_n):
        land = halo if land is None else land
        for sx in ways:
            fx, tx = side_x(sx, halo, a, b)[0], side_x(sx, land, a, b)[1]
            z = pl.ds(start, size)
            ship(src, dst, east if sx > 0 else west, (fx, z), (tx, z))

    both = pl.ds(0, 2)
    lots.append(0)
    to_corners(x0_ref, x0_ref, 2, 1)
    to_corners(face_ref.at[both], edge_ref, 3, 1, land=1)
    to_z(x0_ref, x0_ref, 2, 1, 1)
    to_z(face_ref.at[1], edge_ref.at[1], 3, 1, 1, (1,), land=1)
    to_z(face_ref.at[0], edge_ref.at[0], 3, 1, 1, land=1, start=cx_n - 1, size=1)
    to_x(x0_ref, x0_ref, 2, 1, 1)
    to_x(face_ref.at[0], edge_ref.at[0], 3, 1, 1, (1,), land=1)
    to_x(face_ref.at[1], edge_ref.at[1], 3, 1, 1, land=1, start=cz_n - 1, size=1)

    level = lax.broadcasted_iota(jnp.int32, (rows, ny), 1)
    bottom = level == 0
    top = level == ny - 1
    def y_prev(f):
        return pltpu.roll(f, 1, f.ndim - 1)

    def y_next(f):
        return pltpu.roll(f, ny - 1, f.ndim - 1)

    own_z = pl.ds(0, cz_n)
    own_x = pl.ds(3, cx_n)
    shelf = lax.broadcasted_iota(jnp.int32, (cz_n, ny), 0)
    ends = lax.broadcasted_iota(jnp.int32, (cz_n, ny), 1)
    cy = face_ref[2, own_x, own_z]
    rim = (ends == 0) | (ends == ny - 1)
    main = face_ref[3, own_x, own_z] + jnp.where(rim, jnp.broadcast_to(cy[..., ny - 1 :], cy.shape), 0.0)
    rise = jnp.where(ends == ny - 1, 0.0, cy)

    def within(f):
        none = jnp.zeros((1, cz_n, ny), jnp.float32)
        flux_x = face_ref[0, pl.ds(3, cx_n - 1), own_z] * (f[:-1] - f[1:])
        flux_x = jnp.concatenate([none, flux_x, none], 0)
        flux_z = face_ref[1, own_x, own_z] * (f - pltpu.roll(f, cz_n - 1, 1))
        flux_z = jnp.where(shelf == cz_n - 1, 0.0, flux_z)
        flux_y = rise * (f - y_next(f))
        total = main * f + (flux_x[1:] - flux_x[:-1])
        return total + (flux_z - pltpu.roll(flux_z, 1, 1)) + (flux_y - y_prev(flux_y))

    for c in range(3):
        rho_ref[c, pl.ds(1, cx_n), own_z] = src_ref[c] - within(x0_ref[c, pl.ds(2, cx_n), own_z])
    to_z(rho_ref, rho_ref, 1, 1, 1)
    to_x(rho_ref, rho_ref, 1, 1, 1)

    lots.append(0)
    to_corners(x0_ref, x0_late, 2, 2)
    to_corners(face_ref, face_ref, 3, 2)
    to_corners(rho_ref, rho_late, 1, 1, land=2)
    to_z(rho_ref, rho_late, 1, 2, 2, land=2)
    for x in (0, cx_n - 1):
        to_z(x0_ref, x0_late, 2, 2, 2, start=x, size=1)
    to_z(face_ref, face_ref, 3, 1, 2)
    to_z(face_ref.at[1], face_ref.at[1], 3, 3, 3, (1,))
    to_x(rho_ref, rho_late, 1, 2, 2, land=2)
    for z in (0, cz_n - 1):
        to_x(x0_ref, x0_late, 2, 2, 2, start=z, size=1)
    to_x(face_ref, face_ref, 3, 1, 2)
    to_x(face_ref.at[0], face_ref.at[0], 3, 3, 3, (1,))

    eye = lax.broadcasted_iota(jnp.int32, (cz_n, cz_n), 0) == lax.broadcasted_iota(
        jnp.int32, (cz_n, cz_n), 1
    )

    def column(side):
        flags = bc_ref[side]
        parts = [
            jnp.sum(
                jnp.where(eye, jnp.broadcast_to(flags[i : i + 1], (cz_n, cz_n)), 0),
                axis=1, keepdims=True,
            )
            for i in range(cx_n)
        ]
        return jnp.broadcast_to(jnp.concatenate(parts, 0), (rows, ny))

    def scatter(msg, got, sem, others):
        for d, to in enumerate(others):
            send(msg, got.at[d], sent.at[0], sem, to)
        extra.append(math.prod(got.shape) // ny)

    def gathered(msg, got, sem):
        pltpu.make_async_copy(got, got, sem).wait()
        return msg[...] + jnp.sum(got[...], axis=0)

    def z_roll(f, shift):
        flat = f.reshape((-1,) + f.shape[-2:])
        return pltpu.roll(flat, shift % deep, 1).reshape(f.shape)

    def apply(f):
        h = (f.shape[0] - cx_n) // 2 - 1
        n = cx_n + 2 * h
        g = f[1:-1]
        flux_x = face_ref[0, pl.ds(2 - h, n + 1)] * (f[:-1] - f[1:])
        flux_z = face_ref[1, pl.ds(3 - h, n)] * (g - z_roll(g, -1))
        flux_y = coef[1, pl.ds(2 - h, n)] * (g - y_next(g))
        total = coef[0, pl.ds(2 - h, n)] * g + (flux_x[1:] - flux_x[:-1])
        return total + (flux_z - z_roll(flux_z, 1)) + (flux_y - y_prev(flux_y))

    def own(f):
        h = (f.shape[0] - cx_n) // 2
        return f[h : h + cx_n, :cz_n].reshape(rows, ny)

    def products(fields, pairs):
        sums = [None] * len(pairs)
        for p in range(0, rows, 8):
            tile = [f[p : p + 8] for f in fields]
            for k, (a, b) in enumerate(pairs):
                term = tile[a] * tile[b]
                sums[k] = term if sums[k] is None else sums[k] + term
        return sums

    def pack(sums):
        sums = [jnp.sum(s, axis=0, keepdims=True) for s in sums]
        while len(sums) < 3 * PAD:
            sums.append(jnp.zeros_like(sums[0]))
        total = jnp.sum(jnp.concatenate(sums, 0), axis=1, keepdims=True)
        shape = (3 * PAD, 128)
        pick = lax.broadcasted_iota(jnp.int32, shape, 0) == lax.broadcasted_iota(
            jnp.int32, shape, 1
        )
        return jnp.sum(
            jnp.where(pick, jnp.broadcast_to(total, shape), 0.0), axis=0, keepdims=True
        )

    def sums_start(i, pairs):
        msg[i] = pack(pairs)
        scatter(msg.at[i], got.at[i], sum_sem.at[i, 0], sum_to)

    def sums_end(i, count):
        total = gathered(msg.at[i], got.at[i], sum_sem.at[i, 0])
        if not direct:
            msg_z[i] = total
            scatter(msg_z.at[i], got_z.at[i], sum_sem.at[i, 1], row_z)
            total = gathered(msg_z.at[i], got_z.at[i], sum_sem.at[i, 1])
        shape = (8, 128)
        place = lax.broadcasted_iota(jnp.int32, shape, 0) * PAD
        lane = lax.broadcasted_iota(jnp.int32, shape, 1)
        wide = jnp.broadcast_to(total, shape)
        return [
            jnp.broadcast_to(
                jnp.sum(jnp.where(lane == place + k, wide, 0.0), axis=1, keepdims=True), shape
            )
            for k in range(count)
        ]

    slot = lax.broadcasted_iota(jnp.int32, (deep, ny), 0)
    floor = lax.broadcasted_iota(jnp.int32, (deep, ny), 1) == 0
    lid = lax.broadcasted_iota(jnp.int32, (deep, ny), 1) == ny - 1
    for load in loads[5:]:
        load.wait()
    flag = jnp.where(bottom, column(0), 0) + jnp.where(top, column(1), 0)
    code = map_ref[...] + COARSE * flag
    code_ref[pl.ds(2, cx_n), pl.ds(0, cz_n)] = code.reshape(cx_n, cz_n, ny)

    lots.append(0)
    to_corners(code_ref, code_ref, 2, 1)
    to_z(code_ref, code_ref, 2, 1, 2)
    to_x(code_ref, code_ref, 2, 1, 2)
    for k, to in enumerate((east, west)):
        send(inv_ref, inv_side.at[k], side_s.at[0], side_r.at[0], to)

    arrive(0)

    def prepare(low, high):
        for x in range(low, high):
            cy = face_ref[2, x + 1]
            wall = jnp.where(floor | lid, jnp.broadcast_to(cy[:, ny - 1 :], (deep, ny)), 0.0)
            coef[0, x] = face_ref[3, x + 1] + wall
            coef[1, x] = jnp.where(lid, 0.0, cy)

    seam = (slot == cz_n - 1) | (slot == deep - 1)

    def mend(part, f, coef_w, coef_e, coef_z):
        flux_w, flux_e = coef_w * (f[0] - f[1]), coef_e * (f[-2] - f[-1])
        flux_z = jnp.where(seam, coef_z * (f - z_roll(f, -1)), 0.0)
        part = part - (flux_z - z_roll(flux_z, 1))
        return jnp.concatenate(
            [
                (part[0] - flux_w)[None], (part[1] + flux_w)[None], part[2:-2],
                (part[-2] - flux_e)[None], (part[-1] + flux_e)[None],
            ], 0,
        )

    tail = pl.ds(cz_n, 8)
    coef_w = edge_ref[0, 0]
    coef_e = jnp.concatenate([face_ref[0, cx_n + 2, own_z], edge_ref[0, cx_n, tail]], 0)
    coef_z = jnp.concatenate(
        [edge_ref[1, pl.ds(0, 1), own_z], face_ref[1, own_x, own_z], edge_ref[1, pl.ds(cx_n + 1, 1), own_z]], 0
    )
    coef_z = jnp.concatenate([coef_z, edge_ref[1, :, tail]], 1)
    zero = jnp.zeros((8, ny), jnp.float32)
    dots = []
    for c in range(3):
        r = mend(rho_ref[c], x0_ref[c, pl.ds(1, cx_n + 2)], coef_w, coef_e, coef_z)
        r_own = own(r)
        v = jnp.concatenate([-within(r[1:-1, :cz_n]), jnp.zeros((cx_n, 8, ny), jnp.float32)], 1)
        none = jnp.zeros((1, deep, ny), jnp.float32)
        v = -mend(jnp.concatenate([none, v, none], 0), r, coef_w, coef_e, coef_z)
        v_own = own(v)
        vk_ref[c, pl.ds(3, cx_n), own_z] = v[1:-1, :cz_n]
        dots += products([r_own, v_own], [(0, 0), (0, 1)]) + [zero] * (PAD - 2)
    sums_start(0, dots)
    lots.append(0)
    to_corners(vk_ref, vk_ref, 3, 2)
    to_z(vk_ref, vk_ref, 3, 2, 3)
    to_x(vk_ref, vk_ref, 3, 2, 3)

    arrive(1)
    prepare(0, cx_n + 4)
    mine = (slot <= cz_n) | (slot == deep - 1)
    body_rows = slot < cz_n

    def widen(near, far):
        n = near.shape[0] - 2
        mid = jnp.where(mine, near[1:-1], far[2:-2])
        low = jnp.where(body_rows, near[0], far[1])
        high = jnp.where(body_rows, near[n + 1], far[n + 2])
        return jnp.concatenate([far[:1], low[None], mid, high[None], far[-1:]], 0)

    coef_w, coef_e = face_ref[0, 2], face_ref[0, cx_n + 2]
    coef_z = face_ref[1, pl.ds(1, cx_n + 4)]
    for c in range(3):
        r = widen(rho_ref[c], rho_late[c])
        f = widen(x0_ref[c, pl.ds(1, cx_n + 2)], x0_late[c])
        flux_w, flux_e = coef_w * (f[1] - f[2]), coef_e * (f[-3] - f[-2])
        flux_z = jnp.where(seam, coef_z * (f - z_roll(f, -1)), 0.0)
        r = r - (flux_z - z_roll(flux_z, 1))
        r = jnp.concatenate(
            [
                r[:1], (r[1] - flux_w)[None], (r[2] + flux_w)[None], r[3:-3],
                (r[-3] - flux_e)[None], (r[-2] + flux_e)[None], r[-1:],
            ], 0,
        )
        res_ref[c] = r
        v_ref[c] = apply(r)

    arrive(3)
    m0, m1 = sums_end(0, 2)
    sigma = m1 / m0
    dots = []
    for c in range(3):
        s = sigma[c : c + 1]
        mid = jnp.where(mine, v_ref[c, pl.ds(1, cx_n)], vk_ref[c, pl.ds(3, cx_n)])
        low = jnp.where(body_rows, v_ref[c, 0], vk_ref[c, 2])
        high = jnp.where(body_rows, v_ref[c, cx_n + 1], vk_ref[c, cx_n + 3])
        v = jnp.concatenate(
            [vk_ref[c, pl.ds(0, 2)], low[None], mid, high[None], vk_ref[c, pl.ds(cx_n + 4, 2)]], 0
        )
        r = res_ref[c]
        u = apply(v)
        v = v[1:-1]
        a1 = v - s * r
        a2 = (u - s * v) - s * a1
        a3 = apply(a2) - s * a2[1:-1]
        a4 = apply(a3) - s * a3[1:-1]
        dots += products(
            [own(r), own(a1), own(a2), own(a3), own(a4)],
            [(0, 1), (1, 1), (1, 2), (2, 2), (2, 3), (3, 3), (3, 4), (4, 4)],
        )
        a1_ref[c] = a1[1:-1]
        a2_ref[c] = a2[1:-1]
        a3_ref[c] = a3
    sums_start(1, dots)
    arrive(2)
    for sem in (side_s, side_r):
        pltpu.make_async_copy(inv_side, inv_side, sem.at[0]).wait()
    for x in range(cx_n + 4):
        mark = code_ref[x] >= COARSE
        edge = floor | lid
        pd = jnp.where(edge, jnp.where(mark, 6.0, 5.0), 6.0)
        pd_ref[x] = pd
        share_ref[x] = jacobi_weight / pd
        cell_ref[x] = jnp.where(mark, code_ref[x] - COARSE, code_ref[x])
    mu = [m0] + sums_end(1, PAD)

    def times(p):
        out = [sigma * p[0]]
        for i in range(1, len(p)):
            out.append(p[i - 1] + sigma * p[i])
        return out + [p[-1]]

    def dot(p, q):
        total = 0.0
        for n in range(len(p) + len(q) - 1):
            terms = [p[i] * q[n - i] for i in range(len(p)) if 0 <= n - i < len(q)]
            total = total + sum(terms[1:], terms[0]) * mu[n]
        return total

    def against(p):
        return sum((p[i] * mu[i] for i in range(1, len(p))), p[0] * mu[0])

    alpha = m0 / (sigma * m0 + mu[1])
    s1 = [1.0 - alpha * sigma, -alpha]
    t1 = times(s1)
    omega = dot(s1, t1) / dot(t1, t1)
    rho_new = against(s1) - omega * against(t1)
    beta = (rho_new / m0) * (alpha / omega)
    r1 = [s1[0] - omega * t1[0], s1[1] - omega * t1[1], -omega * t1[2]]
    p2 = [r1[0] + beta * (1.0 - omega * sigma), r1[1] - beta * omega, r1[2]]
    v2 = times(p2)
    alpha2 = rho_new / against(v2)
    s2 = [r1[i] - alpha2 * v2[i] for i in range(3)] + [-alpha2 * v2[3]]
    t2 = times(s2)
    omega2 = dot(s2, t2) / dot(t2, t2)
    weight = [
        alpha + omega * s1[0] + alpha2 * p2[0] + omega2 * s2[0],
        omega * s1[1] + alpha2 * p2[1] + omega2 * s2[1],
        alpha2 * p2[2] + omega2 * s2[2],
        omega2 * s2[3],
    ]
    speed = []
    for c in range(3):
        w = [k[c : c + 1] for k in weight]
        field = x0_ref[c, pl.ds(1, cx_n + 2)] + w[0] * res_ref[c, pl.ds(1, cx_n + 2)]
        field += w[1] * a1_ref[c] + w[2] * a2_ref[c] + w[3] * a3_ref[c]
        vel_ref[c] = field[1:-1, :cz_n]
        speed.append(field)
    ux, uz, uy = speed
    div = (ux[1:-1] - ux[:-2]) + (uz[1:-1] - z_roll(uz[1:-1], 1))
    uy = uy[1:-1]
    div = div + (uy - jnp.where(floor, 0.0, y_prev(uy)))
    share = share_ref[pl.ds(2, cx_n)]
    q = share * div
    q_ref[pl.ds(3, cx_n), pl.ds(0, cz_n)] = q[:, :cz_n]
    lots.append(0)
    to_corners(q_ref, q_ref, 3, 2)
    to_z(q_ref, q_ref, 3, 1, 3)
    to_x(q_ref, q_ref, 3, 1, 3)

    def smooth(f):
        n = f.shape[0] - 2
        h = (n - cx_n) // 2
        g = f[1:-1]
        near = (f[2:] + f[:-2]) + (z_roll(g, 1) + z_roll(g, -1))
        near += jnp.where(lid, 0.0, y_next(g)) + jnp.where(floor, 0.0, y_prev(g))
        return pd_ref[pl.ds(2 - h, n)] * g - near

    def shares(h):
        return share_ref[pl.ds(2 - h, cx_n + 2 * h)]

    blank = jnp.zeros((2, deep, ny), jnp.float32)
    mine = jnp.where(body_rows, q, 0.0)
    first_cut = -smooth(jnp.concatenate([blank, mine, blank], 0))
    trace = jnp.concatenate(
        [first_cut[:1], first_cut[1:-1] + jnp.where(body_rows, div, 0.0), first_cut[-1:]], 0
    )
    full = jnp.concatenate([blank[:1], trace, blank[:1]], 0)
    full = full - smooth(jnp.concatenate([blank, shares(1) * trace, blank], 0))

    part = [[] for _ in range(6)]
    for m in range(COARSE):
        hit = jnp.where(cell_ref[...] == m, full, 0.0)
        flat = hit[:, :cz_n].reshape(-1, 8, ny)
        step = cz_n // 8
        top_rows = hit[:, cz_n:]
        part[0].append(jnp.sum(flat[: 2 * step], axis=0, keepdims=True))
        part[1].append(jnp.sum(flat[2 * step : -2 * step], axis=0, keepdims=True))
        part[2].append(jnp.sum(flat[-2 * step :], axis=0, keepdims=True))
        part[3].append(top_rows[1:2])
        part[4].append(jnp.sum(top_rows[2:-2], axis=0, keepdims=True))
        part[5].append(top_rows[-2:-1])
    part = [jnp.concatenate(p, 0) for p in part]
    upper_half = lax.broadcasted_iota(jnp.int32, (COARSE, 8, ny), 1) < 4

    def total_of(p):
        return jnp.sum(jnp.sum(p, axis=1), axis=1, keepdims=True)

    shape = (COARSE, lanes)
    spots = (south[1], gz, north[1])
    places = [
        lax.broadcasted_iota(jnp.int32, shape, 1)
        == lax.broadcasted_iota(jnp.int32, shape, 0) + spot * COARSE
        for spot in spots
    ]
    for k in range(3):
        cols = [
            total_of(jnp.where(upper_half, 0.0, part[3 + k])), total_of(part[k]),
            total_of(jnp.where(upper_half, part[3 + k], 0.0)),
        ]
        line = sum(
            jnp.where(place, jnp.broadcast_to(col, shape), 0.0)
            for place, col in zip(places, cols)
        )
        msg_c[k] = jnp.sum(line, axis=0, keepdims=True)
    scatter(msg_c, got_c, coarse_sem.at[0], [at(o) for o in spread_to])

    arrive(4)
    ext = q_ref[...]
    q = 2.0 * ext[1:-1] - shares(2) * smooth(ext)
    q = q[1:-1] + ext[2:-2] - shares(1) * smooth(q)
    q = q[1:-1] + ext[3:-3] - shares(0) * smooth(q)

    pltpu.make_async_copy(got_c, got_c, coarse_sem.at[0]).wait()
    settle(sent.at[0], sum(lots) + sum(extra))

    def restricted(t):
        rows_in = [
            got_c[spread_to.index(fold(-j, k)), t - j + 1]
            for j in (t - 1, t, t + 1) for k in range(n_gz) if fold(-j, k) != (0, 0)
        ]
        return sum(rows_in, msg_c[t + 1])

    def corrections(inv, coarse):
        out = []
        for spot in spots:
            block = inv[pl.ds(pl.multiple_of(spot * COARSE, COARSE), COARSE), :]
            col = jnp.sum(block * coarse[:, : block.shape[1]], axis=1, keepdims=True)
            out.append(jnp.broadcast_to(col, (COARSE, ny)))
        return out

    def lift(cell, table):
        flat = cell.reshape(-1, 8, ny)
        picked = []
        for t in range(flat.shape[0]):
            index = flat[t]
            low = jnp.bitwise_and(index, 7)
            value = jnp.take_along_axis(table[:8], low, axis=0)
            for m in range(8, COARSE, 8):
                value = jnp.where(index >= m, jnp.take_along_axis(table[m : m + 8], low, axis=0), value)
            picked.append(value[None])
        return jnp.concatenate(picked, 0).reshape(cell.shape)

    corr = [corrections(inv, restricted(t)) for inv, t in zip((inv_side.at[0], inv_ref, inv_side.at[1]), (-1, 0, 1))]
    half = lax.broadcasted_iota(jnp.int32, (8, ny), 0) < 4
    spans = (pl.ds(0, 2), pl.ds(2, cx_n), pl.ds(cx_n + 2, 2))
    raised = []
    for k in range(3):
        cell = cell_ref[spans[k]]
        inside = lift(cell[:, :cz_n], corr[k][1])
        outside = jnp.where(
            half, lift(cell[:, cz_n:], corr[k][2]), lift(cell[:, cz_n:], corr[k][0])
        )
        raised.append(jnp.concatenate([inside, outside], 1))
    e = jnp.concatenate(raised, 0)
    e = e[1:-1] - shares(1) * smooth(e)
    e = e[1:-1] - shares(0) * smooth(e)
    out_ref[...] = (q + e)[:, :cz_n]


def put(a_ref, b_ref, a_out, b_out, sem):
    copies = [
        pltpu.make_async_copy(a_ref, a_out, sem.at[0]), pltpu.make_async_copy(b_ref, b_out, sem.at[1])
    ]
    for copy in copies:
        copy.start()
    for copy in copies:
        copy.wait()


def body(n_gx, n_gz, velocity_old, source, diag_coef, face_coef, bc_flags, coarse_map, coarse_inverse):
    cx_n, cz_n, ny = diag_coef.shape
    rows = cx_n * cz_n
    deep = cz_n + 8
    group = coarse_inverse.shape[1]
    lanes = -(-group // 128) * 128
    f32 = jnp.float32
    vmem = pltpu.VMEM
    dma = pltpu.SemaphoreType.DMA
    n_spread = min(5, n_gx) * n_gz - 1
    n_sum = n_gx * n_gz - 1 if n_gx * n_gz <= DIRECT else n_gx - 1

    def block(fields, halo):
        return vmem((fields, cx_n + 2 * halo, deep, ny), f32)

    scratch = [
        block(3, 2),
        vmem((3, cx_n, cz_n, ny), f32),
        block(4, 3),
        vmem(bc_flags.shape, jnp.int32),
        vmem((rows, ny), jnp.int32),
        vmem(coarse_inverse.shape, f32),
        block(3, 2),
        block(3, 1),
        block(3, 2),
        block(2, 1),
        block(2, 2),
        block(3, 2),
        block(3, 1),
        block(3, 3),
        block(3, 1),
        block(3, 1),
        block(3, 1),
        vmem((cx_n + 4, deep, ny), jnp.int32),
        vmem((cx_n + 4, deep, ny), jnp.int32),
        vmem((cx_n + 4, deep, ny), f32),
        vmem((cx_n + 4, deep, ny), f32),
        vmem((cx_n + 6, deep, ny), f32),
        vmem((2,) + coarse_inverse.shape, f32),
        vmem((2, 1, 128), f32),
        vmem((2, n_sum, 1, 128), f32),
        vmem((2, 1, 128), f32),
        vmem((2, n_gz - 1, 1, 128), f32),
        vmem((3, 1, lanes), f32),
        vmem((n_spread, 3, 1, lanes), f32),
        vmem((4096, ny), f32),
        dma((1,)),
        dma((5,)),
        dma((2, 2) if n_sum < n_gx * n_gz - 1 else (2, 1)),
        dma((1,)),
        dma((3,)),
        dma((1,)),
        dma((1,)),
    ]
    spec = pl.BlockSpec(memory_space=pltpu.VMEM)
    velocity, pressure = pl.pallas_call(
        functools.partial(kernel, (n_gx, n_gz, cx_n, cz_n, ny, lanes)),
        out_shape=(
            jax.ShapeDtypeStruct((3, cx_n, cz_n, ny), f32),
            jax.ShapeDtypeStruct((cx_n, cz_n, ny), f32),
        ),
        in_specs=[pl.BlockSpec(memory_space=pltpu.HBM)] * 7,
        out_specs=(spec, spec),
        scratch_shapes=scratch,
        compiler_params=pltpu.CompilerParams(
            collective_id=0, has_side_effects=True, vmem_limit_bytes=48 * 1024 * 1024
        ),
        name="corrector",
    )(
        *[
            pltpu.with_memory_space_constraint(a, pltpu.HBM)
            for a in (
                velocity_old,
                source,
                diag_coef,
                face_coef,
                bc_flags,
                coarse_map.reshape(rows, ny),
                coarse_inverse,
            )
        ]
    )
    velocity, pressure = pl.pallas_call(
        put,
        out_shape=(
            jax.ShapeDtypeStruct(velocity.shape, f32),
            jax.ShapeDtypeStruct(pressure.shape, f32),
        ),
        in_specs=[spec, spec],
        out_specs=[pl.BlockSpec(memory_space=pltpu.HBM)] * 2,
        scratch_shapes=[dma((2,))],
        name="put",
    )(*[pltpu.with_memory_space_constraint(a, pltpu.VMEM) for a in (velocity, pressure)])
    return velocity, pressure


def solution(mesh):
    placed = (
        P(None, "gx", "gz", None),
        P(None, "gx", "gz", None),
        P("gx", "gz", None),
        P(None, "gx", "gz", None),
        P(None, "gx", "gz"),
        P("gx", "gz", None),
        P("gx", None),
    )
    return jax.shard_map(
        functools.partial(body, mesh.shape["gx"], mesh.shape["gz"]),
        mesh=mesh,
        in_specs=placed,
        out_specs=(P(None, "gx", "gz", None), P("gx", "gz", None)),
        check_vma=False,
    )
```

```python
import functools
import math

import jax
import jax.numpy as jnp
from jax import lax
from jax.experimental import pallas as pl
from jax.experimental.pallas import tpu as pltpu
from jax.sharding import PartitionSpec as P

COARSE = 16
PAD = 8
DIRECT = 64

jacobi_weight = 2.0 / 3.0
MESH = pl.DeviceIdType.MESH


def kernel(
    dims,
    x0_in, src_in, diag_in, face_in, bc_in, map_in, inv_in,
    vel_ref, out_ref,
    x0_ref, src_ref, face_ref, bc_ref, map_ref, inv_ref,
    x0_late, rho_ref, rho_late, edge_ref,
    coef, res_ref, v_ref, vk_ref, a1_ref, a2_ref, a3_ref,
    code_ref, cell_ref, pd_ref, share_ref, q_ref, inv_side,
    msg, got, msg_z, got_z, msg_c, got_c,
    tally, sent, near_r, sum_sem, coarse_sem, load_sem, side_s, side_r,
):
    n_gx, n_gz, cx_n, cz_n, ny, lanes = dims
    rows = cx_n * cz_n
    deep = x0_ref.shape[2]
    gx = lax.axis_index("gx")
    gz = lax.axis_index("gz")
    east = (lax.rem(gx + 1, n_gx), gz)
    west = (lax.rem(gx + n_gx - 1, n_gx), gz)
    north = (gx, lax.rem(gz + 1, n_gz))
    south = (gx, lax.rem(gz + n_gz - 1, n_gz))
    row_x = [(lax.rem(gx + d, n_gx), gz) for d in range(1, n_gx)]
    row_z = [(gx, lax.rem(gz + d, n_gz)) for d in range(1, n_gz)]
    direct = n_gx * n_gz <= DIRECT

    def send(src, dst, ssem, rsem, to):
        copy = pltpu.make_async_remote_copy(
            src_ref=src, dst_ref=dst, send_sem=ssem, recv_sem=rsem,
            device_id=to, device_id_type=MESH,
        )
        copy.start()
        return copy

    def settle(sem, count):
        span = tally.at[pl.ds(0, count)]
        pltpu.make_async_copy(span, span, sem).wait()

    corners = [
        (east[0], north[1]), (east[0], south[1]), (west[0], north[1]), (west[0], south[1])
    ]

    def at(offset):
        return (lax.rem(gx + offset[0], n_gx), lax.rem(gz + offset[1], n_gz))

    def fold(d, k):
        return (d % n_gx, k % n_gz)

    around = {fold(d, k) for d in (-1, 0, 1) for k in (-1, 0, 1)} - {(0, 0)}
    spread_to = sorted({fold(d, k) for d in range(-2, 3) for k in range(n_gz)} - {(0, 0)}, key=lambda o: (o[1] == 0, min(o[1], n_gz - o[1]), -min(o[0], n_gx - o[0])))
    every = {(d, k) for d in range(n_gx) for k in range(n_gz)}
    if direct:
        sum_to = [
            (d, k)
            for k in sorted(range(n_gz), key=lambda k: (k == 0, min(k, n_gz - k)))
            for d in sorted(range(n_gx), key=lambda d: (d == 0, d % 4 == 0, d % 2))
            if d or k
        ]
        met = set(around)

        def known(extra):
            reach = met | extra
            return reach | {fold(a + d, b + k) for a, b in around for d, k in reach} | {(0, 0)}

        while every - known(set()):
            pairs = [{o, fold(-o[0], -o[1])} for o in sorted(every - met - {(0, 0)})]
            gain = len(known(set()))
            met |= max(pairs, key=lambda p: (len(known(p)) - gain) / len(p))
        sum_to = [at(o) for o in sum_to]
    else:
        sum_to = row_x
        met = around | set(spread_to)
        met |= {(d, 0) for d in range(1, n_gx)} | {(0, k) for k in range(1, n_gz)}
    near_first = sorted(around, key=lambda o: (o[0] == 0) + (o[1] == 0) * 2)
    partners = [at(o) for o in near_first] + [at(o) for o in sorted(met - around)]

    def inner(ref, halo):
        return ref.at[..., pl.ds(halo, cx_n), pl.ds(0, cz_n), :]

    loads = [
        pltpu.make_async_copy(a, b, load_sem.at[(0, 0, 1, 1, 1, 2, 3)[i]])
        for i, (a, b) in enumerate(
            [
                (x0_in, inner(x0_ref, 2)), (face_in, inner(face_ref.at[pl.ds(0, 3)], 3)),
                (diag_in, inner(face_ref.at[3], 3)), (src_in, src_ref),
                (map_in, map_ref), (bc_in, bc_ref), (inv_in, inv_ref),
            ]
        )
    ]
    barrier = pltpu.get_barrier_semaphore()
    for other in partners:
        pl.semaphore_signal(barrier, inc=1, device_id=other, device_id_type=MESH)
    for load in loads:
        load.start()
    settle(load_sem.at[0], 6 * rows)
    pl.semaphore_wait(barrier, len(partners))


    def side_x(sign, halo, a, b):
        if sign > 0:
            return pl.ds(halo + cx_n - b, b - a + 1), pl.ds(halo - b, b - a + 1)
        return pl.ds(halo + a - 1, b - a + 1), pl.ds(halo + cx_n + a - 1, b - a + 1)

    def side_z(sign, a, b):
        if sign > 0:
            return pl.ds(cz_n - b, b - a + 1), pl.ds(deep - b, b - a + 1)
        return pl.ds(a - 1, b - a + 1), pl.ds(cz_n + a - 1, b - a + 1)

    lots = []
    extra = []

    def ship(src, dst, to, where_from, where_to):
        target = dst.at[(..., *where_to, slice(None))]
        lots[-1] += math.prod(target.shape[:-1])
        i = len(lots) - 1
        send(src.at[(..., *where_from, slice(None))], target, sent.at[0], near_r.at[i], to)

    def arrive(i):
        settle(near_r.at[i], lots[i])

    def to_corners(src, dst, halo, n, land=None):
        land = halo if land is None else land
        for to, sx, sz in zip(corners, (1, 1, -1, -1), (1, -1, 1, -1)):
            fz, tz = side_z(sz, 1, n)
            ship(src, dst, to, (side_x(sx, halo, 1, n)[0], fz), (side_x(sx, land, 1, n)[1], tz))

    def to_z(src, dst, halo, a, b, ways=(1, -1), land=None, start=0, size=cx_n):
        land = halo if land is None else land
        for sz in ways:
            fz, tz = side_z(sz, a, b)
            where_from, where_to = (pl.ds(halo + start, size), fz), (pl.ds(land + start, size), tz)
            ship(src, dst, north if sz > 0 else south, where_from, where_to)

    def to_x(src, dst, halo, a, b, ways=(1, -1), land=None, start=0, size=cz_n):
        land = halo if land is None else land
        for sx in ways:
            fx, tx = side_x(sx, halo, a, b)[0], side_x(sx, land, a, b)[1]
            z = pl.ds(start, size)
            ship(src, dst, east if sx > 0 else west, (fx, z), (tx, z))

    both = pl.ds(0, 2)
    lots.append(0)
    to_corners(x0_ref, x0_ref, 2, 1)
    to_corners(face_ref.at[both], edge_ref, 3, 1, land=1)
    to_z(x0_ref, x0_ref, 2, 1, 1)
    to_z(face_ref.at[1], edge_ref.at[1], 3, 1, 1, (1,), land=1)
    to_z(face_ref.at[0], edge_ref.at[0], 3, 1, 1, land=1, start=cx_n - 1, size=1)
    to_x(x0_ref, x0_ref, 2, 1, 1)
    to_x(face_ref.at[0], edge_ref.at[0], 3, 1, 1, (1,), land=1)
    to_x(face_ref.at[1], edge_ref.at[1], 3, 1, 1, land=1, start=cz_n - 1, size=1)

    level = lax.broadcasted_iota(jnp.int32, (rows, ny), 1)
    bottom = level == 0
    top = level == ny - 1
    def y_prev(f):
        return pltpu.roll(f, 1, f.ndim - 1)

    def y_next(f):
        return pltpu.roll(f, ny - 1, f.ndim - 1)

    settle(load_sem.at[1], 5 * rows)
    own_z = pl.ds(0, cz_n)
    own_x = pl.ds(3, cx_n)
    shelf = lax.broadcasted_iota(jnp.int32, (cz_n, ny), 0)
    ends = lax.broadcasted_iota(jnp.int32, (cz_n, ny), 1)
    cy = face_ref[2, own_x, own_z]
    rim = (ends == 0) | (ends == ny - 1)
    main = face_ref[3, own_x, own_z] + jnp.where(rim, jnp.broadcast_to(cy[..., ny - 1 :], cy.shape), 0.0)
    rise = jnp.where(ends == ny - 1, 0.0, cy)

    def within(f):
        none = jnp.zeros((1, cz_n, ny), jnp.float32)
        flux_x = face_ref[0, pl.ds(3, cx_n - 1), own_z] * (f[:-1] - f[1:])
        flux_x = jnp.concatenate([none, flux_x, none], 0)
        flux_z = face_ref[1, own_x, own_z] * (f - pltpu.roll(f, cz_n - 1, 1))
        flux_z = jnp.where(shelf == cz_n - 1, 0.0, flux_z)
        flux_y = rise * (f - y_next(f))
        total = main * f + (flux_x[1:] - flux_x[:-1])
        return total + (flux_z - pltpu.roll(flux_z, 1, 1)) + (flux_y - y_prev(flux_y))

    for c in range(3):
        rho_ref[c, pl.ds(1, cx_n), own_z] = src_ref[c] - within(x0_ref[c, pl.ds(2, cx_n), own_z])
    to_z(rho_ref, rho_ref, 1, 1, 1)
    to_x(rho_ref, rho_ref, 1, 1, 1)

    lots.append(0)
    to_corners(x0_ref, x0_late, 2, 2)
    to_corners(face_ref, face_ref, 3, 2)
    to_corners(rho_ref, rho_late, 1, 1, land=2)
    to_z(rho_ref, rho_late, 1, 2, 2, land=2)
    for x in (0, cx_n - 1):
        to_z(x0_ref, x0_late, 2, 2, 2, start=x, size=1)
    to_z(face_ref, face_ref, 3, 1, 2)
    to_z(face_ref.at[1], face_ref.at[1], 3, 3, 3, (1,))
    to_x(rho_ref, rho_late, 1, 2, 2, land=2)
    for z in (0, cz_n - 1):
        to_x(x0_ref, x0_late, 2, 2, 2, start=z, size=1)
    to_x(face_ref, face_ref, 3, 1, 2)
    to_x(face_ref.at[0], face_ref.at[0], 3, 3, 3, (1,))

    eye = lax.broadcasted_iota(jnp.int32, (cz_n, cz_n), 0) == lax.broadcasted_iota(
        jnp.int32, (cz_n, cz_n), 1
    )

    def column(side):
        flags = bc_ref[side]
        parts = [
            jnp.sum(
                jnp.where(eye, jnp.broadcast_to(flags[i : i + 1], (cz_n, cz_n)), 0),
                axis=1, keepdims=True,
            )
            for i in range(cx_n)
        ]
        return jnp.broadcast_to(jnp.concatenate(parts, 0), (rows, ny))

    def scatter(msg, got, sem, others):
        for d, to in enumerate(others):
            send(msg, got.at[d], sent.at[0], sem, to)
        extra.append(math.prod(got.shape) // ny)

    def gathered(msg, got, sem):
        pltpu.make_async_copy(got, got, sem).wait()
        return msg[...] + jnp.sum(got[...], axis=0)

    def z_roll(f, shift):
        flat = f.reshape((-1,) + f.shape[-2:])
        return pltpu.roll(flat, shift % deep, 1).reshape(f.shape)

    def apply(f):
        h = (f.shape[0] - cx_n) // 2 - 1
        n = cx_n + 2 * h
        g = f[1:-1]
        flux_x = face_ref[0, pl.ds(2 - h, n + 1)] * (f[:-1] - f[1:])
        flux_z = face_ref[1, pl.ds(3 - h, n)] * (g - z_roll(g, -1))
        flux_y = coef[1, pl.ds(2 - h, n)] * (g - y_next(g))
        total = coef[0, pl.ds(2 - h, n)] * g + (flux_x[1:] - flux_x[:-1])
        return total + (flux_z - z_roll(flux_z, 1)) + (flux_y - y_prev(flux_y))

    def own(f):
        h = (f.shape[0] - cx_n) // 2
        return f[h : h + cx_n, :cz_n].reshape(rows, ny)

    def products(fields, pairs):
        sums = [None] * len(pairs)
        for p in range(0, rows, 8):
            tile = [f[p : p + 8] for f in fields]
            for k, (a, b) in enumerate(pairs):
                term = tile[a] * tile[b]
                sums[k] = term if sums[k] is None else sums[k] + term
        return sums

    def pack(sums):
        sums = [jnp.sum(s, axis=0, keepdims=True) for s in sums]
        while len(sums) < 3 * PAD:
            sums.append(jnp.zeros_like(sums[0]))
        total = jnp.sum(jnp.concatenate(sums, 0), axis=1, keepdims=True)
        shape = (3 * PAD, 128)
        pick = lax.broadcasted_iota(jnp.int32, shape, 0) == lax.broadcasted_iota(
            jnp.int32, shape, 1
        )
        return jnp.sum(
            jnp.where(pick, jnp.broadcast_to(total, shape), 0.0), axis=0, keepdims=True
        )

    def sums_start(i, pairs):
        msg[i] = pack(pairs)
        scatter(msg.at[i], got.at[i], sum_sem.at[i, 0], sum_to)

    def sums_end(i, count):
        total = gathered(msg.at[i], got.at[i], sum_sem.at[i, 0])
        if not direct:
            msg_z[i] = total
            scatter(msg_z.at[i], got_z.at[i], sum_sem.at[i, 1], row_z)
            total = gathered(msg_z.at[i], got_z.at[i], sum_sem.at[i, 1])
        shape = (8, 128)
        place = lax.broadcasted_iota(jnp.int32, shape, 0) * PAD
        lane = lax.broadcasted_iota(jnp.int32, shape, 1)
        wide = jnp.broadcast_to(total, shape)
        return [
            jnp.broadcast_to(
                jnp.sum(jnp.where(lane == place + k, wide, 0.0), axis=1, keepdims=True), shape
            )
            for k in range(count)
        ]

    slot = lax.broadcasted_iota(jnp.int32, (deep, ny), 0)
    floor = lax.broadcasted_iota(jnp.int32, (deep, ny), 1) == 0
    lid = lax.broadcasted_iota(jnp.int32, (deep, ny), 1) == ny - 1
    for load in loads[5:]:
        load.wait()
    flag = jnp.where(bottom, column(0), 0) + jnp.where(top, column(1), 0)
    code = map_ref[...] + COARSE * flag
    code_ref[pl.ds(2, cx_n), pl.ds(0, cz_n)] = code.reshape(cx_n, cz_n, ny)

    lots.append(0)
    to_corners(code_ref, code_ref, 2, 1)
    to_z(code_ref, code_ref, 2, 1, 2)
    to_x(code_ref, code_ref, 2, 1, 2)
    for k, to in enumerate((east, west)):
        send(inv_ref, inv_side.at[k], side_s.at[0], side_r.at[0], to)

    arrive(0)

    def prepare(low, high):
        for x in range(low, high):
            cy = face_ref[2, x + 1]
            wall = jnp.where(floor | lid, jnp.broadcast_to(cy[:, ny - 1 :], (deep, ny)), 0.0)
            coef[0, x] = face_ref[3, x + 1] + wall
            coef[1, x] = jnp.where(lid, 0.0, cy)

    seam = (slot == cz_n - 1) | (slot == deep - 1)

    def mend(part, f, coef_w, coef_e, coef_z):
        flux_w, flux_e = coef_w * (f[0] - f[1]), coef_e * (f[-2] - f[-1])
        flux_z = jnp.where(seam, coef_z * (f - z_roll(f, -1)), 0.0)
        part = part - (flux_z - z_roll(flux_z, 1))
        return jnp.concatenate(
            [
                (part[0] - flux_w)[None], (part[1] + flux_w)[None], part[2:-2],
                (part[-2] - flux_e)[None], (part[-1] + flux_e)[None],
            ], 0,
        )

    tail = pl.ds(cz_n, 8)
    coef_w = edge_ref[0, 0]
    coef_e = jnp.concatenate([face_ref[0, cx_n + 2, own_z], edge_ref[0, cx_n, tail]], 0)
    coef_z = jnp.concatenate(
        [edge_ref[1, pl.ds(0, 1), own_z], face_ref[1, own_x, own_z], edge_ref[1, pl.ds(cx_n + 1, 1), own_z]], 0
    )
    coef_z = jnp.concatenate([coef_z, edge_ref[1, :, tail]], 1)
    zero = jnp.zeros((8, ny), jnp.float32)
    dots = []
    for c in range(3):
        r = mend(rho_ref[c], x0_ref[c, pl.ds(1, cx_n + 2)], coef_w, coef_e, coef_z)
        r_own = own(r)
        v = jnp.concatenate([-within(r[1:-1, :cz_n]), jnp.zeros((cx_n, 8, ny), jnp.float32)], 1)
        none = jnp.zeros((1, deep, ny), jnp.float32)
        v = -mend(jnp.concatenate([none, v, none], 0), r, coef_w, coef_e, coef_z)
        v_own = own(v)
        vk_ref[c, pl.ds(3, cx_n), own_z] = v[1:-1, :cz_n]
        dots += products([r_own, v_own], [(0, 0), (0, 1)]) + [zero] * (PAD - 2)
    sums_start(0, dots)
    lots.append(0)
    to_corners(vk_ref, vk_ref, 3, 2)
    to_z(vk_ref, vk_ref, 3, 2, 3)
    to_x(vk_ref, vk_ref, 3, 2, 3)

    arrive(1)
    prepare(0, cx_n + 4)
    mine = (slot <= cz_n) | (slot == deep - 1)
    body_rows = slot < cz_n

    def widen(near, far):
        n = near.shape[0] - 2
        mid = jnp.where(mine, near[1:-1], far[2:-2])
        low = jnp.where(body_rows, near[0], far[1])
        high = jnp.where(body_rows, near[n + 1], far[n + 2])
        return jnp.concatenate([far[:1], low[None], mid, high[None], far[-1:]], 0)

    coef_w, coef_e = face_ref[0, 2], face_ref[0, cx_n + 2]
    coef_z = face_ref[1, pl.ds(1, cx_n + 4)]
    for c in range(3):
        r = widen(rho_ref[c], rho_late[c])
        f = widen(x0_ref[c, pl.ds(1, cx_n + 2)], x0_late[c])
        flux_w, flux_e = coef_w * (f[1] - f[2]), coef_e * (f[-3] - f[-2])
        flux_z = jnp.where(seam, coef_z * (f - z_roll(f, -1)), 0.0)
        r = r - (flux_z - z_roll(flux_z, 1))
        r = jnp.concatenate(
            [
                r[:1], (r[1] - flux_w)[None], (r[2] + flux_w)[None], r[3:-3],
                (r[-3] - flux_e)[None], (r[-2] + flux_e)[None], r[-1:],
            ], 0,
        )
        res_ref[c] = r
        v_ref[c] = apply(r)

    arrive(3)
    m0, m1 = sums_end(0, 2)
    sigma = m1 / m0
    dots = []
    for c in range(3):
        s = sigma[c : c + 1]
        mid = jnp.where(mine, v_ref[c, pl.ds(1, cx_n)], vk_ref[c, pl.ds(3, cx_n)])
        low = jnp.where(body_rows, v_ref[c, 0], vk_ref[c, 2])
        high = jnp.where(body_rows, v_ref[c, cx_n + 1], vk_ref[c, cx_n + 3])
        v = jnp.concatenate(
            [vk_ref[c, pl.ds(0, 2)], low[None], mid, high[None], vk_ref[c, pl.ds(cx_n + 4, 2)]], 0
        )
        r = res_ref[c]
        u = apply(v)
        v = v[1:-1]
        a1 = v - s * r
        a2 = (u - s * v) - s * a1
        a3 = apply(a2) - s * a2[1:-1]
        a4 = apply(a3) - s * a3[1:-1]
        dots += products(
            [own(r), own(a1), own(a2), own(a3), own(a4)],
            [(0, 1), (1, 1), (1, 2), (2, 2), (2, 3), (3, 3), (3, 4), (4, 4)],
        )
        a1_ref[c] = a1[1:-1]
        a2_ref[c] = a2[1:-1]
        a3_ref[c] = a3
    sums_start(1, dots)
    arrive(2)
    for sem in (side_s, side_r):
        pltpu.make_async_copy(inv_side, inv_side, sem.at[0]).wait()
    for x in range(cx_n + 4):
        mark = code_ref[x] >= COARSE
        edge = floor | lid
        pd = jnp.where(edge, jnp.where(mark, 6.0, 5.0), 6.0)
        pd_ref[x] = pd
        share_ref[x] = jacobi_weight / pd
        cell_ref[x] = jnp.where(mark, code_ref[x] - COARSE, code_ref[x])
    mu = [m0] + sums_end(1, PAD)

    def times(p):
        out = [sigma * p[0]]
        for i in range(1, len(p)):
            out.append(p[i - 1] + sigma * p[i])
        return out + [p[-1]]

    def dot(p, q):
        total = 0.0
        for n in range(len(p) + len(q) - 1):
            terms = [p[i] * q[n - i] for i in range(len(p)) if 0 <= n - i < len(q)]
            total = total + sum(terms[1:], terms[0]) * mu[n]
        return total

    def against(p):
        return sum((p[i] * mu[i] for i in range(1, len(p))), p[0] * mu[0])

    alpha = m0 / (sigma * m0 + mu[1])
    s1 = [1.0 - alpha * sigma, -alpha]
    t1 = times(s1)
    omega = dot(s1, t1) / dot(t1, t1)
    rho_new = against(s1) - omega * against(t1)
    beta = (rho_new / m0) * (alpha / omega)
    r1 = [s1[0] - omega * t1[0], s1[1] - omega * t1[1], -omega * t1[2]]
    p2 = [r1[0] + beta * (1.0 - omega * sigma), r1[1] - beta * omega, r1[2]]
    v2 = times(p2)
    alpha2 = rho_new / against(v2)
    s2 = [r1[i] - alpha2 * v2[i] for i in range(3)] + [-alpha2 * v2[3]]
    t2 = times(s2)
    omega2 = dot(s2, t2) / dot(t2, t2)
    weight = [
        alpha + omega * s1[0] + alpha2 * p2[0] + omega2 * s2[0],
        omega * s1[1] + alpha2 * p2[1] + omega2 * s2[1],
        alpha2 * p2[2] + omega2 * s2[2],
        omega2 * s2[3],
    ]
    speed = []
    for c in range(3):
        w = [k[c : c + 1] for k in weight]
        field = x0_ref[c, pl.ds(1, cx_n + 2)] + w[0] * res_ref[c, pl.ds(1, cx_n + 2)]
        field += w[1] * a1_ref[c] + w[2] * a2_ref[c] + w[3] * a3_ref[c]
        vel_ref[c] = field[1:-1, :cz_n]
        speed.append(field)
    ux, uz, uy = speed
    div = (ux[1:-1] - ux[:-2]) + (uz[1:-1] - z_roll(uz[1:-1], 1))
    uy = uy[1:-1]
    div = div + (uy - jnp.where(floor, 0.0, y_prev(uy)))
    share = share_ref[pl.ds(2, cx_n)]
    q = share * div
    q_ref[pl.ds(3, cx_n), pl.ds(0, cz_n)] = q[:, :cz_n]
    lots.append(0)
    to_corners(q_ref, q_ref, 3, 2)
    to_z(q_ref, q_ref, 3, 1, 3)
    to_x(q_ref, q_ref, 3, 1, 3)

    def smooth(f):
        n = f.shape[0] - 2
        h = (n - cx_n) // 2
        g = f[1:-1]
        near = (f[2:] + f[:-2]) + (z_roll(g, 1) + z_roll(g, -1))
        near += jnp.where(lid, 0.0, y_next(g)) + jnp.where(floor, 0.0, y_prev(g))
        return pd_ref[pl.ds(2 - h, n)] * g - near

    def shares(h):
        return share_ref[pl.ds(2 - h, cx_n + 2 * h)]

    blank = jnp.zeros((2, deep, ny), jnp.float32)
    mine = jnp.where(body_rows, q, 0.0)
    first_cut = -smooth(jnp.concatenate([blank, mine, blank], 0))
    trace = jnp.concatenate(
        [first_cut[:1], first_cut[1:-1] + jnp.where(body_rows, div, 0.0), first_cut[-1:]], 0
    )
    full = jnp.concatenate([blank[:1], trace, blank[:1]], 0)
    full = full - smooth(jnp.concatenate([blank, shares(1) * trace, blank], 0))

    def binned(spots_in):
        sums = [None] * COARSE
        for x, z in spots_in:
            cell, value = cell_ref[x, pl.ds(z, 8)], full[x, z : z + 8]
            for m in range(COARSE):
                term = jnp.where(cell == m, value, 0.0)
                sums[m] = term if sums[m] is None else sums[m] + term
        return jnp.concatenate([s[None] for s in sums], 0)

    steps = range(0, cz_n, 8)
    middle = range(2, cx_n + 2)
    part = [
        binned([(x, z) for x in span for z in steps])
        for span in (range(2), middle, range(cx_n + 2, cx_n + 4))
    ]
    part += [binned([(x, cz_n) for x in span]) for span in ((1,), middle, (cx_n + 2,))]
    upper_half = lax.broadcasted_iota(jnp.int32, (COARSE, 8, ny), 1) < 4

    def total_of(p):
        return jnp.sum(jnp.sum(p, axis=1), axis=1, keepdims=True)

    shape = (COARSE, lanes)
    spots = (south[1], gz, north[1])
    places = [
        lax.broadcasted_iota(jnp.int32, shape, 1)
        == lax.broadcasted_iota(jnp.int32, shape, 0) + spot * COARSE
        for spot in spots
    ]
    for k in range(3):
        cols = [
            total_of(jnp.where(upper_half, 0.0, part[3 + k])), total_of(part[k]),
            total_of(jnp.where(upper_half, part[3 + k], 0.0)),
        ]
        line = sum(
            jnp.where(place, jnp.broadcast_to(col, shape), 0.0)
            for place, col in zip(places, cols)
        )
        msg_c[k] = jnp.sum(line, axis=0, keepdims=True)
    scatter(msg_c, got_c, coarse_sem.at[0], [at(o) for o in spread_to])

    arrive(4)
    ext = q_ref[...]
    q = 2.0 * ext[1:-1] - shares(2) * smooth(ext)
    q = q[1:-1] + ext[2:-2] - shares(1) * smooth(q)
    q = q[1:-1] + ext[3:-3] - shares(0) * smooth(q)

    pltpu.make_async_copy(got_c, got_c, coarse_sem.at[0]).wait()
    settle(sent.at[0], sum(lots) + sum(extra))

    def restricted(t):
        rows_in = [
            got_c[spread_to.index(fold(-j, k)), t - j + 1]
            for j in (t - 1, t, t + 1) for k in range(n_gz) if fold(-j, k) != (0, 0)
        ]
        return sum(rows_in, msg_c[t + 1])

    def corrections(inv, coarse):
        out = []
        for spot in spots:
            block = inv[pl.ds(pl.multiple_of(spot * COARSE, COARSE), COARSE), :]
            col = jnp.sum(block * coarse[:, : block.shape[1]], axis=1, keepdims=True)
            out.append(jnp.broadcast_to(col, (COARSE, ny)))
        return out

    def lift(cell, table):
        flat = cell.reshape(-1, 8, ny)
        picked = []
        for t in range(flat.shape[0]):
            index = flat[t]
            low = jnp.bitwise_and(index, 7)
            value = jnp.take_along_axis(table[:8], low, axis=0)
            for m in range(8, COARSE, 8):
                value = jnp.where(index >= m, jnp.take_along_axis(table[m : m + 8], low, axis=0), value)
            picked.append(value[None])
        return jnp.concatenate(picked, 0).reshape(cell.shape)

    corr = [corrections(inv, restricted(t)) for inv, t in zip((inv_side.at[0], inv_ref, inv_side.at[1]), (-1, 0, 1))]
    half = lax.broadcasted_iota(jnp.int32, (8, ny), 0) < 4
    spans = (pl.ds(0, 2), pl.ds(2, cx_n), pl.ds(cx_n + 2, 2))
    raised = []
    for k in range(3):
        cell = cell_ref[spans[k]]
        inside = lift(cell[:, :cz_n], corr[k][1])
        outside = jnp.where(
            half, lift(cell[:, cz_n:], corr[k][2]), lift(cell[:, cz_n:], corr[k][0])
        )
        raised.append(jnp.concatenate([inside, outside], 1))
    e = jnp.concatenate(raised, 0)
    e = e[1:-1] - shares(1) * smooth(e)
    e = e[1:-1] - shares(0) * smooth(e)
    out_ref[...] = (q + e)[:, :cz_n]


def put(a_ref, b_ref, a_out, b_out, sem):
    copies = [
        pltpu.make_async_copy(a_ref, a_out, sem.at[0]), pltpu.make_async_copy(b_ref, b_out, sem.at[1])
    ]
    for copy in copies:
        copy.start()
    for copy in copies:
        copy.wait()


def body(n_gx, n_gz, velocity_old, source, diag_coef, face_coef, bc_flags, coarse_map, coarse_inverse):
    cx_n, cz_n, ny = diag_coef.shape
    rows = cx_n * cz_n
    deep = cz_n + 8
    group = coarse_inverse.shape[1]
    lanes = -(-group // 128) * 128
    f32 = jnp.float32
    vmem = pltpu.VMEM
    dma = pltpu.SemaphoreType.DMA
    n_spread = min(5, n_gx) * n_gz - 1
    n_sum = n_gx * n_gz - 1 if n_gx * n_gz <= DIRECT else n_gx - 1

    def block(fields, halo):
        return vmem((fields, cx_n + 2 * halo, deep, ny), f32)

    scratch = [
        block(3, 2),
        vmem((3, cx_n, cz_n, ny), f32),
        block(4, 3),
        vmem(bc_flags.shape, jnp.int32),
        vmem((rows, ny), jnp.int32),
        vmem(coarse_inverse.shape, f32),
        block(3, 2),
        block(3, 1),
        block(3, 2),
        block(2, 1),
        block(2, 2),
        block(3, 2),
        block(3, 1),
        block(3, 3),
        block(3, 1),
        block(3, 1),
        block(3, 1),
        vmem((cx_n + 4, deep, ny), jnp.int32),
        vmem((cx_n + 4, deep, ny), jnp.int32),
        vmem((cx_n + 4, deep, ny), f32),
        vmem((cx_n + 4, deep, ny), f32),
        vmem((cx_n + 6, deep, ny), f32),
        vmem((2,) + coarse_inverse.shape, f32),
        vmem((2, 1, 128), f32),
        vmem((2, n_sum, 1, 128), f32),
        vmem((2, 1, 128), f32),
        vmem((2, n_gz - 1, 1, 128), f32),
        vmem((3, 1, lanes), f32),
        vmem((n_spread, 3, 1, lanes), f32),
        vmem((4096, ny), f32),
        dma((1,)),
        dma((5,)),
        dma((2, 2) if n_sum < n_gx * n_gz - 1 else (2, 1)),
        dma((1,)),
        dma((4,)),
        dma((1,)),
        dma((1,)),
    ]
    spec = pl.BlockSpec(memory_space=pltpu.VMEM)
    velocity, pressure = pl.pallas_call(
        functools.partial(kernel, (n_gx, n_gz, cx_n, cz_n, ny, lanes)),
        out_shape=(
            jax.ShapeDtypeStruct((3, cx_n, cz_n, ny), f32),
            jax.ShapeDtypeStruct((cx_n, cz_n, ny), f32),
        ),
        in_specs=[pl.BlockSpec(memory_space=pltpu.HBM)] * 7,
        out_specs=(spec, spec),
        scratch_shapes=scratch,
        compiler_params=pltpu.CompilerParams(
            collective_id=0, has_side_effects=True, vmem_limit_bytes=48 * 1024 * 1024
        ),
        name="corrector",
    )(
        *[
            pltpu.with_memory_space_constraint(a, pltpu.HBM)
            for a in (
                velocity_old,
                source,
                diag_coef,
                face_coef,
                bc_flags,
                coarse_map.reshape(rows, ny),
                coarse_inverse,
            )
        ]
    )
    velocity, pressure = pl.pallas_call(
        put,
        out_shape=(
            jax.ShapeDtypeStruct(velocity.shape, f32),
            jax.ShapeDtypeStruct(pressure.shape, f32),
        ),
        in_specs=[spec, spec],
        out_specs=[pl.BlockSpec(memory_space=pltpu.HBM)] * 2,
        scratch_shapes=[dma((2,))],
        name="put",
    )(*[pltpu.with_memory_space_constraint(a, pltpu.VMEM) for a in (velocity, pressure)])
    return velocity, pressure


def solution(mesh):
    placed = (
        P(None, "gx", "gz", None),
        P(None, "gx", "gz", None),
        P("gx", "gz", None),
        P(None, "gx", "gz", None),
        P(None, "gx", "gz"),
        P("gx", "gz", None),
        P("gx", None),
    )
    return jax.shard_map(
        functools.partial(body, mesh.shape["gx"], mesh.shape["gz"]),
        mesh=mesh,
        in_specs=placed,
        out_specs=(P(None, "gx", "gz", None), P("gx", "gz", None)),
        check_vma=False,
    )
```
